32 devices in a mesh: seq: 4 (over z), batch: 8 (over y, x, core).
Axes of the slice: x: 2, y: 2, z: 4, core: 2. Of those that a mesh axis runs over, the one named last changes fastest.
Arguments:
- inputs: bfloat16 [16, 512, 1024], P('batch', 'seq'), may hold values from -6 to 6
- lengths: int32 [16, 3], P('batch'), may hold values from 1 to 256, 512 in all within a row
- ln1_gain: bfloat16 [1024], replicated, may hold values from 0.5 to 1.5
- ln1_bias: bfloat16 [1024], replicated, may hold values from -1 to 1
- ln2_gain: bfloat16 [1024], replicated, may hold values from 0.5 to 1.5
- ln2_bias: bfloat16 [1024], replicated, may hold values from -1 to 1
- qkv_weight: bfloat16 [1024, 3072], replicated, may hold values from -0.1875 to 0.1875
- qkv_bias: bfloat16 [3072], replicated, may hold values from -1 to 1
- dense_weight: bfloat16 [1024, 1024], replicated, may hold values from -1.5 to 1.5
- dense_bias: bfloat16 [1024], replicated, may hold values from -1 to 1
- up_weight: bfloat16 [1024, 4096], replicated, may hold values from -0.1875 to 0.1875
- up_bias: bfloat16 [4096], replicated, may hold values from -1 to 1
- down_weight: bfloat16 [4096, 1024], replicated, may hold values from -0.09375 to 0.09375
- down_bias: bfloat16 [1024], replicated, may hold values from -1 to 1
- qmc_points: float32 [64, 64], replicated, may hold values from -4 to 4
- qmc_weights: float32 [64], replicated, may hold values from 0.25 to 4
- cotangent: bfloat16 [16, 512, 1024], P('batch', 'seq'), may hold values from -6 to 6
Outputs:
- output: bfloat16 [16, 512, 1024], P('batch', 'seq')
- input_grad: float32 [16, 512, 1024], P('batch', 'seq')
- ln1_gain_grad: float32 [1024], P('batch')
- ln1_bias_grad: float32 [1024], P('batch')
- ln2_gain_grad: float32 [1024], P('batch')
- ln2_bias_grad: float32 [1024], P('batch')
- qkv_weight_grad: float32 [1024, 3072], P('batch')
- qkv_bias_grad: float32 [3072], P('batch')
- dense_weight_grad: float32 [1024, 1024], P('batch')
- dense_bias_grad: float32 [1024], P('batch')
- up_weight_grad: float32 [1024, 4096], P('batch')
- up_bias_grad: float32 [4096], P('batch')
- down_weight_grad: float32 [4096, 1024], P('batch')
- down_bias_grad: float32 [1024], P('batch')
The draws below stay inside these ranges and needn't reach their ends.
Inputs may be any that keep to these rules, and one draw needn't show every extreme that they name: `lengths`: each row sums to 512; its largest entry is exactly 256.
All inputs are finite; a program needn't handle non-finite values.
Results may differ from the reference program's by a relative error of at most 0.015.
Values sent between devices are 32-bit elements; how exact they have to be, the bound alone decides.
No kernel may reach another device: no remote copies, remote signals or barrier semaphores. Data moves between devices by JAX's collectives and lax.ppermute only.
A program may use at most 192 MiB of HBM per device.

```python
import math
import jax
import jax.numpy as jnp
import numpy as np
from jax import lax

D = 1024
HEADS = 16
HEAD = 64
FF = 4096
ROT = 16
FEAT = 64
GROUP = 64
NDOC = 3
LEN = 512
SEQS = 16


def spiked(entries, stream_key, source, target, blocks, factor):
    def block_of(position):
        return (jnp.arange(entries.shape[position]) // (entries.shape[position] // blocks)).reshape((-1,) + (1,) * (entries.ndim - 1 - position))

    near = jax.random.permutation(stream_key, blocks)[block_of(target)]
    other_side = (block_of(target) + blocks // 2) % blocks
    return jnp.where((block_of(source) == near) | (block_of(source) == other_side), factor * entries, entries)


def shard_levels(own_key, extent, split, low, largest):
    def one(dim, blocks):
        heights = jax.random.uniform(jax.random.fold_in(jax.random.fold_in(own_key, 6), dim), (blocks,), jnp.float32, low / len(split), largest / len(split))
        return jnp.repeat(jnp.exp(heights), extent[dim] // blocks).reshape((-1,) + (1,) * (len(extent) - dim - 1))

    gain = one(*split[0])
    for cut in split[1:]:
        gain = gain * one(*cut)
    return gain


def split_up(amount, total, reach, skew):
    weights = [(1 << 20) // math.isqrt(standing ** skew) + 1 for standing in range(2, amount + 1)]
    surplus, holding = total - reach - (amount - 1), [1] * (amount - 1)
    while surplus > 0:
        candidates = [i for i in range(amount - 1) if holding[i] < reach]
        mass, remaining = sum([weights[i] for i in candidates]), surplus
        for i in candidates:
            addition = min(reach - holding[i], max(1, remaining * weights[i] // mass), surplus)
            holding[i] = holding[i] + addition
            surplus = surplus - addition
    return np.array([reach] + holding)


def ragged_sizes(rng, count, total, most, slope):
    if count == 2:
        one = jax.random.randint(rng, (), max(1, total - most), min(most, total - 1) + 1)
        return jnp.stack([one, total - one])
    tallies = jnp.asarray(split_up(count, total, most, slope), jnp.int32)
    twos = (count - 1) // 2
    donor, sink = tallies[1:1 + 2 * twos:2], tallies[2:2 + 2 * twos:2]
    margin = jnp.minimum(donor - 1, most - sink)
    passed = jax.random.randint(jax.random.fold_in(rng, 1), (twos,), 0, 1 << 20) % (margin + 1)
    tallies = tallies.at[1:1 + 2 * twos:2].set(donor - passed).at[2:2 + 2 * twos:2].set(sink + passed)
    return tallies[jax.random.permutation(jax.random.fold_in(rng, 2), count)]


def bell_draw(own_key, dims, width, most, pieces=(), kind=jnp.bfloat16):
    loudness = shard_levels(own_key, dims, pieces, -0.22, 0.18) if pieces else 1.0
    drawn = jax.random.normal(own_key, dims, jnp.float32) * width * loudness
    return jnp.minimum(jnp.maximum(drawn, -most), most).astype(kind)


def bell_draw_with(own_key, shape, scale, bound, cuts, heavy, kind=jnp.bfloat16):
    values = scale * jax.random.normal(own_key, shape, jnp.float32)
    if cuts:
        values = values * shard_levels(own_key, shape, cuts, -0.22, 0.18)
    return jnp.clip(spiked(values, jax.random.fold_in(own_key, 3), *heavy), -bound, bound).astype(kind)


def setup_inputs(seed: int = 0) -> dict:
    streams_of = jax.random.split(jax.random.key(seed), 18)
    inputs = bell_draw_with(streams_of[0], (SEQS, LEN, D), 1.0, 6.0, ((0, 8), (1, 4)), (0, 2, 8, 2.0))
    lengths = jax.vmap(lambda own: ragged_sizes(own, NDOC, LEN, LEN // 2, 1))(jax.random.split(streams_of[1], SEQS)).reshape((SEQS, NDOC)).astype(jnp.int32)
    ln1_gain = jnp.clip(1.0 + 0.1 * jax.random.normal(streams_of[2], (D,), jnp.float32), 0.5, 1.5).astype(jnp.bfloat16)
    ln1_bias = bell_draw(streams_of[3], (D,), 0.2, 1.0)
    ln2_gain = jnp.clip(1.0 + 0.1 * jax.random.normal(streams_of[4], (D,), jnp.float32), 0.5, 1.5).astype(jnp.bfloat16)
    ln2_bias = bell_draw(streams_of[5], (D,), 0.2, 1.0)
    qkv_weight = bell_draw(streams_of[6], (D, 3 * D), D ** -0.5, 0.1875)
    qkv_bias = bell_draw(streams_of[7], (3 * D,), 0.2, 1.0)
    dense_weight = bell_draw(streams_of[8], (D, D), (D // 64) ** -0.5, 1.5)
    dense_bias = bell_draw(streams_of[9], (D,), 0.2, 1.0)
    up_weight = bell_draw(streams_of[10], (D, FF), D ** -0.5, 0.1875)
    up_bias = bell_draw(streams_of[11], (FF,), 0.2, 1.0)
    down_weight = bell_draw(streams_of[12], (FF, D), FF ** -0.5, 0.09375)
    down_bias = bell_draw(streams_of[13], (D,), 0.2, 1.0)
    qmc_points = bell_draw(streams_of[14], (HEAD, FEAT), 1.0, 4.0, (), jnp.float32)
    qmc_weights = jnp.clip(jnp.exp(jax.random.uniform(streams_of[15], (FEAT,), jnp.float32, math.log(0.25), math.log(4.0))), 0.25, 4.0)
    cotangent = bell_draw(streams_of[16], (SEQS, LEN, D), 1.0, 6.0, ((0, 8), (1, 4)))
    return {"inputs": inputs, "lengths": lengths, "ln1_gain": ln1_gain, "ln1_bias": ln1_bias, "ln2_gain": ln2_gain, "ln2_bias": ln2_bias, "qkv_weight": qkv_weight, "qkv_bias": qkv_bias, "dense_weight": dense_weight, "dense_bias": dense_bias, "up_weight": up_weight, "up_bias": up_bias, "down_weight": down_weight, "down_bias": down_bias, "qmc_points": qmc_points, "qmc_weights": qmc_weights, "cotangent": cotangent}


HIGH = lax.Precision.HIGHEST
EPSILON = 1e-05
ROTARY_BASE = 10000.0

@jax.custom_vjp
def low(v):
    return lax.optimization_barrier(v.astype(jnp.bfloat16)).astype(jnp.float32)

@jax.custom_vjp
def low_back(v):
    return v

def low_keep(v):
    return (low(v), None)

def low_pass(kept, grad):
    return (grad,)

def back_keep(v):
    return (v, None)

def back_low(kept, grad):
    return (low(grad),)
low.defvjp(low_keep, low_pass)
low_back.defvjp(back_keep, back_low)

def layer_norm(values, norm_gain, norm_shift):
    center = lax.optimization_barrier(jnp.mean(values, axis=-1, keepdims=True))
    centered = values - center
    spread = lax.optimization_barrier(jnp.mean(centered * centered, axis=-1, keepdims=True))
    return centered * lax.rsqrt(spread + EPSILON) * norm_gain + norm_shift

def rotary_tables(positions):
    half_rot = ROT // 2
    freqs_table = ROTARY_BASE ** (-2.0 * jnp.arange(half_rot, dtype=jnp.float32) / ROT)
    angles = positions.astype(jnp.float32)[:, None] * freqs_table[None, :]
    angles = jnp.concatenate([angles, angles], axis=-1)
    return (jnp.cos(angles), jnp.sin(angles))

def rotate(heads_in, cos_table, sin_table):
    half_rot = ROT // 2
    rotary_part = heads_in[..., :ROT]
    turned = jnp.concatenate([-rotary_part[..., half_rot:], rotary_part[..., :half_rot]], axis=-1)
    rotated = rotary_part * cos_table[:, None, :] + turned * sin_table[:, None, :]
    return jnp.concatenate([rotated, heads_in[..., ROT:]], axis=-1)

def dct_matrix():
    freq_rows = jnp.arange(HEAD, dtype=jnp.float32)[:, None]
    sample_cols = jnp.arange(HEAD, dtype=jnp.float32)[None, :]
    cosines = jnp.cos(jnp.pi * (sample_cols + 0.5) * freq_rows / HEAD) * jnp.sqrt(2.0 / HEAD)
    return jnp.where(freq_rows == 0.0, cosines * jnp.sqrt(0.5), cosines)

def feature_map(heads_in, dct_basis, points, feature_weights):
    scaled = heads_in * HEAD ** (-0.25)
    spectrum = jnp.einsum('...n,kn->...k', scaled, dct_basis, precision=HIGH)
    projected = jnp.einsum('...k,km->...m', spectrum, points, precision=HIGH)
    energy = 0.5 * lax.optimization_barrier(jnp.sum(scaled * scaled, axis=-1, keepdims=True))
    return feature_weights * jnp.exp(projected - energy)

def attend(query_low, key_low, value_low, doc_ids, before):
    group_count = LEN // GROUP
    query_groups = query_low.reshape(group_count, GROUP, HEADS, FEAT)
    key_groups = key_low.reshape(group_count, GROUP, HEADS, FEAT)
    value_groups = value_low.reshape(group_count, GROUP, HEADS, HEAD)
    group_ids = doc_ids.reshape(group_count, GROUP)
    causal = jnp.arange(GROUP)[:, None] >= jnp.arange(GROUP)[None, :]

    def group_step(carried, block_in):
        kv_state, key_norm = carried
        query_block, key_block, value_block, block_ids, prev_doc = block_in
        intra_mask = ((block_ids[:, None] == block_ids[None, :]) & causal).astype(jnp.float32)
        scores = jnp.einsum('thm,shm->hts', query_block, key_block, precision=HIGH) * intra_mask[None]
        scores = low(low_back(scores))
        use_state = (block_ids == prev_doc).astype(jnp.float32)
        numerator = jnp.einsum('hts,she->the', scores, value_block, precision=HIGH) + use_state[:, None, None] * jnp.einsum('thm,hme->the', query_block, low(kv_state), precision=HIGH)
        numerator = low_back(numerator)
        denominator = lax.optimization_barrier(jnp.sum(scores, axis=2)).T + use_state[:, None] * jnp.einsum('thm,hm->th', query_block, key_norm, precision=HIGH)
        heads_out = numerator / denominator[:, :, None]
        keep_keys = (block_ids == block_ids[-1]).astype(jnp.float32)
        local_state = low_back(jnp.einsum('shm,she->hme', key_block * keep_keys[:, None, None], value_block, precision=HIGH))
        local_norm = jnp.einsum('shm,s->hm', key_block, keep_keys, precision=HIGH)
        reset_flag = (block_ids[-1] != prev_doc).astype(jnp.float32)
        return ((local_state + (1.0 - reset_flag) * kv_state, local_norm + (1.0 - reset_flag) * key_norm), heads_out)
    initial = (jnp.zeros((HEADS, FEAT, HEAD), jnp.float32), jnp.zeros((HEADS, FEAT), jnp.float32))
    final_state, group_outs = lax.scan(jax.checkpoint(group_step), initial, (query_groups, key_groups, value_groups, group_ids, before))
    return group_outs.reshape(LEN, HEADS * HEAD)

def forward(params, inputs_wide, doc_ids, before, cos_table, sin_table, dct_basis, points, feature_weights):
    attn_gain, attn_shift, mlp_gain, mlp_shift, qkv_weight, qkv_bias, dense_weight, dense_bias, up_weight, up_bias, down_weight, down_bias = params
    normed_attn = layer_norm(inputs_wide, attn_gain, attn_shift)
    normed_mlp = layer_norm(inputs_wide, mlp_gain, mlp_shift)
    qkv_proj = low_back(jnp.dot(low(normed_attn), qkv_weight, precision=HIGH) + qkv_bias).reshape(LEN, HEADS, 3 * HEAD)
    query_rot = rotate(qkv_proj[..., :HEAD], cos_table, sin_table)
    key_rot = rotate(qkv_proj[..., HEAD:2 * HEAD], cos_table, sin_table)
    query_low = low(feature_map(query_rot, dct_basis, points, feature_weights))
    key_low = low(feature_map(key_rot, dct_basis, points, feature_weights))
    value_low = low(qkv_proj[..., 2 * HEAD:])
    heads_out = attend(query_low, key_low, value_low, doc_ids, before)
    attn_out = jnp.dot(low(heads_out), dense_weight, precision=HIGH) + dense_bias
    up_proj = low_back(jnp.dot(low(normed_mlp), up_weight, precision=HIGH) + up_bias)
    mlp_out = jnp.dot(low(jax.nn.gelu(up_proj, approximate=False)), down_weight, precision=HIGH) + down_bias
    return inputs_wide + attn_out + mlp_out

def reference(inputs, lengths, ln1_gain, ln1_bias, ln2_gain, ln2_bias, qkv_weight, qkv_bias, dense_weight, dense_bias, up_weight, up_bias, down_weight, down_bias, qmc_points, qmc_weights, cotangent):
    wide_type = jnp.float32
    params = tuple((weight_arg.astype(wide_type) for weight_arg in (ln1_gain, ln1_bias, ln2_gain, ln2_bias, qkv_weight, qkv_bias, dense_weight, dense_bias, up_weight, up_bias, down_weight, down_bias)))
    dct_basis = dct_matrix()
    positions = jnp.arange(LEN, dtype=jnp.int32)
    cos_table, sin_table = rotary_tables(positions)
    points = qmc_points.astype(wide_type)
    feature_weights = qmc_weights.astype(wide_type)

    def one_sequence(grad_sums, sequence_item):
        seq_inputs, seq_cot, length_row = sequence_item
        doc_starts = jnp.cumsum(length_row) - length_row
        doc_ids = lax.optimization_barrier(jnp.sum((doc_starts[None, :] <= positions[:, None]).astype(jnp.int32), axis=1)) - 1
        group_first = positions[::GROUP] - 1
        before = lax.optimization_barrier(jnp.sum((doc_starts[None, :] <= group_first[:, None]).astype(jnp.int32), axis=1)) - 1

        def run_layer(layer_in, layer_params):
            return forward(layer_params, layer_in, doc_ids, before, cos_table, sin_table, dct_basis, points, feature_weights)
        result, pull_back = jax.vjp(run_layer, seq_inputs.astype(wide_type), params)
        input_grad, param_grads = pull_back(seq_cot.astype(wide_type))
        grad_sums = tuple((total + extra for total, extra in zip(grad_sums, param_grads)))
        return (grad_sums, (result.astype(jnp.bfloat16), input_grad))
    zero_grads = tuple((jnp.zeros_like(weight_arg) for weight_arg in params))
    grad_sums, outputs_all = lax.scan(one_sequence, zero_grads, (inputs, cotangent, lengths))
    output, input_grad = outputs_all
    attn_gain_grad, attn_shift_grad, mlp_gain_grad, mlp_shift_grad, qkv_weight_grad, qkv_bias_grad, dense_weight_grad, dense_bias_grad, up_weight_grad, up_bias_grad, down_weight_grad, down_bias_grad = grad_sums
    return (output, input_grad, attn_gain_grad, attn_shift_grad, mlp_gain_grad, mlp_shift_grad, qkv_weight_grad, qkv_bias_grad, dense_weight_grad, dense_bias_grad, up_weight_grad, up_bias_grad, down_weight_grad, down_bias_grad)
```

```python
from functools import partial

import jax
import jax.numpy as jnp
from jax import lax
from jax.sharding import PartitionSpec as P

D = 1024
HEADS = 16
HEAD = 64
ROT = 16
FEAT = 64
GROUP = 64


HIGH = lax.Precision.HIGHEST
EPSILON = 1e-05
ROTARY_BASE = 10000.0


def shift_rows(value, axis, by):
    count = lax.axis_size(axis)
    return lax.ppermute(
        value, axis, [(i, i + by) for i in range(count) if 0 <= i + by < count]
    )


def carried(own, passing, axis, by):
    hops = max(1, lax.axis_size(axis) // 2)
    arrived = jax.tree.map(lambda a: shift_rows(a, axis, by), own)
    for _ in range(hops - 1):
        arrived = jax.tree.map(
            lambda a, e: shift_rows(
                a + passing.reshape(passing.shape + (1,) * (a.ndim - 1)) * e, axis, by
            ),
            own,
            arrived,
        )
    return arrived


def swap(value, bit):
    count = lax.axis_size("batch")
    return lax.ppermute(value, "batch", [(i, i ^ (1 << bit)) for i in range(count)])


def line_sum(part):
    count = lax.axis_size("seq")
    if count == 1:
        return part
    if count % 2:
        return lax.psum(part, "seq")
    place = lax.axis_index("seq")
    half = count // 2
    for k in range(half - 1):
        part = part + lax.ppermute(part, "seq", [(k, k + 1), (count - 1 - k, count - 2 - k)])
    part = part + lax.ppermute(part, "seq", [(half - 1, half), (half, half - 1)])
    for k in range(half - 2, -1, -1):
        back = lax.ppermute(part, "seq", [(k + 1, k), (count - 2 - k, count - 1 - k)])
        part = jnp.where((place == k) | (place == count - 1 - k), back, part)
    return part


def owner_order(bits):
    return sorted(
        range(1 << len(bits)), key=lambda r: tuple(-((r >> bit) & 1) for bit in bits)
    )


def halving(send, keep, bits, shift):
    for step, bit in enumerate(bits):
        held = keep + swap(send, bit + shift)
        if step + 1 < len(bits):
            half = held.shape[0] // 2
            send, keep = held[:half], held[half:]
    return held


def scatter_vectors(vectors):
    count = lax.axis_size("batch")
    me = lax.axis_index("batch")
    pieces = jnp.concatenate([v.reshape(count, -1) for v in vectors], axis=1)
    bits = list(range(count.bit_length() - 1))
    order = owner_order(bits)
    rows = [lax.dynamic_slice_in_dim(pieces, r ^ me, 1, 0) for r in order]
    half = count // 2
    held = halving(jnp.concatenate(rows[:half]), jnp.concatenate(rows[half:]), bits, 0)
    total = line_sum(held)[0]
    out, at = [], 0
    for v in vectors:
        out.append(total[at : at + v.shape[0] // count])
        at += v.shape[0] // count
    return out


def owner_blocks(features, width, order, at=0, size=None):
    count = lax.axis_size("batch")
    me = lax.axis_index("batch")
    size = width if size is None else size

    def pick(rel):
        return lax.dynamic_slice_in_dim(features, (rel ^ me) * width + at, size, 1)

    mine = jnp.concatenate([pick(2 * r) for r in order], axis=1)
    other = jnp.concatenate([pick(2 * r + 1) for r in order], axis=1)
    return mine, other


def pair_gather(mine, other):
    arrived = swap(other.astype(jnp.float32), 0)
    arrived = arrived * jnp.where(lax.axis_index("seq") < lax.axis_size("seq"), 1.0, 0.5)
    return jnp.concatenate([mine, arrived.astype(jnp.bfloat16)], axis=0)


def grad_scatter(left, right, bits):
    half = left.shape[1] // 2
    send = lax.dot_general(
        left[:, :half], right, (((0,), (0,)), ((), ())), preferred_element_type=jnp.float32
    )
    keep = lax.dot_general(
        left[:, half:], right, (((0,), (0,)), ((), ())), preferred_element_type=jnp.float32
    )
    return line_sum(halving(send, keep, bits, 1))


def rotary_tables(positions):
    half_rot = ROT // 2
    freqs_table = ROTARY_BASE ** (-2.0 * jnp.arange(half_rot, dtype=jnp.float32) / ROT)
    angles = positions.astype(jnp.float32)[:, None] * freqs_table[None, :]
    angles = jnp.concatenate([angles, angles], axis=-1)
    return (jnp.cos(angles), jnp.sin(angles))


def rotate(heads_in, cos_table, sin_table):
    half_rot = ROT // 2
    rotary_part = heads_in[..., :ROT]
    turned = jnp.concatenate([-rotary_part[..., half_rot:], rotary_part[..., :half_rot]], axis=-1)
    rotated = rotary_part * cos_table[:, None, :] + turned * sin_table[:, None, :]
    return jnp.concatenate([rotated, heads_in[..., ROT:]], axis=-1)


def dct_matrix():
    freq_rows = jnp.arange(HEAD, dtype=jnp.float32)[:, None]
    sample_cols = jnp.arange(HEAD, dtype=jnp.float32)[None, :]
    cosines = jnp.cos(jnp.pi * (sample_cols + 0.5) * freq_rows / HEAD) * jnp.sqrt(2.0 / HEAD)
    return jnp.where(freq_rows == 0.0, cosines * jnp.sqrt(0.5), cosines)


def feature_map(heads_in, dct_basis, points, feature_weights):
    scaled = heads_in * HEAD ** (-0.25)
    spectrum = jnp.einsum("...n,kn->...k", scaled, dct_basis, precision=HIGH)
    projected = jnp.einsum("...k,km->...m", spectrum, points, precision=HIGH)
    energy = 0.5 * jnp.sum(scaled * scaled, axis=-1, keepdims=True)
    return feature_weights * jnp.exp(projected - energy)


def shards(
    inputs,
    lengths,
    ln1_gain,
    ln1_bias,
    ln2_gain,
    ln2_bias,
    qkv_weight,
    qkv_bias,
    dense_weight,
    dense_bias,
    up_weight,
    up_bias,
    down_weight,
    down_bias,
    qmc_points,
    qmc_weights,
    cotangent,
):
    narrow = jnp.bfloat16
    wide_type = jnp.float32
    seqs_here, context = (inputs.shape[0], inputs.shape[1])
    group_count = context // GROUP
    positions = lax.axis_index("seq") * context + jnp.arange(context, dtype=jnp.int32)
    doc_starts = jnp.cumsum(lengths, axis=1) - lengths
    doc_ids = (
        jnp.sum((doc_starts[:, None, :] <= positions[None, :, None]).astype(jnp.int32), axis=2) - 1
    )
    group_first = positions[::GROUP] - 1
    before = (
        jnp.sum((doc_starts[:, None, :] <= group_first[None, :, None]).astype(jnp.int32), axis=2)
        - 1
    )
    group_ids = doc_ids.reshape(seqs_here, group_count, GROUP)
    group_ends = group_ids[:, :, -1]
    entry_doc = before[:, 0]
    last_doc = doc_ids[:, -1]
    order_index = jnp.arange(group_count)
    token_index = jnp.arange(GROUP)
    use_state = (group_ids == before[:, :, None]).astype(wide_type)
    keep_keys = (group_ids == group_ends[:, :, None]).astype(wide_type)
    causal = token_index[:, None] >= token_index[None, :]
    intra_mask = ((group_ids[..., :, None] == group_ids[..., None, :]) & causal).astype(wide_type)
    carry_in = (before == entry_doc[:, None]).astype(wide_type)
    link_mask = (
        (group_ends[:, None, :] == before[:, :, None])
        & (order_index[:, None] > order_index[None, :])
    ).astype(wide_type)
    to_end = (group_ends == last_doc[:, None]).astype(wide_type)
    reset_flag = (last_doc != entry_doc).astype(wide_type)
    inputs_wide = inputs.astype(wide_type)
    owners = lax.axis_size("batch")
    owner_bits = list(range(owners.bit_length() - 2))
    orders = (owner_bits, owner_bits[::-1])
    flat = (seqs_here * context, D)
    center = jnp.mean(inputs_wide, axis=-1, keepdims=True)
    centered = inputs_wide - center
    spread = jnp.mean(centered * centered, axis=-1, keepdims=True)
    inv_spread = lax.rsqrt(spread + EPSILON)
    normed = centered * inv_spread
    attn_in = (normed * ln1_gain.astype(wide_type) + ln1_bias.astype(wide_type)).astype(narrow)
    mlp_in = (normed * ln2_gain.astype(wide_type) + ln2_bias.astype(wide_type)).astype(narrow)
    cot_flat = cotangent.reshape(flat)
    cot_pair = pair_gather(cot_flat, cot_flat)
    norm_pairs = []
    for bits in orders:
        mine_a, other_a = owner_blocks(attn_in.reshape(flat), D // owners, owner_order(bits))
        mine_m, other_m = owner_blocks(mlp_in.reshape(flat), D // owners, owner_order(bits))
        norm_pairs.append(
            jnp.split(
                pair_gather(
                    jnp.concatenate([mine_a, mine_m], axis=1),
                    jnp.concatenate([other_a, other_m], axis=1),
                ),
                2,
                axis=1,
            )
        )
    qkv_proj = (
        jnp.dot(attn_in, qkv_weight, preferred_element_type=wide_type) + qkv_bias.astype(wide_type)
    ).reshape(seqs_here, context, HEADS, 3 * HEAD)
    cos_table, sin_table = rotary_tables(positions)
    dct_basis = dct_matrix()

    def both_features(query_heads, key_heads):
        return (
            feature_map(
                rotate(query_heads, cos_table, sin_table), dct_basis, qmc_points, qmc_weights
            ),
            feature_map(
                rotate(key_heads, cos_table, sin_table), dct_basis, qmc_points, qmc_weights
            ),
        )

    feats_pair, feature_back = jax.vjp(
        both_features, qkv_proj[..., :HEAD], qkv_proj[..., HEAD : 2 * HEAD]
    )
    shape_groups = (seqs_here, group_count, GROUP, HEADS)
    query_low = feats_pair[0].astype(narrow).reshape(shape_groups + (FEAT,))
    key_low = feats_pair[1].astype(narrow).reshape(shape_groups + (FEAT,))
    value_low = qkv_proj[..., 2 * HEAD :].astype(narrow).reshape(shape_groups + (HEAD,))
    query_wide = query_low.astype(wide_type)
    keep_narrow = keep_keys.astype(narrow)
    key_kept = key_low * keep_narrow[..., None, None]
    local_state = jnp.einsum(
        "bcshm,bcshe->bchme", key_kept, value_low, preferred_element_type=wide_type
    )
    local_norm = jnp.einsum(
        "bcshm,bcs->bchm", key_low, keep_narrow, preferred_element_type=wide_type
    )
    out_state = jnp.einsum("bc,bchme->bhme", to_end, local_state, precision=HIGH)
    out_norm = jnp.einsum("bc,bchm->bhm", to_end, local_norm, precision=HIGH)
    passing = 1.0 - reset_flag
    in_state, in_norm = carried((out_state, out_norm), passing, "seq", 1)
    group_state = carry_in[..., None, None, None] * in_state[:, None] + jnp.einsum(
        "bcd,bdhme->bchme", link_mask, local_state, precision=HIGH
    )
    group_norm = carry_in[..., None, None] * in_norm[:, None] + jnp.einsum(
        "bcd,bdhm->bchm", link_mask, local_norm, precision=HIGH
    )
    state_low = group_state.astype(narrow)
    scores = (
        jnp.einsum("bcthm,bcshm->bchts", query_low, key_low, preferred_element_type=wide_type)
        * intra_mask[:, :, None]
    )
    scores_low = scores.astype(narrow)
    numerator = jnp.einsum(
        "bchts,bcshe->bcthe", scores_low, value_low, preferred_element_type=wide_type
    ) + use_state[..., None, None] * jnp.einsum(
        "bcthm,bchme->bcthe", query_low, state_low, preferred_element_type=wide_type
    )
    denominator = jnp.swapaxes(jnp.sum(scores_low.astype(wide_type), axis=-1), 2, 3) + use_state[
        ..., None
    ] * jnp.einsum("bcthm,bchm->bcth", query_wide, group_norm, precision=HIGH)
    heads_out = numerator / denominator[..., None]
    attn_low = heads_out.reshape(seqs_here, context, D).astype(narrow)
    attn_out = jnp.dot(
        attn_low, dense_weight, preferred_element_type=wide_type
    ) + dense_bias.astype(wide_type)
    up_proj = jnp.dot(mlp_in, up_weight, preferred_element_type=wide_type) + up_bias.astype(
        wide_type
    )
    activation, gelu_back = jax.vjp(partial(jax.nn.gelu, approximate=False), up_proj)
    act_low = activation.astype(narrow)
    mlp_out = jnp.dot(act_low, down_weight, preferred_element_type=wide_type) + down_bias.astype(
        wide_type
    )
    output = (inputs_wide + attn_out + mlp_out).astype(narrow)
    cot_wide = cotangent.astype(wide_type)
    bias_grad = jnp.sum(cot_wide, axis=(0, 1))
    down_parts = []
    rows_each = 4 * D // owners
    for part, bits in enumerate(orders):
        mine, other = owner_blocks(
            act_low.reshape(-1, 4 * D),
            rows_each,
            owner_order(bits),
            part * rows_each // 2,
            rows_each // 2,
        )
        down_parts.append(grad_scatter(pair_gather(mine, other), cot_pair, bits))
    down_total = jnp.concatenate(down_parts, axis=0)
    mine, other = owner_blocks(attn_low.reshape(flat), D // owners, owner_order(orders[0]))
    dense_total = grad_scatter(pair_gather(mine, other), cot_pair, orders[0])
    attn_grad = jnp.einsum("btj,ij->bti", cotangent, dense_weight, preferred_element_type=wide_type)
    act_grad = jnp.einsum("btj,ij->bti", cotangent, down_weight, preferred_element_type=wide_type)
    up_grad_low = gelu_back(act_grad)[0].astype(narrow)
    up_grad_flat = up_grad_low.reshape(-1, 4 * D)
    up_pair = pair_gather(up_grad_flat, up_grad_flat)
    up_total = jnp.concatenate(
        [
            grad_scatter(norm_pairs[part][1], piece, bits)
            for part, (bits, piece) in enumerate(zip(orders, jnp.split(up_pair, 2, axis=1)))
        ],
        axis=1,
    )
    up_bias_grad = jnp.sum(up_grad_low.astype(wide_type), axis=(0, 1))
    mlp_norm_grad = jnp.einsum(
        "btj,ij->bti", up_grad_low, up_weight, preferred_element_type=wide_type
    )
    heads_grad = attn_grad.reshape(shape_groups + (HEAD,))
    numer_grad = (heads_grad / denominator[..., None]).astype(narrow)
    denom_grad = -jnp.sum(heads_grad * heads_out, axis=-1) / denominator
    scores_grad = (
        jnp.einsum("bcthe,bcshe->bchts", numer_grad, value_low, preferred_element_type=wide_type)
        + jnp.swapaxes(denom_grad, 2, 3)[..., None]
    )
    scores_grad_low = (scores_grad * intra_mask[:, :, None]).astype(narrow)
    numer_used = numer_grad * use_state.astype(narrow)[..., None, None]
    denom_used = denom_grad * use_state[..., None]
    query_grad = (
        jnp.einsum("bchts,bcshm->bcthm", scores_grad_low, key_low, preferred_element_type=wide_type)
        + jnp.einsum("bcthe,bchme->bcthm", numer_used, state_low, preferred_element_type=wide_type)
        + denom_used[..., None] * group_norm[:, :, None]
    )
    key_grad = jnp.einsum(
        "bchts,bcthm->bcshm", scores_grad_low, query_low, preferred_element_type=wide_type
    )
    value_grad = jnp.einsum(
        "bchts,bcthe->bcshe", scores_low, numer_grad, preferred_element_type=wide_type
    )
    state_grad = jnp.einsum(
        "bcthm,bcthe->bchme", query_low, numer_used, preferred_element_type=wide_type
    )
    norm_grad = jnp.einsum("bcthm,bcth->bchm", query_wide, denom_used, precision=HIGH)
    in_state_grad = jnp.einsum("bc,bchme->bhme", carry_in, state_grad, precision=HIGH)
    in_norm_grad = jnp.einsum("bc,bchm->bhm", carry_in, norm_grad, precision=HIGH)
    out_state_grad, out_norm_grad = carried((in_state_grad, in_norm_grad), passing, "seq", -1)
    local_grad = (
        jnp.einsum("bcd,bchme->bdhme", link_mask, state_grad, precision=HIGH)
        + to_end[..., None, None, None] * out_state_grad[:, None]
    ).astype(narrow)
    local_norm_grad = (
        jnp.einsum("bcd,bchm->bdhm", link_mask, norm_grad, precision=HIGH)
        + to_end[..., None, None] * out_norm_grad[:, None]
    )
    keep_wide = keep_keys[..., None, None]
    key_grad = key_grad + keep_wide * (
        jnp.einsum("bcshe,bchme->bcshm", value_low, local_grad, preferred_element_type=wide_type)
        + local_norm_grad[:, :, None]
    )
    value_grad = value_grad + keep_wide * jnp.einsum(
        "bcshm,bchme->bcshe", key_low, local_grad, preferred_element_type=wide_type
    )
    heads_shape = (seqs_here, context, HEADS)
    query_heads_grad, key_heads_grad = feature_back(
        (query_grad.reshape(heads_shape + (FEAT,)), key_grad.reshape(heads_shape + (FEAT,)))
    )
    qkv_grad = (
        jnp.concatenate(
            [query_heads_grad, key_heads_grad, value_grad.reshape(heads_shape + (HEAD,))], axis=-1
        )
        .reshape(seqs_here, context, 3 * D)
        .astype(narrow)
    )
    qkv_grad_flat = qkv_grad.reshape(-1, 3 * D)
    qkv_pair = pair_gather(qkv_grad_flat, qkv_grad_flat)
    qkv_total = jnp.concatenate(
        [
            grad_scatter(norm_pairs[part][0], piece, bits)
            for part, (bits, piece) in enumerate(zip(orders, jnp.split(qkv_pair, 2, axis=1)))
        ],
        axis=1,
    )
    qkv_bias_grad = jnp.sum(qkv_grad.astype(wide_type), axis=(0, 1))
    attn_norm_grad = jnp.einsum(
        "btj,ij->bti", qkv_grad, qkv_weight, preferred_element_type=wide_type
    )
    attn_gain_grad = jnp.sum(attn_norm_grad * normed, axis=(0, 1))
    attn_shift_grad = jnp.sum(attn_norm_grad, axis=(0, 1))
    mlp_gain_grad = jnp.sum(mlp_norm_grad * normed, axis=(0, 1))
    mlp_shift_grad = jnp.sum(mlp_norm_grad, axis=(0, 1))
    normed_grad = attn_norm_grad * ln1_gain.astype(wide_type) + mlp_norm_grad * ln2_gain.astype(
        wide_type
    )
    input_grad = cot_wide + inv_spread * (
        normed_grad
        - jnp.mean(normed_grad, axis=-1, keepdims=True)
        - normed * jnp.mean(normed_grad * normed, axis=-1, keepdims=True)
    )
    mlp_gain_total, mlp_shift_total, up_bias_total, bias_total = scatter_vectors(
        (mlp_gain_grad, mlp_shift_grad, up_bias_grad, bias_grad)
    )
    attn_gain_total, attn_shift_total, qkv_bias_total = scatter_vectors(
        (attn_gain_grad, attn_shift_grad, qkv_bias_grad)
    )
    return (
        output,
        input_grad,
        attn_gain_total,
        attn_shift_total,
        mlp_gain_total,
        mlp_shift_total,
        qkv_total,
        qkv_bias_total,
        dense_total,
        bias_total,
        up_total,
        up_bias_total,
        down_total,
        bias_total,
    )


def solution(mesh):
    placed = (
        P("batch", "seq", None),
        P("batch", None),
        P(),
        P(),
        P(),
        P(),
        P(),
        P(),
        P(),
        P(),
        P(),
        P(),
        P(),
        P(),
        P(),
        P(),
        P("batch", "seq", None),
    )
    return jax.shard_map(
        shards,
        mesh=mesh,
        in_specs=placed,
        out_specs=(
            P("batch", "seq", None),
            P("batch", "seq", None),
            P("batch"),
            P("batch"),
            P("batch"),
            P("batch"),
            P("batch", None),
            P("batch"),
            P("batch", None),
            P("batch"),
            P("batch", None),
            P("batch"),
            P("batch", None),
            P("batch"),
        ),
        check_vma=False,
    )
```

```python
import math
from functools import partial

import jax
import jax.numpy as jnp
import numpy as np
from jax import lax
from jax.experimental import pallas as pl
from jax.experimental.pallas import tpu as pltpu
from jax.sharding import PartitionSpec as P

D = 1024
HEADS = 16
HEAD = 64
ROT = 16
FF = 4096
PAIR = 2 * HEAD
BLOCK = 128
COLUMNS = 512

EPSILON = 1e-05
ROTARY_BASE = 10000.0

ROWS_COLS = ((1,), (0,))
ROWS_ROWS = ((1,), (1,))
COLS_COLS = ((0,), (0,))
NARROW = jnp.bfloat16
WIDE = jnp.float32


def plain_dot(left, right, dims):
    return lax.dot_general(left, right, (dims, ((), ())), preferred_element_type=WIDE)


def whole_spec(shape):
    return pl.BlockSpec(shape, lambda *_: (0,) * len(shape))


def shift_rows(value, axis, by):
    count = lax.axis_size(axis)
    return lax.ppermute(
        value, axis, [(i, i + by) for i in range(count) if 0 <= i + by < count]
    )


def swap(value, bit):
    count = lax.axis_size("batch")
    return lax.ppermute(value, "batch", [(i, i ^ (1 << bit)) for i in range(count)])


def owner_order(bits):
    return sorted(
        range(1 << len(bits)), key=lambda r: tuple(-((r >> bit) & 1) for bit in bits)
    )


def line_rounds(count):
    half = count // 2
    rounds = [("in", [(k, k + 1), (count - 1 - k, count - 2 - k)], k) for k in range(half - 1)]
    rounds.append(("in", [(half - 1, half), (half, half - 1)], -1))
    for k in range(half - 2, -1, -1):
        rounds.append(("out", [(k + 1, k), (count - 2 - k, count - 1 - k)], k))
    return rounds


class Line:
    def __init__(self):
        self.last = None

    def wait(self, *values):
        if self.last is not None:
            values, _ = lax.optimization_barrier((values, self.last))
        return values

    def send(self, value, how):
        return how(*self.wait(value))

    def step(self, function, *values):
        out = function(*self.wait(*values))
        self.last = jax.tree.leaves(out)[0]
        return out


class Vectors:
    def __init__(self, line, vectors):
        owners = lax.axis_size("batch")
        me = lax.axis_index("batch")
        self.line = line
        self.sizes = [v.shape[0] // owners for v in vectors]
        pieces = jnp.concatenate([v.reshape(owners, -1) for v in vectors], axis=1)
        bits = list(range(owners.bit_length() - 1))
        rows = [lax.dynamic_slice_in_dim(pieces, r ^ me, 1, 0) for r in owner_order(bits)]
        self.held = jnp.concatenate(rows)
        count = lax.axis_size("seq")
        self.steps = [("swap", bit, 0) for bit in bits]
        self.steps += line_rounds(count) if count % 2 == 0 else []
        self.moving = None
        self.now = None
        self.send()

    def send(self):
        if self.moving is not None or not self.steps:
            return
        self.now = kind, what, _ = self.steps.pop(0)
        if kind == "swap":
            half = self.held.shape[0] // 2
            self.moving = self.line.send(self.held[:half], lambda a: swap(a, what))
            self.held = self.held[half:]
        else:
            self.moving = self.line.send(self.held, lambda a: lax.ppermute(a, "seq", what))

    def take(self):
        if self.moving is None:
            return
        kind, _, at = self.now
        if kind == "out":
            place, count = lax.axis_index("seq"), lax.axis_size("seq")
            edge = (place == at) | (place == count - 1 - at)
            self.held = self.line.step(
                lambda a, b: jnp.where(edge, b, a), self.held, self.moving
            )
        else:
            self.held = self.line.step(lambda a, b: a + b, self.held, self.moving)
        self.moving = None

    def results(self):
        while self.moving is not None or self.steps:
            self.take()
            self.send()
        if lax.axis_size("seq") % 2 and lax.axis_size("seq") > 1:
            self.held = lax.psum(self.held, "seq")
        out, at = [], 0
        for size in self.sizes:
            out.append(self.held[0, at : at + size])
            at += size
        return out


class Reduction:
    def __init__(self, line, left, right, bits):
        self.line = line
        half = left.shape[1] // 2
        send = line.step(lambda a, b: plain_dot(a, b, COLS_COLS), left[:, :half], right)
        self.held = line.step(lambda a, b: plain_dot(a, b, COLS_COLS), left[:, half:], right)
        count = lax.axis_size("seq")
        self.steps = [("swap", bit + 1, 0) for bit in bits]
        self.steps += line_rounds(count) if count % 2 == 0 else []
        self.moving = swap(send, bits[0] + 1)

    def finish(self):
        place, count = lax.axis_index("seq"), lax.axis_size("seq")
        for i, (kind, _, at) in enumerate(self.steps):
            if kind == "out":
                edge = (place == at) | (place == count - 1 - at)
                self.held = self.line.step(
                    lambda a, b: jnp.where(edge, b, a), self.held, self.moving
                )
            else:
                self.held = self.line.step(lambda a, b: a + b, self.held, self.moving)
            if i + 1 == len(self.steps):
                break
            kind, what, _ = self.steps[i + 1]
            if kind == "swap":
                half = self.held.shape[0] // 2
                self.moving = swap(self.held[:half], what)
                self.held = self.held[half:]
            else:
                self.moving = lax.ppermute(self.held, "seq", what)
        return self.held if count % 2 == 0 or count == 1 else lax.psum(self.held, "seq")


class Singly:
    def __init__(self, line, bits):
        self.line, self.bits = line, bits
        self.pieces = []

    def prepare(self, pairs):
        for piece in (one for pair in pairs for one in pair):
            left, left_in, block, right, right_in, column = piece
            columns = slice(column * COLUMNS, (column + 1) * COLUMNS)
            left = jnp.concatenate([left[block], rounded(left_in[block])], axis=0)
            right = jnp.concatenate([right[:, columns], rounded(right_in[:, columns])], axis=0)
            self.pieces.append(Reduction(self.line, left, right, self.bits))

    def step(self):
        pass

    def finished(self):
        return True

    def results(self):
        return [one.finish() for one in self.pieces]


def rounded(arrived):
    one = jnp.where(lax.axis_index("seq") < lax.axis_size("seq"), 1.0, 0.5)
    return (arrived * one).astype(NARROW)


def product_kernel(count, *refs):
    ins, (to_x, to_y, hold_a, hold_b) = refs[: 8 * count], refs[-4:]
    for p in range(count):
        for i, (to, hold) in enumerate(((to_x, hold_a), (to_y, hold_b))):
            left, left_in, right, right_in = ins[8 * p + 4 * i : 8 * p + 4 * i + 4]
            whole = jnp.concatenate([left[0], left_in[0].astype(NARROW)], axis=0)
            right = jnp.concatenate([right[...], right_in[...].astype(NARROW)], axis=0)

            def product(first, second):
                rows = [whole[:, k * BLOCK : (k + 1) * BLOCK] for k in (first, second)]
                return plain_dot(jnp.concatenate(rows, axis=1), right, COLS_COLS)

            out = pl.ds(p * 2 * BLOCK, 2 * BLOCK)
            to[out, :] = product(0, 1 if i else 2)
            hold[out, :] = product(2 if i else 1, 3)


def round_kernel(counts, *refs):
    first, second, inward, middle, outward = counts
    refs = list(refs)
    edge = refs.pop(0)[0] != 0

    def take(flag, count):
        return [refs.pop(0) for _ in range(count)] if flag else [None] * count

    from_x, from_y = take(first or second, 2)
    hold_a, hold_b = take(first, 2)
    kept_a, kept_b = take(second, 2)
    (sums,) = take(inward, 1)
    (from_end,) = take(inward or outward, 1)
    inner, from_middle = take(middle, 2)
    (whole,) = take(outward, 1)
    to_x, to_y, keep_a, keep_b = take(first, 4)
    (new_sums,) = take(second, 1)
    (to_end,) = take(second or middle, 1)
    (new_inner,) = take(inward, 1)
    (new_whole,) = take(middle, 1)
    (final,) = take(outward, 1)
    for p in range(first):
        low = pl.ds(2 * p * BLOCK, BLOCK)
        high = pl.ds((2 * p + 1) * BLOCK, BLOCK)
        out = pl.ds(p * BLOCK, BLOCK)
        to_y[out, :] = hold_a[low, :] + from_x[low, :]
        to_x[out, :] = hold_b[low, :] + from_y[low, :]
        keep_a[out, :] = hold_a[high, :] + from_x[high, :]
        keep_b[out, :] = hold_b[high, :] + from_y[high, :]
    for p in range(max(second, middle)):
        for i, (kept, arrived) in enumerate(((kept_a, from_y), (kept_b, from_x))):
            out = pl.ds((2 * p + i) * BLOCK, BLOCK)
            ends = inners = None
            if p < second:
                come = pl.ds((2 * first + p) * BLOCK, BLOCK)
                ends = kept[pl.ds(p * BLOCK, BLOCK), :] + arrived[come, :]
                new_sums[out, :] = ends
            if p < middle:
                inners = inner[out, :] + from_middle[out, :]
                new_whole[out, :] = inners
            if ends is None:
                to_end[out, :] = inners
            elif inners is None:
                to_end[out, :] = ends
            else:
                to_end[out, :] = jnp.where(edge, ends, inners)
    if inward:
        new_inner[...] = sums[...] + from_end[: 2 * inward * BLOCK, :]
    if outward:
        final[...] = jnp.where(edge, from_end[: 2 * outward * BLOCK, :], whole[...])


class Rounds:
    PARTS = 2

    def __init__(self, line, edge, counts):
        self.line, self.edge, self.counts = line, edge, counts
        self.made = self.at = 0
        self.buffers, self.moving, self.hold, self.kept = {}, {}, {}, {}
        self.sums, self.inner, self.whole, self.finals = {}, {}, {}, []
        self.end = self.middle = None
        self.wide = COLUMNS // self.PARTS

    def count(self, group):
        return self.counts[group] if 0 <= group < len(self.counts) else 0

    def rows_spec(self, rows, at=0):
        return pl.BlockSpec((rows, self.wide), lambda i: (at, i))

    def prepare(self, pairs):
        r = self.made
        self.made += 1
        count = len(pairs)
        args, specs = [], []
        for left, left_in, block, right, right_in, column in (
            one for pair in pairs for one in pair
        ):
            for value in (left, left_in):
                args.append(value)
                specs.append(
                    pl.BlockSpec((1, *value.shape[1:]), lambda i, block=block: (block, 0, 0))
                )
            for value in (right, right_in):
                args.append(value)
                specs.append(
                    pl.BlockSpec(
                        (value.shape[0], self.wide),
                        lambda i, c=column: (0, c * self.PARTS + i),
                    )
                )
        rows = 2 * count * BLOCK
        total = rows + self.count(r - 2) * BLOCK
        aliases = {}
        if r in self.buffers:
            aliases = {len(args) + i: i for i in range(2)}
            args += list(self.buffers.pop(r))
            specs += [pl.BlockSpec(memory_space=pl.ANY)] * 2
        call = pl.pallas_call(
            partial(product_kernel, count),
            grid=(self.PARTS,),
            in_specs=specs,
            out_specs=[self.rows_spec(rows)] * 4,
            out_shape=[jax.ShapeDtypeStruct((total, COLUMNS), WIDE)] * 2
            + [jax.ShapeDtypeStruct((rows, COLUMNS), WIDE)] * 2,
            input_output_aliases=aliases,
            name="piece_products",
        )
        to_x, to_y, hold_a, hold_b = self.line.step(call, *args)
        self.hold[r] = (hold_a, hold_b)
        self.moving[r] = (swap(to_x, 1), swap(to_y, 2))

    def step(self):
        r = self.at
        self.at += 1
        counts = [self.count(r - back) for back in (0, 2, 3, 4, 5)]
        first, second, inward, middle, outward = counts
        args, specs = [self.edge], [pl.BlockSpec(memory_space=pltpu.SMEM)]

        def add(value):
            args.append(value)
            specs.append(self.rows_spec(value.shape[0]))

        if first or second:
            for value in self.moving.pop(r):
                add(value)
        if first:
            for value in self.hold.pop(r):
                add(value)
        if second:
            for value in self.kept.pop(r - 2):
                add(value)
        if inward:
            add(self.sums.pop(r - 3))
        if inward or outward:
            add(self.end)
        if middle:
            add(self.inner.pop(r - 4))
            add(self.middle)
        if outward:
            add(self.whole.pop(r - 5))
        outs, out_specs = [], []

        def out(rows, at=0, of=None):
            outs.append(jax.ShapeDtypeStruct((of or rows, COLUMNS), WIDE))
            out_specs.append(self.rows_spec(rows, at))

        ahead = self.count(r + 2)
        if first:
            for _ in range(2):
                out(first * BLOCK, 2 * ahead // first, (2 * ahead + first) * BLOCK)
            out(first * BLOCK)
            out(first * BLOCK)
        if second:
            out(2 * second * BLOCK)
        if second or middle:
            out(2 * max(second, middle) * BLOCK)
        for count in (inward, middle, outward):
            if count:
                out(2 * count * BLOCK)
        call = pl.pallas_call(
            partial(round_kernel, counts),
            grid=(self.PARTS,),
            in_specs=specs,
            out_specs=out_specs,
            out_shape=outs,
            name="reduce_round",
        )
        got = list(self.line.step(call, *args))
        if first:
            to = (got.pop(0), got.pop(0))
            if ahead:
                self.buffers[r + 2] = to
            else:
                self.moving[r + 2] = (swap(to[0], 1), swap(to[1], 2))
            self.kept[r] = (got.pop(0), got.pop(0))
        if second:
            self.sums[r - 2] = got.pop(0)
        if second or middle:
            self.end = lax.ppermute(got.pop(0), "seq", [(0, 1), (1, 0), (2, 3), (3, 2)])
        if inward:
            self.inner[r - 3] = got.pop(0)
            self.middle = lax.ppermute(self.inner[r - 3], "seq", [(1, 2), (2, 1)])
        if middle:
            self.whole[r - 4] = got.pop(0)
        if outward:
            self.finals.append(got.pop(0))

    def finished(self):
        return len(self.finals) == len(self.counts)

    def results(self):
        return [
            final[k * BLOCK : (k + 1) * BLOCK]
            for final in self.finals
            for k in range(final.shape[0] // BLOCK)
        ]


def pick_kernel(me_ref, *refs):
    ins, (keep_ref, send_ref) = refs[:-2], refs[-2:]
    half = keep_ref.shape[2] // BLOCK
    for i, ref in enumerate(ins):
        for p in range(half):
            for core in range(2):
                owner = (2 * (half - 1 - p) + core) ^ me_ref[0]
                columns = ref[:, pl.ds(pl.multiple_of(owner * BLOCK, BLOCK), BLOCK)]
                at = slice(p * BLOCK, (p + 1) * BLOCK)
                if core:
                    send_ref[i, :, at] = columns.astype(WIDE)
                else:
                    keep_ref[i, :, at] = columns


def pick(arrays, me):
    owners = lax.axis_size("batch")
    half = owners // 2
    tokens, features = arrays[0].shape
    size = features // owners
    if size != BLOCK:

        def columns(value, core):
            return jnp.concatenate(
                [
                    lax.dynamic_slice_in_dim(value, ((2 * r + core) ^ me[0]) * size, size, 1)
                    for r in range(half)[::-1]
                ],
                axis=1,
            )

        return (
            jnp.stack([columns(a, 0) for a in arrays]),
            jnp.stack([columns(a, 1) for a in arrays]).astype(WIDE),
        )
    shape = (len(arrays), tokens, half * size)
    return pl.pallas_call(
        pick_kernel,
        in_specs=[pl.BlockSpec(memory_space=pltpu.SMEM)]
        + [pl.BlockSpec(memory_space=pltpu.VMEM)] * len(arrays),
        out_specs=[pl.BlockSpec(memory_space=pltpu.VMEM)] * 2,
        out_shape=[jax.ShapeDtypeStruct(shape, NARROW), jax.ShapeDtypeStruct(shape, WIDE)],
        name="pick_columns",
    )(me, *arrays)


def norm_kernel(x_ref, gain1, bias1, gain2, bias2, attn_ref, mlp_ref, unit_ref, rate_ref):
    x = x_ref[...].astype(WIDE)
    centered = x - jnp.mean(x, axis=-1, keepdims=True)
    rate = lax.rsqrt(jnp.mean(centered * centered, axis=-1, keepdims=True) + EPSILON)
    unit = centered * rate
    unit_ref[...] = unit
    rate_ref[...] = jnp.broadcast_to(rate, rate_ref.shape)
    for gain, bias, out in ((gain1, bias1, attn_ref), (gain2, bias2, mlp_ref)):
        out[...] = (unit * gain[...].astype(WIDE) + bias[...].astype(WIDE)).astype(NARROW)


def two_norms(inputs, *gains):
    tokens = inputs.shape[0]
    rows = tokens // 4
    by_rows = pl.BlockSpec((rows, D), lambda i: (i, 0))
    return pl.pallas_call(
        norm_kernel,
        grid=(4,),
        in_specs=[by_rows] + [whole_spec((1, D))] * 4,
        out_specs=[by_rows, by_rows, by_rows, pl.BlockSpec((rows, 128), lambda i: (i, 0))],
        out_shape=[
            jax.ShapeDtypeStruct((tokens, D), NARROW),
            jax.ShapeDtypeStruct((tokens, D), NARROW),
            jax.ShapeDtypeStruct((tokens, D), WIDE),
            jax.ShapeDtypeStruct((tokens, 128), WIDE),
        ],
        name="two_norms",
    )(inputs, *gains)


def up_kernel(
    half, me_ref, x_ref, weight_ref, bias_ref, act_ref, slope_ref, keep_ref, send_ref
):
    step = pl.program_id(0)
    up = plain_dot(x_ref[...], weight_ref[...], ROWS_COLS) + bias_ref[...].astype(WIDE)
    below = 0.5 * (1.0 + lax.erf(up * (0.5**0.5)))
    act = (up * below).astype(NARROW)
    act_ref[...] = act
    slope_ref[...] = below + up * jnp.exp(-0.5 * up * up) * ((2.0 * math.pi) ** -0.5)

    @pl.when(step < half)
    def _():
        for i in range(keep_ref.shape[0]):
            keep_ref[i] = act[:, i * BLOCK : (i + 1) * BLOCK]

    @pl.when(step >= half)
    def _():
        wide = act.astype(WIDE)
        for i in range(send_ref.shape[0]):
            send_ref[i] = wide[:, i * BLOCK : (i + 1) * BLOCK]


def mlp_up(mlp_in, up_weight, up_bias, me):
    owners = lax.axis_size("batch")
    tokens = mlp_in.shape[0]
    half = owners // 2
    each = FF // owners
    subs = each // BLOCK

    def natural(i, me):
        return (0, (2 * (i % half) + i // half) ^ me[0])

    return pl.pallas_call(
        partial(up_kernel, half),
        grid_spec=pltpu.PrefetchScalarGridSpec(
            num_scalar_prefetch=1,
            grid=(owners,),
            in_specs=[
                pl.BlockSpec((tokens, D), lambda i, me: (0, 0)),
                pl.BlockSpec((D, each), natural),
                pl.BlockSpec((1, each), natural),
            ],
            out_specs=[
                pl.BlockSpec((tokens, each), natural),
                pl.BlockSpec((tokens, each), natural),
                pl.BlockSpec(
                    (subs, tokens, BLOCK),
                    lambda i, me: (0, 0, half - 1 - jnp.minimum(i, half - 1)),
                ),
                pl.BlockSpec(
                    (subs, tokens, BLOCK),
                    lambda i, me: (0, 0, half - 1 - jnp.maximum(i - half, 0)),
                ),
            ],
        ),
        out_shape=[
            jax.ShapeDtypeStruct((tokens, FF), NARROW),
            jax.ShapeDtypeStruct((tokens, FF), WIDE),
            jax.ShapeDtypeStruct((subs, tokens, half * BLOCK), NARROW),
            jax.ShapeDtypeStruct((subs, tokens, half * BLOCK), WIDE),
        ],
        name="mlp_up",
    )(me, mlp_in, up_weight, up_bias)


def back_kernel(
    cot_ref, down_ref, up_ref, act_ref, slope_ref, grad_ref, send_ref, sums_ref, out_ref, norm_ref
):
    step = pl.program_id(0)
    down = down_ref[...]
    grad = plain_dot(cot_ref[...], down, ROWS_ROWS) * slope_ref[...]
    grad = grad.astype(NARROW)
    grad_ref[...] = grad
    wide = grad.astype(WIDE)
    send_ref[...] = wide
    sums_ref[...] = jnp.sum(wide, axis=0, keepdims=True)
    out = plain_dot(act_ref[...], down, ROWS_COLS)
    norm = plain_dot(grad, up_ref[...], ROWS_ROWS)

    @pl.when(step == 0)
    def _():
        out_ref[...] = out
        norm_ref[...] = norm

    @pl.when(step > 0)
    def _():
        out_ref[...] += out
        norm_ref[...] += norm


def mlp_back(cot, down_weight, up_weight, act, slope):
    tokens = cot.shape[0]
    each = 1024
    by_column = pl.BlockSpec((tokens, each), lambda i: (0, i))
    total = whole_spec((tokens, D))
    return pl.pallas_call(
        back_kernel,
        grid=(FF // each,),
        in_specs=[
            total,
            pl.BlockSpec((each, D), lambda i: (i, 0)),
            pl.BlockSpec((D, each), lambda i: (0, i)),
            by_column,
            by_column,
        ],
        out_specs=[
            by_column,
            by_column,
            pl.BlockSpec((1, each), lambda i: (0, i)),
            total,
            total,
        ],
        out_shape=[
            jax.ShapeDtypeStruct((tokens, FF), NARROW),
            jax.ShapeDtypeStruct((tokens, FF), WIDE),
            jax.ShapeDtypeStruct((1, FF), WIDE),
            jax.ShapeDtypeStruct((tokens, D), WIDE),
            jax.ShapeDtypeStruct((tokens, D), WIDE),
        ],
        name="mlp_back",
    )(cot, down_weight, up_weight, act, slope)


def output_kernel(low_ref, weight_ref, x_ref, mlp_ref, dense_ref, down_ref, out_ref):
    attn = plain_dot(low_ref[...], weight_ref[...], ROWS_COLS) + dense_ref[...].astype(WIDE)
    mlp = mlp_ref[...] + down_ref[...].astype(WIDE)
    out_ref[...] = (x_ref[...].astype(WIDE) + attn + mlp).astype(NARROW)


def layer_output(low, dense_weight, inputs, mlp_out, *biases):
    tokens = inputs.shape[0]
    each = 512
    by_column = pl.BlockSpec((tokens, each), lambda i: (0, i))
    return pl.pallas_call(
        output_kernel,
        grid=(D // each,),
        in_specs=[
            whole_spec((tokens, D)),
            pl.BlockSpec((D, each), lambda i: (0, i)),
            by_column,
            by_column,
            pl.BlockSpec((1, each), lambda i: (0, i)),
            pl.BlockSpec((1, each), lambda i: (0, i)),
        ],
        out_specs=by_column,
        out_shape=jax.ShapeDtypeStruct((tokens, D), NARROW),
        name="layer_output",
    )(low, dense_weight, inputs, mlp_out, *biases)


def norm_back_kernel(
    qkv_ref,
    weight_ref,
    mlp_ref,
    unit_ref,
    rate_ref,
    cot_ref,
    gain1,
    gain2,
    grad_ref,
    sums_ref,
    qkv_sums,
):
    step = pl.program_id(0)
    qkv = qkv_ref[...]
    qkv_sums[...] = jnp.sum(qkv.astype(WIDE), axis=0, keepdims=True)
    part = plain_dot(qkv, weight_ref[...], ROWS_ROWS)

    @pl.when(step == 0)
    def _():
        grad_ref[...] = part

    @pl.when(step > 0)
    def _():
        grad_ref[...] += part

    @pl.when(step == pl.num_programs(0) - 1)
    def _():
        size = 64
        gain_attn, gain_mlp = gain1[...].astype(WIDE), gain2[...].astype(WIDE)
        totals = [jnp.zeros((1, D), WIDE)] * 5
        for k in range(grad_ref.shape[0] // size):
            rows = pl.ds(k * size, size)
            attn, mlp, unit = grad_ref[rows, :], mlp_ref[rows, :], unit_ref[rows, :]
            cot = cot_ref[rows, :].astype(WIDE)
            together = attn * gain_attn + mlp * gain_mlp
            grad_ref[rows, :] = cot + rate_ref[rows, 0:1] * (
                together
                - jnp.mean(together, axis=-1, keepdims=True)
                - unit * jnp.mean(together * unit, axis=-1, keepdims=True)
            )
            for i, value in enumerate((attn * unit, attn, mlp * unit, mlp, cot)):
                totals[i] = totals[i] + jnp.sum(value, axis=0, keepdims=True)
        for i, value in enumerate(totals):
            sums_ref[i : i + 1, :] = value
        sums_ref[5:8, :] = jnp.zeros((3, D), WIDE)


def norm_back(qkv_grad, qkv_weight, mlp_norm_grad, unit, rate, cot, gain1, gain2):
    tokens = cot.shape[0]
    each = 512
    total = whole_spec((tokens, D))
    return pl.pallas_call(
        norm_back_kernel,
        grid=(3 * D // each,),
        in_specs=[
            pl.BlockSpec((tokens, each), lambda i: (0, i)),
            pl.BlockSpec((D, each), lambda i: (0, i)),
            total,
            total,
            whole_spec(rate.shape),
            total,
            whole_spec((1, D)),
            whole_spec((1, D)),
        ],
        out_specs=[total, whole_spec((8, D)), pl.BlockSpec((1, each), lambda i: (0, i))],
        out_shape=[
            jax.ShapeDtypeStruct((tokens, D), WIDE),
            jax.ShapeDtypeStruct((8, D), WIDE),
            jax.ShapeDtypeStruct((1, 3 * D), WIDE),
        ],
        name="norm_back",
    )(qkv_grad, qkv_weight, mlp_norm_grad, unit, rate, cot, gain1, gain2)


def dct_matrix():
    rows = np.arange(HEAD)[:, None]
    columns = np.arange(HEAD)[None, :]
    cosines = np.cos(np.pi * (columns + 0.5) * rows / HEAD) * np.sqrt(2.0 / HEAD)
    return np.where(rows == 0, cosines * np.sqrt(0.5), cosines).astype(np.float32)


def attention_tables(positions, points, weights):
    half_rot = ROT // 2
    lane = jnp.arange(PAIR) % HEAD
    freq = ROTARY_BASE ** (-2.0 * (lane % half_rot).astype(WIDE) / ROT)
    angles = positions.astype(WIDE)[:, None] * freq[None, :]
    sin = jnp.sin(angles)
    tables = jnp.stack(
        [
            jnp.where(lane < ROT, jnp.cos(angles), 1.0),
            jnp.where(lane < half_rot, -sin, 0.0),
            jnp.where((lane >= half_rot) & (lane < ROT), sin, 0.0),
        ]
    )
    mix = HEAD ** (-0.25) * jnp.einsum(
        "kn,km->nm", dct_matrix(), points, precision=lax.Precision.HIGHEST
    )
    side = jnp.arange(PAIR) // HEAD
    mix = jnp.where(side[:, None] == side[None, :], jnp.tile(mix, (2, 2)), 0.0)
    return tables, mix, jnp.tile(weights, 2)[None, :]


def lane_is_low(shape):
    return lax.broadcasted_iota(jnp.int32, shape, len(shape) - 1) % PAIR < HEAD


def halves(full):
    return jnp.where(lane_is_low((HEAD, PAIR)), full[:HEAD], full[HEAD:])


def spread_pair(block):
    low = lane_is_low(block.shape)
    zero = jnp.zeros_like(block)
    return jnp.concatenate([jnp.where(low, block, zero), jnp.where(low, zero, block)], axis=0)


def one_head(tile, head):
    low = lane_is_low(tile.shape)
    zero = jnp.zeros_like(tile)
    return jnp.where(low, tile, zero) if head == 0 else jnp.where(low, zero, tile)


def in_two(value):
    high = value.astype(NARROW)
    return high, (value - high.astype(WIDE)).astype(NARROW)


def fine_dot(left, right, dims):
    left_high, left_low = in_two(left)
    right_high, right_low = in_two(right)
    return (
        plain_dot(left_high, right_high, dims)
        + plain_dot(left_low, right_high, dims)
        + plain_dot(left_high, right_low, dims)
    )


def head_sums(tile):
    rows = lax.broadcasted_iota(jnp.int32, (PAIR, PAIR), 0) // HEAD
    columns = lax.broadcasted_iota(jnp.int32, (PAIR, PAIR), 1) // HEAD
    ones = (rows == columns).astype(WIDE).astype(NARROW)
    high, low = in_two(tile)
    return plain_dot(
        jnp.concatenate([high, low], axis=1), jnp.concatenate([ones, ones], axis=0), ROWS_COLS
    )


def turn(tile, cos, sin_up, sin_down):
    half_rot = ROT // 2
    return (
        tile * cos
        + pltpu.roll(tile, PAIR - half_rot, 1) * sin_up
        + pltpu.roll(tile, half_rot, 1) * sin_down
    )


def turn_back(tile, cos, sin_up, sin_down):
    half_rot = ROT // 2
    return (
        tile * cos
        + pltpu.roll(tile * sin_up, half_rot, 1)
        + pltpu.roll(tile * sin_down, PAIR - half_rot, 1)
    )


def all_rows(tables_ref, seqs):
    return [jnp.concatenate([tables_ref[k]] * seqs, axis=0) for k in range(3)]


def feature_grad(grad, phi, turned, mix, tables):
    weighted = grad * phi
    back = fine_dot(weighted, mix, ROWS_ROWS) - (HEAD**-0.5) * turned * head_sums(weighted)
    return turn_back(back, *tables)


def doc_at(where, lengths_ref, b):
    start, found = 0, jnp.zeros_like(where) - 1
    for k in range(lengths_ref.shape[1]):
        found = found + jnp.where(start <= where, 1, 0)
        start = start + lengths_ref[b, k]
    return found


def same_doc_before(lengths_ref, b, first, context):
    query = first + lax.broadcasted_iota(jnp.int32, (context, context), 0)
    key = first + lax.broadcasted_iota(jnp.int32, (context, context), 1)
    same = doc_at(query, lengths_ref, b) == doc_at(key, lengths_ref, b)
    return jnp.where(same & (key <= query), 1.0, 0.0)


def in_doc_of(lengths_ref, b, first, context, where):
    rows = first + lax.broadcasted_iota(jnp.int32, (context, PAIR), 0)
    return jnp.where(doc_at(rows, lengths_ref, b) == doc_at(where, lengths_ref, b), 1.0, 0.0)


def local_kernel(
    seqs,
    lengths_ref,
    first_ref,
    attn_ref,
    weight_ref,
    bias_ref,
    tables_ref,
    mix_ref,
    wrow_ref,
    fq_ref,
    fk_ref,
    val_ref,
    phiq_ref,
    phik_ref,
    rotq_ref,
    rotk_ref,
    num_ref,
    den_ref,
    score_ref,
    carry_ref,
):
    context = tables_ref.shape[1]
    first = first_ref[0]
    mix, wrow = mix_ref[...], wrow_ref[...]
    tables = all_rows(tables_ref, seqs)
    low = lane_is_low((seqs * context, PAIR))
    block = plain_dot(attn_ref[...], weight_ref[...], ROWS_COLS) + bias_ref[...].astype(WIDE)
    one, two, three = block[:, :PAIR], block[:, PAIR : 2 * PAIR], block[:, 2 * PAIR :]
    query = jnp.where(low, one, two)
    key = pltpu.roll(jnp.where(low, three, one), HEAD, 1)
    value_all = jnp.where(low, two, three).astype(NARROW)
    val_ref[...] = value_all

    def features(raw):
        turned = turn(raw, *tables)
        power = fine_dot(turned, mix, ROWS_COLS) - (0.5 * HEAD**-0.5) * head_sums(turned * turned)
        return turned, wrow * jnp.exp(power)

    turned_q, phi_q = features(query)
    turned_k, phi_k = features(key)
    rotq_ref[...], rotk_ref[...] = turned_q, turned_k
    phiq_ref[...], phik_ref[...] = phi_q, phi_k
    fq_all, fk_all = phi_q.astype(NARROW), phi_k.astype(NARROW)
    fq_ref[...], fk_ref[...] = fq_all, fk_all
    low = lane_is_low((context, PAIR))
    for b in range(seqs):
        rows = slice(b * context, (b + 1) * context)
        fq, fk, value = fq_all[rows], fk_all[rows], value_all[rows]
        mask = same_doc_before(lengths_ref, b, first, context)
        keep = in_doc_of(lengths_ref, b, first, context, first + context - 1)
        wide_value = jnp.concatenate([value, jnp.ones_like(value)], axis=1)
        sums = []
        for h in range(2):
            scores = (plain_dot(one_head(fq, h), fk, ROWS_ROWS) * mask).astype(NARROW)
            score_ref[0, b, h] = scores
            sums.append(plain_dot(scores, wide_value, ROWS_COLS))
        num_ref[rows, :] = jnp.where(low, sums[0][:, :PAIR], sums[1][:, :PAIR])
        den_ref[rows, :] = jnp.where(low, sums[0][:, PAIR:], sums[1][:, PAIR:])
        kept = fk * keep.astype(NARROW)
        carry_ref[b, 0, :HEAD, :] = halves(plain_dot(kept, value, COLS_COLS))
        norm = jnp.sum(kept.astype(WIDE), axis=0, keepdims=True)
        carry_ref[b, 0, HEAD:, :] = jnp.broadcast_to(norm, (8, PAIR))


def middle_kernel(
    seqs,
    lengths_ref,
    first_ref,
    cot_ref,
    dense_ref,
    fq_ref,
    fk_ref,
    val_ref,
    phiq_ref,
    rotq_ref,
    num_ref,
    den_ref,
    score_ref,
    carry_ref,
    tables_ref,
    mix_ref,
    low_ref,
    gradq_ref,
    gradk_ref,
    gradv_ref,
    out_ref,
):
    context = tables_ref.shape[1]
    first = first_ref[0]
    mix = mix_ref[...]
    tables = all_rows(tables_ref, seqs)
    low = lane_is_low((context, PAIR))
    back_all = plain_dot(cot_ref[...], dense_ref[...], ROWS_ROWS)
    grads_q = []
    for b in range(seqs):
        rows = pl.ds(b * context, context)
        fq, fk, value = fq_ref[rows, :], fk_ref[rows, :], val_ref[rows, :]
        use = in_doc_of(lengths_ref, b, first, context, first - 1)
        state = spread_pair(carry_ref[b, 0, :HEAD, :].astype(NARROW))
        norm = carry_ref[b, 0, HEAD : HEAD + 1, :]
        wide_fq = fq.astype(WIDE)
        num = num_ref[rows, :] + use * plain_dot(fq, state, ROWS_COLS)
        den = den_ref[rows, :] + use * head_sums(wide_fq * norm)
        heads_out = num / den
        low_ref[rows, :] = heads_out.astype(NARROW)
        back = back_all[b * context : (b + 1) * context]
        num_grad = (back / den).astype(NARROW)
        den_grad = -head_sums(back * heads_out) / den
        mask = same_doc_before(lengths_ref, b, first, context)
        parts_q, parts_k, parts_v = [], [], []
        for h in range(2):
            column = den_grad[:, h * HEAD : h * HEAD + 1]
            score_grad = plain_dot(one_head(num_grad, h), value, ROWS_ROWS) + column
            score_grad = (score_grad * mask).astype(NARROW)
            parts_q.append(plain_dot(score_grad, fk, ROWS_COLS))
            parts_k.append(plain_dot(score_grad, fq, COLS_COLS))
            parts_v.append(plain_dot(score_ref[0, b, h], num_grad, COLS_COLS))
        gradk_ref[rows, :] = jnp.where(low, parts_k[0], parts_k[1])
        gradv_ref[rows, :] = jnp.where(low, parts_v[0], parts_v[1])
        num_used = num_grad * use.astype(NARROW)
        den_used = den_grad * use
        grads_q.append(
            jnp.where(low, parts_q[0], parts_q[1])
            + plain_dot(num_used, state, ROWS_ROWS)
            + den_used * norm
        )
        out_ref[b, 0, :HEAD, :] = halves(plain_dot(fq, num_used, COLS_COLS))
        norm_grad = jnp.sum(den_used * wide_fq, axis=0, keepdims=True)
        out_ref[b, 0, HEAD:, :] = jnp.broadcast_to(norm_grad, (8, PAIR))
    gradq_ref[...] = feature_grad(
        jnp.concatenate(grads_q, axis=0), phiq_ref[...], rotq_ref[...], mix, tables
    ).astype(NARROW)


def last_kernel(
    seqs,
    lengths_ref,
    first_ref,
    gradq_ref,
    gradk_ref,
    gradv_ref,
    fk_ref,
    val_ref,
    phik_ref,
    rotk_ref,
    carry_ref,
    tables_ref,
    mix_ref,
    out_ref,
    send_ref,
):
    context = tables_ref.shape[1]
    first = first_ref[0]
    tables = all_rows(tables_ref, seqs)
    grads_k, grads_v = [], []
    for b in range(seqs):
        rows = pl.ds(b * context, context)
        keep = in_doc_of(lengths_ref, b, first, context, first + context - 1)
        state = spread_pair(carry_ref[b, 0, :HEAD, :].astype(NARROW))
        norm = carry_ref[b, 0, HEAD : HEAD + 1, :]
        grads_k.append(
            gradk_ref[rows, :] + keep * (plain_dot(val_ref[rows, :], state, ROWS_ROWS) + norm)
        )
        grads_v.append(gradv_ref[rows, :] + keep * plain_dot(fk_ref[rows, :], state, ROWS_COLS))
    grad_k = feature_grad(
        jnp.concatenate(grads_k, axis=0), phik_ref[...], rotk_ref[...], mix_ref[...], tables
    )
    grad_k = pltpu.roll(grad_k, HEAD, 1)
    grad_v = jnp.concatenate(grads_v, axis=0)
    grad_q = gradq_ref[...].astype(WIDE)
    low = lane_is_low(grad_q.shape)
    grad = jnp.concatenate(
        [
            jnp.where(low, grad_q, grad_k),
            jnp.where(low, grad_v, grad_q),
            jnp.where(low, grad_k, grad_v),
        ],
        axis=1,
    ).astype(NARROW)
    out_ref[...] = grad
    send_ref[...] = grad.astype(WIDE)


def pass_kernel(lengths_ref, first_ref, own_ref, arrived_ref, out_ref):
    context = first_ref[1]
    for b in range(own_ref.shape[0]):
        last = doc_at(first_ref[0] + context - 1, lengths_ref, b)
        through = last == doc_at(first_ref[0] - 1, lengths_ref, b)
        out_ref[b] = own_ref[b] + jnp.where(through, arrived_ref[b], 0.0)


SMEM_SPEC = pl.BlockSpec(memory_space=pltpu.SMEM)


def pass_on(own, arrived, lengths, first):
    seqs, pairs = own.shape[:2]
    spec = pl.BlockSpec((seqs, pairs // 2, *own.shape[2:]), lambda i: (0, i, 0, 0))
    return pl.pallas_call(
        pass_kernel,
        grid=(2,),
        in_specs=[SMEM_SPEC, SMEM_SPEC, spec, spec],
        out_specs=spec,
        out_shape=jax.ShapeDtypeStruct(own.shape, WIDE),
        name="pass_carry",
    )(lengths, first, own, arrived)


def pair_spec(rows):
    return pl.BlockSpec((None, rows, PAIR), lambda i: (i, 0, 0))


def pair_shapes(tokens):
    shape = (HEADS // 2, tokens, PAIR)
    return jax.ShapeDtypeStruct(shape, NARROW), jax.ShapeDtypeStruct(shape, WIDE)


def attention_specs(seqs, context):
    carry = pl.BlockSpec((seqs, 1, HEAD + 8, PAIR), lambda i: (0, i, 0, 0))
    scores = pl.BlockSpec((1, seqs, 2, context, context), lambda i: (i, 0, 0, 0, 0))
    return carry, scores, [whole_spec((3, context, PAIR)), whole_spec((PAIR, PAIR))]


def attention_local(lengths, first, attn_in, weight, bias, tables, mix, wrow):
    seqs, context, tokens = lengths.shape[0], tables.shape[1], attn_in.shape[0]
    pairs = HEADS // 2
    carry, scores, shared = attention_specs(seqs, context)
    narrow, wide = pair_shapes(tokens)
    return pl.pallas_call(
        partial(local_kernel, seqs),
        grid=(pairs,),
        in_specs=[
            SMEM_SPEC,
            SMEM_SPEC,
            whole_spec((tokens, D)),
            pl.BlockSpec((D, 3 * PAIR), lambda i: (0, i)),
            pl.BlockSpec((1, 3 * PAIR), lambda i: (0, i)),
            *shared,
            whole_spec((1, PAIR)),
        ],
        out_specs=[pair_spec(tokens)] * 9 + [scores, carry],
        out_shape=[narrow] * 3
        + [wide] * 6
        + [
            jax.ShapeDtypeStruct((pairs, seqs, 2, context, context), NARROW),
            jax.ShapeDtypeStruct((seqs, pairs, HEAD + 8, PAIR), WIDE),
        ],
        name="attention_local",
    )(lengths, first, attn_in, weight, bias, tables, mix, wrow)


def attention_middle(lengths, first, cot, dense_weight, *rest):
    seqs, context, tokens = lengths.shape[0], rest[-2].shape[1], cot.shape[0]
    pairs = HEADS // 2
    carry, scores, shared = attention_specs(seqs, context)
    narrow, wide = pair_shapes(tokens)
    return pl.pallas_call(
        partial(middle_kernel, seqs),
        grid=(pairs,),
        in_specs=[
            SMEM_SPEC,
            SMEM_SPEC,
            whole_spec((tokens, D)),
            pl.BlockSpec((PAIR, D), lambda i: (i, 0)),
        ]
        + [pair_spec(tokens)] * 7
        + [scores, carry, *shared],
        out_specs=[pl.BlockSpec((tokens, PAIR), lambda i: (0, i))]
        + [pair_spec(tokens)] * 3
        + [carry],
        out_shape=[jax.ShapeDtypeStruct((tokens, D), NARROW), narrow, wide, wide]
        + [jax.ShapeDtypeStruct((seqs, pairs, HEAD + 8, PAIR), WIDE)],
        name="attention_middle",
    )(lengths, first, cot, dense_weight, *rest)


def attention_last(lengths, first, *rest):
    seqs, context, tokens = lengths.shape[0], rest[-2].shape[1], rest[0].shape[1]
    carry, _, shared = attention_specs(seqs, context)
    return pl.pallas_call(
        partial(last_kernel, seqs),
        grid=(HEADS // 2,),
        in_specs=[SMEM_SPEC, SMEM_SPEC] + [pair_spec(tokens)] * 7 + [carry, *shared],
        out_specs=[pl.BlockSpec((tokens, 3 * PAIR), lambda i: (0, i))] * 2,
        out_shape=[
            jax.ShapeDtypeStruct((tokens, 3 * D), NARROW),
            jax.ShapeDtypeStruct((tokens, 3 * D), WIDE),
        ],
        name="attention_last",
    )(lengths, first, *rest)


def shards(
    inputs,
    lengths,
    ln1_gain,
    ln1_bias,
    ln2_gain,
    ln2_bias,
    qkv_weight,
    qkv_bias,
    dense_weight,
    dense_bias,
    up_weight,
    up_bias,
    down_weight,
    down_bias,
    qmc_points,
    qmc_weights,
    cotangent,
):
    seqs, context = inputs.shape[:2]
    tokens = seqs * context
    owners, count, place = lax.axis_size("batch"), lax.axis_size("seq"), lax.axis_index("seq")
    bits = list(range(owners.bit_length() - 2))[::-1]
    across = D // COLUMNS
    hops = max(1, count // 2)

    line = Line()
    me = lax.axis_index("batch").astype(jnp.int32)[None]
    edge = ((place == 0) | (place == count - 1)).astype(jnp.int32)[None]
    if owners == 8 and count == 4:
        reduction = Rounds(line, edge, [2, 2, 2, 2, 1, 1, 1, 1])
    else:
        reduction = Singly(line, bits)

    def pieces(left, left_in, blocks, right, right_in, columns):
        return [
            (left, left_in, block, right, right_in, column)
            for column in columns
            for block in blocks
        ]

    def pairs(parts):
        return list(zip(parts[::2], parts[1::2]))

    inputs_flat = inputs.reshape(tokens, D)
    cot = cotangent.reshape(tokens, D)
    cot_in = swap(cot.astype(WIDE), 0)
    gains = [v[None, :] for v in (ln1_gain, ln1_bias, ln2_gain, ln2_bias)]
    attn_in, mlp_in, unit, rate = line.step(two_norms, inputs_flat, *gains)
    act, slope, act_own, act_send = line.step(mlp_up, mlp_in, up_weight, up_bias[None, :], me)
    act_in = swap(act_send, 0)
    norm_own, norm_send = line.step(lambda *a: pick(a[:2], a[2]), attn_in, mlp_in, me)
    subs = act_own.shape[0]
    down_parts = [
        pieces(act_own, act_in, range(sub, sub + 2), cot, cot_in, range(across))
        for sub in range(0, subs, 2)
    ]
    reduction.prepare(pairs(down_parts[0]))
    up_grad, up_send, up_sums, mlp_out, mlp_norm_grad = line.step(
        mlp_back, cot, down_weight, up_weight, act, slope
    )
    for part in down_parts[1:]:
        reduction.prepare(pairs(part))
    reduction.step()
    up_in = line.send(up_send, lambda a: swap(a, 0))
    norm_in = line.send(norm_send, lambda a: swap(a, 0))

    start, lengths_here = line.wait(place * context, lengths)
    first = jnp.stack([start, jnp.full((), context, jnp.int32)])
    positions = start + jnp.arange(context, dtype=jnp.int32)
    tables, mix, wrow = attention_tables(positions, qmc_points, qmc_weights)
    fq, fk, value, phi_q, phi_k, rot_q, rot_k, num, den, scores, carry = line.step(
        attention_local,
        lengths_here,
        first,
        attn_in,
        qkv_weight,
        qkv_bias[None, :],
        tables,
        mix,
        wrow,
    )
    arrived = shift_rows(carry, "seq", 1)
    up_pieces = pieces(norm_own, norm_in, [1], up_grad, up_in, range(FF // COLUMNS))
    up_pairs = pairs(up_pieces)
    reduction.prepare(up_pairs[:2])
    reduction.step()
    reduction.prepare(up_pairs[2:])
    for _ in range(hops - 1):
        passed = line.step(pass_on, carry, arrived, lengths_here, first)
        arrived = shift_rows(passed, "seq", 1)
    attn_low, grad_q, grad_k, grad_v, carry_back = line.step(
        attention_middle,
        lengths_here,
        first,
        cot,
        dense_weight,
        fq,
        fk,
        value,
        phi_q,
        rot_q,
        num,
        den,
        scores,
        arrived,
        tables,
        mix,
    )
    arrived_back = shift_rows(carry_back, "seq", -1)
    low_own, low_send = line.step(lambda *a: pick(a[:1], a[1]), attn_low, me)
    low_in = swap(low_send, 0)
    output = line.step(
        layer_output,
        attn_low,
        dense_weight,
        inputs_flat,
        mlp_out,
        dense_bias[None, :],
        down_bias[None, :],
    )
    reduction.step()
    for _ in range(hops - 1):
        passed = line.step(pass_on, carry_back, arrived_back, lengths_here, first)
        arrived_back = shift_rows(passed, "seq", -1)
    dense_pieces = pieces(low_own, low_in, [0], cot, cot_in, range(across))
    reduction.prepare(pairs(dense_pieces))
    qkv_grad, qkv_send = line.step(
        attention_last,
        lengths_here,
        first,
        grad_q,
        grad_k,
        grad_v,
        fk,
        value,
        phi_k,
        rot_k,
        arrived_back,
        tables,
        mix,
    )
    reduction.step()
    qkv_in = line.send(qkv_send, lambda a: swap(a, 0))
    input_grad, sums, qkv_sums = line.step(
        norm_back, qkv_grad, qkv_weight, mlp_norm_grad, unit, rate, cot, gains[0], gains[2]
    )
    qkv_pieces = pieces(norm_own, norm_in, [0], qkv_grad, qkv_in, range(3 * D // COLUMNS))
    qkv_pairs = pairs(qkv_pieces)
    reduction.prepare(qkv_pairs[:1])
    vectors = Vectors(
        line, (sums[0], sums[1], sums[2], sums[3], qkv_sums[0], sums[4], up_sums[0])
    )
    for pair in qkv_pairs[1:]:
        vectors.take()
        reduction.step()
        reduction.prepare([pair])
        vectors.send()
    while not reduction.finished():
        vectors.take()
        reduction.step()
        vectors.send()
    totals = reduction.results()
    (
        attn_gain_total,
        attn_shift_total,
        mlp_gain_total,
        mlp_shift_total,
        qkv_bias_total,
        bias_total,
        up_bias_total,
    ) = vectors.results()

    def next_totals(parts):
        taken = totals[: len(parts)]
        del totals[: len(parts)]
        return taken

    down_total = []
    for part in down_parts:
        taken = next_totals(part)
        each = len(part) // across
        down_total += [jnp.concatenate(taken[block::each], axis=1) for block in range(each)]
    down_total = jnp.concatenate(down_total, axis=0)
    up_total, dense_total, qkv_total = (
        jnp.concatenate(next_totals(part), axis=1)
        for part in (up_pieces, dense_pieces, qkv_pieces)
    )
    return (
        output.reshape(inputs.shape),
        input_grad.reshape(inputs.shape),
        attn_gain_total,
        attn_shift_total,
        mlp_gain_total,
        mlp_shift_total,
        qkv_total,
        qkv_bias_total,
        dense_total,
        bias_total,
        up_total,
        up_bias_total,
        down_total,
        bias_total,
    )


def solution(mesh):
    placed = (
        P("batch", "seq", None),
        P("batch", None),
        P(),
        P(),
        P(),
        P(),
        P(),
        P(),
        P(),
        P(),
        P(),
        P(),
        P(),
        P(),
        P(),
        P(),
        P("batch", "seq", None),
    )
    return jax.shard_map(
        shards,
        mesh=mesh,
        in_specs=placed,
        out_specs=(
            P("batch", "seq", None),
            P("batch", "seq", None),
            P("batch"),
            P("batch"),
            P("batch"),
            P("batch"),
            P("batch", None),
            P("batch"),
            P("batch", None),
            P("batch"),
            P("batch", None),
            P("batch"),
            P("batch", None),
            P("batch"),
        ),
        check_vma=False,
    )
```

```python
import math
from functools import partial

import jax
import jax.numpy as jnp
import numpy as np
from jax import lax
from jax.experimental import pallas as pl
from jax.experimental.pallas import tpu as pltpu
from jax.sharding import PartitionSpec as P

D = 1024
HEADS = 16
HEAD = 64
ROT = 16
FF = 4096
PAIR = 2 * HEAD
BLOCK = 128
COLUMNS = 512

EPSILON = 1e-05
ROTARY_BASE = 10000.0

UP_AT = 3 * D
LN1_GAIN, LN1_BIAS, LN2_GAIN, LN2_BIAS, DENSE, DOWN = range((UP_AT + FF) // D, (UP_AT + FF) // D + 6)

def lasting(microseconds):
    return pl.CostEstimate(
        flops=int(microseconds * 1.15e9), transcendentals=0, bytes_accessed=0
    )


ROWS_COLS = ((1,), (0,))
ROWS_ROWS = ((1,), (1,))
COLS_COLS = ((0,), (0,))
NARROW = jnp.bfloat16
WIDE = jnp.float32


def plain_dot(left, right, dims):
    return lax.dot_general(left, right, (dims, ((), ())), preferred_element_type=WIDE)


def whole_spec(shape):
    return pl.BlockSpec(shape, lambda *_: (0,) * len(shape))


def shift_rows(value, axis, by):
    count = lax.axis_size(axis)
    return lax.ppermute(
        value, axis, [(i, i + by) for i in range(count) if 0 <= i + by < count]
    )


def swap(value, bit):
    count = lax.axis_size("batch")
    return lax.ppermute(value, "batch", [(i, i ^ (1 << bit)) for i in range(count)])


def owner_order(bits):
    return sorted(
        range(1 << len(bits)), key=lambda r: tuple(-((r >> bit) & 1) for bit in bits)
    )


def line_rounds(count):
    half = count // 2
    rounds = [("in", [(k, k + 1), (count - 1 - k, count - 2 - k)], k) for k in range(half - 1)]
    rounds.append(("in", [(half - 1, half), (half, half - 1)], -1))
    for k in range(half - 2, -1, -1):
        rounds.append(("out", [(k + 1, k), (count - 2 - k, count - 1 - k)], k))
    return rounds


class Line:
    def __init__(self):
        self.last = None

    def wait(self, *values):
        if self.last is not None:
            values, _ = lax.optimization_barrier((values, self.last))
        return values

    def send(self, value, how):
        return how(*self.wait(value))

    def step(self, function, *values):
        out = function(*self.wait(*values))
        self.last = jax.tree.leaves(out)[0]
        return out


class Vectors:
    def __init__(self, line, vectors):
        owners = lax.axis_size("batch")
        me = lax.axis_index("batch")
        self.line = line
        self.sizes = [v.shape[0] // owners for v in vectors]
        pieces = jnp.concatenate([v.reshape(owners, -1) for v in vectors], axis=1)
        bits = list(range(owners.bit_length() - 1))
        rows = [lax.dynamic_slice_in_dim(pieces, r ^ me, 1, 0) for r in owner_order(bits)]
        self.held = jnp.concatenate(rows)
        count = lax.axis_size("seq")
        self.steps = [("swap", bit, 0) for bit in bits]
        self.steps += line_rounds(count) if count % 2 == 0 else []
        self.moving = None
        self.now = None
        self.send()

    def send(self):
        if self.moving is not None or not self.steps:
            return
        self.now = kind, what, _ = self.steps.pop(0)
        if kind == "swap":
            half = self.held.shape[0] // 2
            self.moving = self.line.send(self.held[:half], lambda a: swap(a, what))
            self.held = self.held[half:]
        else:
            self.moving = self.line.send(self.held, lambda a: lax.ppermute(a, "seq", what))

    def take(self):
        if self.moving is None:
            return
        kind, _, at = self.now
        if kind == "out":
            place, count = lax.axis_index("seq"), lax.axis_size("seq")
            edge = (place == at) | (place == count - 1 - at)
            self.held = self.line.step(
                lambda a, b: jnp.where(edge, b, a), self.held, self.moving
            )
        else:
            self.held = self.line.step(lambda a, b: a + b, self.held, self.moving)
        self.moving = None

    def results(self):
        while self.moving is not None or self.steps:
            self.take()
            self.send()
        if lax.axis_size("seq") % 2 and lax.axis_size("seq") > 1:
            self.held = lax.psum(self.held, "seq")
        out, at = [], 0
        for size in self.sizes:
            out.append(self.held[0, at : at + size])
            at += size
        return out


class Reduction:
    def __init__(self, line, left, right, bits):
        self.line = line
        half = left.shape[1] // 2
        send = line.step(lambda a, b: plain_dot(a, b, COLS_COLS), left[:, :half], right)
        self.held = line.step(lambda a, b: plain_dot(a, b, COLS_COLS), left[:, half:], right)
        count = lax.axis_size("seq")
        self.steps = [("swap", bit + 1, 0) for bit in bits]
        self.steps += line_rounds(count) if count % 2 == 0 else []
        self.moving = swap(send, bits[0] + 1)

    def finish(self):
        place, count = lax.axis_index("seq"), lax.axis_size("seq")
        for i, (kind, _, at) in enumerate(self.steps):
            if kind == "out":
                edge = (place == at) | (place == count - 1 - at)
                self.held = self.line.step(
                    lambda a, b: jnp.where(edge, b, a), self.held, self.moving
                )
            else:
                self.held = self.line.step(lambda a, b: a + b, self.held, self.moving)
            if i + 1 == len(self.steps):
                break
            kind, what, _ = self.steps[i + 1]
            if kind == "swap":
                half = self.held.shape[0] // 2
                self.moving = swap(self.held[:half], what)
                self.held = self.held[half:]
            else:
                self.moving = lax.ppermute(self.held, "seq", what)
        return self.held if count % 2 == 0 or count == 1 else lax.psum(self.held, "seq")


class Singly:
    def __init__(self, line, bits):
        self.line, self.bits = line, bits
        self.pieces, self.outputs = [], {}

    def prepare(self, target, pieces):
        _, _, at, size = target
        for left, left_in, block, right, right_in, (row, column) in pieces:
            wide = COLUMNS // Rounds.PARTS
            across = size[1] // wide
            starts = [((at[1] + i) * across + column) * wide for i in range(Rounds.PARTS)]
            right, right_in = (
                jnp.concatenate([value[:, k : k + wide] for k in starts], axis=1)
                for value in (right, right_in)
            )
            left = jnp.concatenate([left[block], rounded(left_in[block])], axis=0)
            right = jnp.concatenate([right, rounded(right_in)], axis=0)
            done = Reduction(self.line, left, right, self.bits)
            self.pieces.append((target, row, starts, wide, done))

    def step(self):
        pass

    def finished(self):
        return True

    def results(self):
        for (name, shape, at, size), row, starts, wide, piece in self.pieces:
            whole = self.outputs.get(name, jnp.zeros(shape, WIDE))
            total = piece.finish()
            top = at[0] * size[0] + row * total.shape[0]
            for i, k in enumerate(starts):
                whole = lax.dynamic_update_slice(
                    whole, total[:, i * wide : (i + 1) * wide], (top, k)
                )
            self.outputs[name] = whole
        return self.outputs


def rounded(arrived):
    one = jnp.where(lax.axis_index("seq") < lax.axis_size("seq"), 1.0, 0.5)
    return (arrived * one).astype(NARROW)


def product_kernel(count, *refs):
    ins, (to_x, to_y, hold_a, hold_b) = refs[: 8 * count], refs[-4:]
    for p in range(count):
        for i, (to, hold) in enumerate(((to_x, hold_a), (to_y, hold_b))):
            left, left_in, right, right_in = ins[8 * p + 4 * i : 8 * p + 4 * i + 4]
            whole = jnp.concatenate([left[0], left_in[0].astype(NARROW)], axis=0)
            right = jnp.concatenate([right[...], right_in[...].astype(NARROW)], axis=0)

            def product(first, second):
                rows = [whole[:, k * BLOCK : (k + 1) * BLOCK] for k in (first, second)]
                return plain_dot(jnp.concatenate(rows, axis=1), right, COLS_COLS)

            out = pl.ds(p * 2 * BLOCK, 2 * BLOCK)
            to[out, :] = product(0, 1 if i else 2)
            hold[out, :] = product(2 if i else 1, 3)


def round_kernel(counts, places, skip, *refs):
    first, second, inward, middle, outward = counts
    refs = list(refs)
    edge = refs.pop(0)[0] != 0

    def take(flag, count):
        return [refs.pop(0) for _ in range(count)] if flag else [None] * count

    from_x, from_y = take(first or second, 2)
    hold_a, hold_b = take(first, 2)
    kept_a, kept_b = take(second, 2)
    (sums,) = take(inward, 1)
    (from_end,) = take(inward or outward, 1)
    inner, from_middle = take(middle, 2)
    (whole,) = take(outward, 1)
    take(True, skip)
    to_x, to_y, keep_a, keep_b = take(first, 4)
    (new_sums,) = take(second, 1)
    (to_end,) = take(second or middle, 1)
    (new_inner,) = take(inward, 1)
    (new_whole,) = take(middle, 1)
    (final,) = take(outward, 1)
    for p in range(first):
        low = pl.ds(2 * p * BLOCK, BLOCK)
        high = pl.ds((2 * p + 1) * BLOCK, BLOCK)
        out = pl.ds(p * BLOCK, BLOCK)
        to_y[out, :] = hold_a[low, :] + from_x[low, :]
        to_x[out, :] = hold_b[low, :] + from_y[low, :]
        keep_a[out, :] = hold_a[high, :] + from_x[high, :]
        keep_b[out, :] = hold_b[high, :] + from_y[high, :]
    for p in range(max(second, middle)):
        for i, (kept, arrived) in enumerate(((kept_a, from_y), (kept_b, from_x))):
            out = pl.ds((2 * p + i) * BLOCK, BLOCK)
            ends = inners = None
            if p < second:
                come = pl.ds((2 * first + p) * BLOCK, BLOCK)
                ends = kept[pl.ds(p * BLOCK, BLOCK), :] + arrived[come, :]
                new_sums[out, :] = ends
            if p < middle:
                inners = inner[out, :] + from_middle[out, :]
                new_whole[out, :] = inners
            if ends is None:
                to_end[out, :] = inners
            elif inners is None:
                to_end[out, :] = ends
            else:
                to_end[out, :] = jnp.where(edge, ends, inners)
    if inward:
        new_inner[...] = sums[...] + from_end[: 2 * inward * BLOCK, :]
    for k, (row, column) in enumerate(places):
        rows = pl.ds(k * BLOCK, BLOCK)
        wide = whole.shape[1]
        total = jnp.where(edge, from_end[rows, :], whole[rows, :])
        final[row * BLOCK : (row + 1) * BLOCK, column * wide : (column + 1) * wide] = total


class Rounds:
    PARTS = 2

    def __init__(self, line, edge, counts):
        self.line, self.edge, self.counts = line, edge, counts
        self.made = self.at = 0
        self.buffers, self.moving, self.hold, self.kept = {}, {}, {}, {}
        self.sums, self.inner, self.whole, self.targets = {}, {}, {}, []
        self.outputs = {}
        self.end = self.middle = None
        self.wide = COLUMNS // self.PARTS

    def count(self, group):
        return self.counts[group] if 0 <= group < len(self.counts) else 0

    def rows_spec(self, rows, at=0):
        return pl.BlockSpec((rows, self.wide), lambda i: (at, i))

    def prepare(self, target, pieces):
        r = self.made
        self.made += 1
        self.targets.append((target, [piece[5] for piece in pieces]))
        count = len(pieces) // 2
        name, shape, at, size = target
        across = size[1] // self.wide
        args, specs = [], []
        for left, left_in, block, right, right_in, (_, column) in pieces:
            for value in (left, left_in):
                args.append(value)
                specs.append(
                    pl.BlockSpec((1, *value.shape[1:]), lambda i, block=block: (block, 0, 0))
                )
            for value in (right, right_in):
                args.append(value)
                specs.append(
                    pl.BlockSpec(
                        (value.shape[0], self.wide),
                        lambda i, c=column: (0, (at[1] + i) * across + c),
                    )
                )
        rows = 2 * count * BLOCK
        total = rows + self.count(r - 1) * BLOCK
        call = pl.pallas_call(
            partial(product_kernel, count),
            grid=(self.PARTS,),
            in_specs=specs,
            out_specs=[self.rows_spec(rows)] * 4,
            out_shape=[jax.ShapeDtypeStruct((total, COLUMNS), WIDE)] * 2
            + [jax.ShapeDtypeStruct((rows, COLUMNS), WIDE)] * 2,
            cost_estimate=lasting(5.0),
        name="piece_products",
        )
        to_x, to_y, hold_a, hold_b = self.line.step(call, *args)
        self.hold[r] = (hold_a, hold_b)
        if r:
            self.buffers[r] = (to_x, to_y)
        else:
            self.moving[r] = (swap(to_x, 1), swap(to_y, 2))

    def step(self):
        r = self.at
        self.at += 1
        counts = [self.count(r - back) for back in (0, 1, 2, 3, 4)]
        first, second, inward, middle, outward = counts
        aliases = {}
        args, specs = [self.edge], [pl.BlockSpec(memory_space=pltpu.SMEM)]

        def add(value):
            args.append(value)
            specs.append(self.rows_spec(value.shape[0]))

        if first or second:
            for value in self.moving.pop(r):
                add(value)
        if first:
            for value in self.hold.pop(r):
                add(value)
        if second:
            for value in self.kept.pop(r - 1):
                add(value)
        if inward:
            add(self.sums.pop(r - 2))
        if inward or outward:
            add(self.end)
        if middle:
            add(self.inner.pop(r - 3))
            add(self.middle)
        if outward:
            add(self.whole.pop(r - 4))
        outs, out_specs = [], []

        def out(rows, at=0, of=None):
            outs.append(jax.ShapeDtypeStruct((of or rows, COLUMNS), WIDE))
            out_specs.append(self.rows_spec(rows, at))

        ahead = self.count(r + 1)
        if ahead:
            aliases = {len(args): 0, len(args) + 1: 1}
            args += list(self.buffers.pop(r + 1))
            specs += [pl.BlockSpec(memory_space=pl.ANY)] * 2
        if first:
            for _ in range(2):
                out(first * BLOCK, 2 * ahead // first, (2 * ahead + first) * BLOCK)
            out(first * BLOCK)
            out(first * BLOCK)
        if second:
            out(2 * second * BLOCK)
        if second or middle:
            out(2 * max(second, middle) * BLOCK)
        for count in (inward, middle):
            if count:
                out(2 * count * BLOCK)
        places = ()
        if outward:
            (name, shape, at, size), places = self.targets[r - 4]
            if name in self.outputs:
                aliases[len(args)] = len(outs)
                args.append(self.outputs[name])
                specs.append(pl.BlockSpec(memory_space=pl.ANY))
            outs.append(jax.ShapeDtypeStruct(shape, WIDE))
            out_specs.append(pl.BlockSpec(size, lambda i: (at[0], at[1] + i)))
        call = pl.pallas_call(
            partial(round_kernel, counts, places, len(aliases)),
            grid=(self.PARTS,),
            in_specs=specs,
            out_specs=out_specs,
            out_shape=outs,
            input_output_aliases=aliases,
            cost_estimate=lasting(5.0),
            name="reduce_round",
        )
        got = list(self.line.step(call, *args))
        if first:
            self.moving[r + 1] = (swap(got.pop(0), 1), swap(got.pop(0), 2))
            self.kept[r] = (got.pop(0), got.pop(0))
        if second:
            self.sums[r - 1] = got.pop(0)
        if second or middle:
            self.end = lax.ppermute(got.pop(0), "seq", [(0, 1), (1, 0), (2, 3), (3, 2)])
        if inward:
            self.inner[r - 2] = got.pop(0)
            self.middle = lax.ppermute(self.inner[r - 2], "seq", [(1, 2), (2, 1)])
        if middle:
            self.whole[r - 3] = got.pop(0)
        if outward:
            self.outputs[name] = got.pop(0)

    def finished(self):
        return self.at == len(self.counts) + 4

    def results(self):
        return self.outputs


def pick_kernel(me_ref, *refs):
    ins, (keep_ref, send_ref) = refs[:-2], refs[-2:]
    half = keep_ref.shape[2] // BLOCK
    for i, ref in enumerate(ins):
        for p in range(half):
            for core in range(2):
                owner = (2 * (half - 1 - p) + core) ^ me_ref[0]
                columns = ref[:, pl.ds(pl.multiple_of(owner * BLOCK, BLOCK), BLOCK)]
                at = slice(p * BLOCK, (p + 1) * BLOCK)
                if core:
                    send_ref[i, :, at] = columns.astype(WIDE)
                else:
                    keep_ref[i, :, at] = columns


def pick(arrays, me):
    owners = lax.axis_size("batch")
    half = owners // 2
    tokens, features = arrays[0].shape
    size = features // owners
    if size != BLOCK:

        def columns(value, core):
            return jnp.concatenate(
                [
                    lax.dynamic_slice_in_dim(value, ((2 * r + core) ^ me[0]) * size, size, 1)
                    for r in range(half)[::-1]
                ],
                axis=1,
            )

        return (
            jnp.stack([columns(a, 0) for a in arrays]),
            jnp.stack([columns(a, 1) for a in arrays]).astype(WIDE),
        )
    shape = (len(arrays), tokens, half * size)
    return pl.pallas_call(
        pick_kernel,
        in_specs=[pl.BlockSpec(memory_space=pltpu.SMEM)]
        + [pl.BlockSpec(memory_space=pltpu.VMEM)] * len(arrays),
        out_specs=[pl.BlockSpec(memory_space=pltpu.VMEM)] * 2,
        out_shape=[jax.ShapeDtypeStruct(shape, NARROW), jax.ShapeDtypeStruct(shape, WIDE)],
        cost_estimate=lasting(2.0),
        name="pick_columns",
    )(me, *arrays)


def norm_kernel(x_ref, gain1, bias1, gain2, bias2, attn_ref, mlp_ref, unit_ref, rate_ref):
    x = x_ref[...].astype(WIDE)
    centered = x - jnp.mean(x, axis=-1, keepdims=True)
    rate = lax.rsqrt(jnp.mean(centered * centered, axis=-1, keepdims=True) + EPSILON)
    unit = centered * rate
    unit_ref[...] = unit
    rate_ref[...] = jnp.broadcast_to(rate, rate_ref.shape)
    for gain, bias, out in ((gain1, bias1, attn_ref), (gain2, bias2, mlp_ref)):
        out[...] = (unit * gain[...] + bias[...]).astype(NARROW)


def two_norms(inputs, row, gains):
    tokens = inputs.shape[0]
    rows = tokens // 4
    by_rows = pl.BlockSpec((rows, D), lambda i: (i, 0))
    return pl.pallas_call(
        norm_kernel,
        grid=(4,),
        in_specs=[by_rows] + [pl.BlockSpec((1, D), lambda i, k=k: (0, k)) for k in gains],
        out_specs=[by_rows, by_rows, by_rows, pl.BlockSpec((rows, 128), lambda i: (i, 0))],
        out_shape=[
            jax.ShapeDtypeStruct((tokens, D), NARROW),
            jax.ShapeDtypeStruct((tokens, D), NARROW),
            jax.ShapeDtypeStruct((tokens, D), WIDE),
            jax.ShapeDtypeStruct((tokens, 128), WIDE),
        ],
        cost_estimate=lasting(4.0),
        name="two_norms",
    )(inputs, *[row] * 4)


def up_kernel(
    half, me_ref, x_ref, weight_ref, bias_ref, act_ref, slope_ref, keep_ref, send_ref
):
    step = pl.program_id(0)
    up = plain_dot(x_ref[...], weight_ref[...], ROWS_COLS) + bias_ref[...]
    below = 0.5 * (1.0 + lax.erf(up * (0.5**0.5)))
    act = (up * below).astype(NARROW)
    act_ref[...] = act
    slope_ref[...] = below + up * jnp.exp(-0.5 * up * up) * ((2.0 * math.pi) ** -0.5)

    @pl.when(step < half)
    def _():
        for i in range(keep_ref.shape[0]):
            keep_ref[i] = act[:, i * BLOCK : (i + 1) * BLOCK]

    @pl.when(step >= half)
    def _():
        wide = act.astype(WIDE)
        for i in range(send_ref.shape[0]):
            send_ref[i] = wide[:, i * BLOCK : (i + 1) * BLOCK]


def mlp_up(mlp_in, up_weight, row, me):
    owners = lax.axis_size("batch")
    tokens = mlp_in.shape[0]
    half = owners // 2
    each = FF // owners
    subs = each // BLOCK

    def natural(i, me):
        return (0, (2 * (i % half) + i // half) ^ me[0])

    return pl.pallas_call(
        partial(up_kernel, half),
        grid_spec=pltpu.PrefetchScalarGridSpec(
            num_scalar_prefetch=1,
            grid=(owners,),
            in_specs=[
                pl.BlockSpec((tokens, D), lambda i, me: (0, 0)),
                pl.BlockSpec((D, each), natural),
                pl.BlockSpec(
                    (1, each), lambda i, me: (0, UP_AT // each + natural(i, me)[1])
                ),
            ],
            out_specs=[
                pl.BlockSpec((tokens, each), natural),
                pl.BlockSpec((tokens, each), natural),
                pl.BlockSpec(
                    (subs, tokens, BLOCK),
                    lambda i, me: (0, 0, half - 1 - jnp.minimum(i, half - 1)),
                ),
                pl.BlockSpec(
                    (subs, tokens, BLOCK),
                    lambda i, me: (0, 0, half - 1 - jnp.maximum(i - half, 0)),
                ),
            ],
        ),
        out_shape=[
            jax.ShapeDtypeStruct((tokens, FF), NARROW),
            jax.ShapeDtypeStruct((tokens, FF), WIDE),
            jax.ShapeDtypeStruct((subs, tokens, half * BLOCK), NARROW),
            jax.ShapeDtypeStruct((subs, tokens, half * BLOCK), WIDE),
        ],
        cost_estimate=lasting(11.0),
        name="mlp_up",
    )(me, mlp_in, up_weight, row)


def back_kernel(
    cot_ref, down_ref, up_ref, act_ref, slope_ref, grad_ref, send_ref, sums_ref, out_ref, norm_ref
):
    step = pl.program_id(0)
    down = down_ref[...]
    grad = plain_dot(cot_ref[...], down, ROWS_ROWS) * slope_ref[...]
    grad = grad.astype(NARROW)
    grad_ref[...] = grad
    wide = grad.astype(WIDE)
    send_ref[...] = wide
    sums_ref[...] = jnp.sum(wide, axis=0, keepdims=True)
    out = plain_dot(act_ref[...], down, ROWS_COLS)
    norm = plain_dot(grad, up_ref[...], ROWS_ROWS)

    @pl.when(step == 0)
    def _():
        out_ref[...] = out
        norm_ref[...] = norm

    @pl.when(step > 0)
    def _():
        out_ref[...] += out
        norm_ref[...] += norm


def mlp_back(cot, down_weight, up_weight, act, slope):
    tokens = cot.shape[0]
    each = 1024
    by_column = pl.BlockSpec((tokens, each), lambda i: (0, i))
    total = whole_spec((tokens, D))
    return pl.pallas_call(
        back_kernel,
        grid=(FF // each,),
        in_specs=[
            total,
            pl.BlockSpec((each, D), lambda i: (i, 0)),
            pl.BlockSpec((D, each), lambda i: (0, i)),
            by_column,
            by_column,
        ],
        out_specs=[
            by_column,
            by_column,
            pl.BlockSpec((1, each), lambda i: (0, i)),
            total,
            total,
        ],
        out_shape=[
            jax.ShapeDtypeStruct((tokens, FF), NARROW),
            jax.ShapeDtypeStruct((tokens, FF), WIDE),
            jax.ShapeDtypeStruct((1, FF), WIDE),
            jax.ShapeDtypeStruct((tokens, D), WIDE),
            jax.ShapeDtypeStruct((tokens, D), WIDE),
        ],
        cost_estimate=lasting(16.0),
        name="mlp_back",
    )(cot, down_weight, up_weight, act, slope)


def output_kernel(low_ref, weight_ref, x_ref, mlp_ref, dense_ref, down_ref, out_ref):
    attn = plain_dot(low_ref[...], weight_ref[...], ROWS_COLS) + dense_ref[...]
    mlp = mlp_ref[...] + down_ref[...]
    out_ref[...] = (x_ref[...].astype(WIDE) + attn + mlp).astype(NARROW)


def layer_output(low, dense_weight, inputs, mlp_out, row, biases):
    tokens = inputs.shape[0]
    each = 512
    by_column = pl.BlockSpec((tokens, each), lambda i: (0, i))
    return pl.pallas_call(
        output_kernel,
        grid=(D // each,),
        in_specs=[
            whole_spec((tokens, D)),
            pl.BlockSpec((D, each), lambda i: (0, i)),
            by_column,
            by_column,
        ]
        + [pl.BlockSpec((1, each), lambda i, k=k: (0, k * (D // each) + i)) for k in biases],
        out_specs=by_column,
        out_shape=jax.ShapeDtypeStruct((tokens, D), NARROW),
        cost_estimate=lasting(3.0),
        name="layer_output",
    )(low, dense_weight, inputs, mlp_out, row, row)


def norm_back_kernel(
    qkv_ref,
    weight_ref,
    mlp_ref,
    unit_ref,
    rate_ref,
    cot_ref,
    gain1,
    gain2,
    grad_ref,
    sums_ref,
    qkv_sums,
):
    step = pl.program_id(0)
    qkv = qkv_ref[...]
    qkv_sums[...] = jnp.sum(qkv.astype(WIDE), axis=0, keepdims=True)
    part = plain_dot(qkv, weight_ref[...], ROWS_ROWS)

    @pl.when(step == 0)
    def _():
        grad_ref[...] = part

    @pl.when(step > 0)
    def _():
        grad_ref[...] += part

    @pl.when(step == pl.num_programs(0) - 1)
    def _():
        size = 64
        gain_attn, gain_mlp = gain1[...], gain2[...]
        totals = [jnp.zeros((1, D), WIDE)] * 5
        for k in range(grad_ref.shape[0] // size):
            rows = pl.ds(k * size, size)
            attn, mlp, unit = grad_ref[rows, :], mlp_ref[rows, :], unit_ref[rows, :]
            cot = cot_ref[rows, :].astype(WIDE)
            together = attn * gain_attn + mlp * gain_mlp
            grad_ref[rows, :] = cot + rate_ref[rows, 0:1] * (
                together
                - jnp.mean(together, axis=-1, keepdims=True)
                - unit * jnp.mean(together * unit, axis=-1, keepdims=True)
            )
            for i, value in enumerate((attn * unit, attn, mlp * unit, mlp, cot)):
                totals[i] = totals[i] + jnp.sum(value, axis=0, keepdims=True)
        for i, value in enumerate(totals):
            sums_ref[i : i + 1, :] = value
        sums_ref[5:8, :] = jnp.zeros((3, D), WIDE)


def norm_back(qkv_grad, qkv_weight, mlp_norm_grad, unit, rate, cot, row, gains):
    tokens = cot.shape[0]
    each = 512
    total = whole_spec((tokens, D))
    return pl.pallas_call(
        norm_back_kernel,
        grid=(3 * D // each,),
        in_specs=[
            pl.BlockSpec((tokens, each), lambda i: (0, i)),
            pl.BlockSpec((D, each), lambda i: (0, i)),
            total,
            total,
            whole_spec(rate.shape),
            total,
        ]
        + [pl.BlockSpec((1, D), lambda i, k=k: (0, k)) for k in gains],
        out_specs=[total, whole_spec((8, D)), pl.BlockSpec((1, each), lambda i: (0, i))],
        out_shape=[
            jax.ShapeDtypeStruct((tokens, D), WIDE),
            jax.ShapeDtypeStruct((8, D), WIDE),
            jax.ShapeDtypeStruct((1, 3 * D), WIDE),
        ],
        cost_estimate=lasting(9.0),
        name="norm_back",
    )(qkv_grad, qkv_weight, mlp_norm_grad, unit, rate, cot, row, row)


def dct_matrix():
    rows = np.arange(HEAD)[:, None]
    columns = np.arange(HEAD)[None, :]
    cosines = np.cos(np.pi * (columns + 0.5) * rows / HEAD) * np.sqrt(2.0 / HEAD)
    return np.where(rows == 0, cosines * np.sqrt(0.5), cosines).astype(np.float32)


def attention_tables(positions, points, weights):
    half_rot = ROT // 2
    lane = jnp.arange(PAIR) % HEAD
    freq = ROTARY_BASE ** (-2.0 * (lane % half_rot).astype(WIDE) / ROT)
    angles = positions.astype(WIDE)[:, None] * freq[None, :]
    sin = jnp.sin(angles)
    tables = jnp.stack(
        [
            jnp.where(lane < ROT, jnp.cos(angles), 1.0),
            jnp.where(lane < half_rot, -sin, 0.0),
            jnp.where((lane >= half_rot) & (lane < ROT), sin, 0.0),
        ]
    )
    mix = HEAD ** (-0.25) * jnp.einsum(
        "kn,km->nm", dct_matrix(), points, precision=lax.Precision.HIGHEST
    )
    side = jnp.arange(PAIR) // HEAD
    mix = jnp.where(side[:, None] == side[None, :], jnp.tile(mix, (2, 2)), 0.0)
    return tables, mix, jnp.tile(weights, 2)[None, :]


def lane_is_low(shape):
    return lax.broadcasted_iota(jnp.int32, shape, len(shape) - 1) % PAIR < HEAD


def halves(full):
    return jnp.where(lane_is_low((HEAD, PAIR)), full[:HEAD], full[HEAD:])


def spread_pair(block):
    low = lane_is_low(block.shape)
    zero = jnp.zeros_like(block)
    return jnp.concatenate([jnp.where(low, block, zero), jnp.where(low, zero, block)], axis=0)


def one_head(tile, head):
    low = lane_is_low(tile.shape)
    zero = jnp.zeros_like(tile)
    return jnp.where(low, tile, zero) if head == 0 else jnp.where(low, zero, tile)


def in_two(value):
    high = value.astype(NARROW)
    return high, (value - high.astype(WIDE)).astype(NARROW)


def fine_dot(left, right, dims):
    left_high, left_low = in_two(left)
    right_high, right_low = in_two(right)
    return (
        plain_dot(left_high, right_high, dims)
        + plain_dot(left_low, right_high, dims)
        + plain_dot(left_high, right_low, dims)
    )


def head_sums(tile):
    rows = lax.broadcasted_iota(jnp.int32, (PAIR, PAIR), 0) // HEAD
    columns = lax.broadcasted_iota(jnp.int32, (PAIR, PAIR), 1) // HEAD
    ones = (rows == columns).astype(WIDE).astype(NARROW)
    high, low = in_two(tile)
    return plain_dot(
        jnp.concatenate([high, low], axis=1), jnp.concatenate([ones, ones], axis=0), ROWS_COLS
    )


def turn(tile, cos, sin_up, sin_down):
    half_rot = ROT // 2
    return (
        tile * cos
        + pltpu.roll(tile, PAIR - half_rot, 1) * sin_up
        + pltpu.roll(tile, half_rot, 1) * sin_down
    )


def turn_back(tile, cos, sin_up, sin_down):
    half_rot = ROT // 2
    return (
        tile * cos
        + pltpu.roll(tile * sin_up, half_rot, 1)
        + pltpu.roll(tile * sin_down, PAIR - half_rot, 1)
    )


def all_rows(tables_ref, seqs):
    return [jnp.concatenate([tables_ref[k]] * seqs, axis=0) for k in range(3)]


def feature_grad(grad, phi, turned, mix, tables):
    weighted = grad * phi
    back = fine_dot(weighted, mix, ROWS_ROWS) - (HEAD**-0.5) * turned * head_sums(weighted)
    return turn_back(back, *tables)


def doc_at(where, lengths_ref, b):
    start, found = 0, jnp.zeros_like(where) - 1
    for k in range(lengths_ref.shape[1]):
        found = found + jnp.where(start <= where, 1, 0)
        start = start + lengths_ref[b, k]
    return found


def same_doc_before(lengths_ref, b, first, context):
    query = first + lax.broadcasted_iota(jnp.int32, (context, context), 0)
    key = first + lax.broadcasted_iota(jnp.int32, (context, context), 1)
    same = doc_at(query, lengths_ref, b) == doc_at(key, lengths_ref, b)
    return jnp.where(same & (key <= query), 1.0, 0.0)


def in_doc_of(lengths_ref, b, first, context, where):
    rows = first + lax.broadcasted_iota(jnp.int32, (context, PAIR), 0)
    return jnp.where(doc_at(rows, lengths_ref, b) == doc_at(where, lengths_ref, b), 1.0, 0.0)


def local_kernel(
    seqs,
    lengths_ref,
    first_ref,
    attn_ref,
    weight_ref,
    bias_ref,
    tables_ref,
    mix_ref,
    wrow_ref,
    fq_ref,
    fk_ref,
    val_ref,
    phiq_ref,
    phik_ref,
    rotq_ref,
    rotk_ref,
    num_ref,
    den_ref,
    score_ref,
    carry_ref,
):
    context = tables_ref.shape[1]
    first = first_ref[0]
    mix, wrow = mix_ref[...], wrow_ref[...]
    tables = all_rows(tables_ref, seqs)
    low = lane_is_low((seqs * context, PAIR))
    block = plain_dot(attn_ref[...], weight_ref[...], ROWS_COLS) + bias_ref[...]
    one, two, three = block[:, :PAIR], block[:, PAIR : 2 * PAIR], block[:, 2 * PAIR :]
    query = jnp.where(low, one, two)
    key = pltpu.roll(jnp.where(low, three, one), HEAD, 1)
    value_all = jnp.where(low, two, three).astype(NARROW)
    val_ref[...] = value_all

    def features(raw):
        turned = turn(raw, *tables)
        power = fine_dot(turned, mix, ROWS_COLS) - (0.5 * HEAD**-0.5) * head_sums(turned * turned)
        return turned, wrow * jnp.exp(power)

    turned_q, phi_q = features(query)
    turned_k, phi_k = features(key)
    rotq_ref[...], rotk_ref[...] = turned_q, turned_k
    phiq_ref[...], phik_ref[...] = phi_q, phi_k
    fq_all, fk_all = phi_q.astype(NARROW), phi_k.astype(NARROW)
    fq_ref[...], fk_ref[...] = fq_all, fk_all
    low = lane_is_low((context, PAIR))
    for b in range(seqs):
        rows = slice(b * context, (b + 1) * context)
        fq, fk, value = fq_all[rows], fk_all[rows], value_all[rows]
        mask = same_doc_before(lengths_ref, b, first, context)
        keep = in_doc_of(lengths_ref, b, first, context, first + context - 1)
        wide_value = jnp.concatenate([value, jnp.ones_like(value)], axis=1)
        sums = []
        for h in range(2):
            scores = (plain_dot(one_head(fq, h), fk, ROWS_ROWS) * mask).astype(NARROW)
            score_ref[0, b, h] = scores
            sums.append(plain_dot(scores, wide_value, ROWS_COLS))
        num_ref[rows, :] = jnp.where(low, sums[0][:, :PAIR], sums[1][:, :PAIR])
        den_ref[rows, :] = jnp.where(low, sums[0][:, PAIR:], sums[1][:, PAIR:])
        kept = fk * keep.astype(NARROW)
        carry_ref[b, 0, :HEAD, :] = halves(plain_dot(kept, value, COLS_COLS))
        norm = jnp.sum(kept.astype(WIDE), axis=0, keepdims=True)
        carry_ref[b, 0, HEAD:, :] = jnp.broadcast_to(norm, (8, PAIR))


def middle_kernel(
    seqs,
    lengths_ref,
    first_ref,
    cot_ref,
    dense_ref,
    fq_ref,
    fk_ref,
    val_ref,
    phiq_ref,
    rotq_ref,
    num_ref,
    den_ref,
    score_ref,
    carry_ref,
    tables_ref,
    mix_ref,
    low_ref,
    gradq_ref,
    gradk_ref,
    gradv_ref,
    out_ref,
):
    context = tables_ref.shape[1]
    first = first_ref[0]
    mix = mix_ref[...]
    tables = all_rows(tables_ref, seqs)
    low = lane_is_low((context, PAIR))
    back_all = plain_dot(cot_ref[...], dense_ref[...], ROWS_ROWS)
    grads_q = []
    for b in range(seqs):
        rows = pl.ds(b * context, context)
        fq, fk, value = fq_ref[rows, :], fk_ref[rows, :], val_ref[rows, :]
        use = in_doc_of(lengths_ref, b, first, context, first - 1)
        state = spread_pair(carry_ref[b, 0, :HEAD, :].astype(NARROW))
        norm = carry_ref[b, 0, HEAD : HEAD + 1, :]
        wide_fq = fq.astype(WIDE)
        num = num_ref[rows, :] + use * plain_dot(fq, state, ROWS_COLS)
        den = den_ref[rows, :] + use * head_sums(wide_fq * norm)
        heads_out = num / den
        low_ref[rows, :] = heads_out.astype(NARROW)
        back = back_all[b * context : (b + 1) * context]
        num_grad = (back / den).astype(NARROW)
        den_grad = -head_sums(back * heads_out) / den
        mask = same_doc_before(lengths_ref, b, first, context)
        parts_q, parts_k, parts_v = [], [], []
        for h in range(2):
            column = den_grad[:, h * HEAD : h * HEAD + 1]
            score_grad = plain_dot(one_head(num_grad, h), value, ROWS_ROWS) + column
            score_grad = (score_grad * mask).astype(NARROW)
            parts_q.append(plain_dot(score_grad, fk, ROWS_COLS))
            parts_k.append(plain_dot(score_grad, fq, COLS_COLS))
            parts_v.append(plain_dot(score_ref[0, b, h], num_grad, COLS_COLS))
        gradk_ref[rows, :] = jnp.where(low, parts_k[0], parts_k[1])
        gradv_ref[rows, :] = jnp.where(low, parts_v[0], parts_v[1])
        num_used = num_grad * use.astype(NARROW)
        den_used = den_grad * use
        grads_q.append(
            jnp.where(low, parts_q[0], parts_q[1])
            + plain_dot(num_used, state, ROWS_ROWS)
            + den_used * norm
        )
        out_ref[b, 0, :HEAD, :] = halves(plain_dot(fq, num_used, COLS_COLS))
        norm_grad = jnp.sum(den_used * wide_fq, axis=0, keepdims=True)
        out_ref[b, 0, HEAD:, :] = jnp.broadcast_to(norm_grad, (8, PAIR))
    gradq_ref[...] = feature_grad(
        jnp.concatenate(grads_q, axis=0), phiq_ref[...], rotq_ref[...], mix, tables
    ).astype(NARROW)


def last_kernel(
    seqs,
    lengths_ref,
    first_ref,
    gradq_ref,
    gradk_ref,
    gradv_ref,
    fk_ref,
    val_ref,
    phik_ref,
    rotk_ref,
    carry_ref,
    tables_ref,
    mix_ref,
    out_ref,
    send_ref,
):
    context = tables_ref.shape[1]
    first = first_ref[0]
    tables = all_rows(tables_ref, seqs)
    grads_k, grads_v = [], []
    for b in range(seqs):
        rows = pl.ds(b * context, context)
        keep = in_doc_of(lengths_ref, b, first, context, first + context - 1)
        state = spread_pair(carry_ref[b, 0, :HEAD, :].astype(NARROW))
        norm = carry_ref[b, 0, HEAD : HEAD + 1, :]
        grads_k.append(
            gradk_ref[rows, :] + keep * (plain_dot(val_ref[rows, :], state, ROWS_ROWS) + norm)
        )
        grads_v.append(gradv_ref[rows, :] + keep * plain_dot(fk_ref[rows, :], state, ROWS_COLS))
    grad_k = feature_grad(
        jnp.concatenate(grads_k, axis=0), phik_ref[...], rotk_ref[...], mix_ref[...], tables
    )
    grad_k = pltpu.roll(grad_k, HEAD, 1)
    grad_v = jnp.concatenate(grads_v, axis=0)
    grad_q = gradq_ref[...].astype(WIDE)
    low = lane_is_low(grad_q.shape)
    grad = jnp.concatenate(
        [
            jnp.where(low, grad_q, grad_k),
            jnp.where(low, grad_v, grad_q),
            jnp.where(low, grad_k, grad_v),
        ],
        axis=1,
    ).astype(NARROW)
    out_ref[...] = grad
    send_ref[...] = grad.astype(WIDE)


def pass_kernel(lengths_ref, first_ref, own_ref, arrived_ref, out_ref):
    context = first_ref[1]
    for b in range(own_ref.shape[0]):
        last = doc_at(first_ref[0] + context - 1, lengths_ref, b)
        through = last == doc_at(first_ref[0] - 1, lengths_ref, b)
        out_ref[b] = own_ref[b] + jnp.where(through, arrived_ref[b], 0.0)


SMEM_SPEC = pl.BlockSpec(memory_space=pltpu.SMEM)


def pass_on(own, arrived, lengths, first):
    seqs, pairs = own.shape[:2]
    spec = pl.BlockSpec((seqs, pairs // 2, *own.shape[2:]), lambda i: (0, i, 0, 0))
    return pl.pallas_call(
        pass_kernel,
        grid=(2,),
        in_specs=[SMEM_SPEC, SMEM_SPEC, spec, spec],
        out_specs=spec,
        out_shape=jax.ShapeDtypeStruct(own.shape, WIDE),
        cost_estimate=lasting(2.0),
        name="pass_carry",
    )(lengths, first, own, arrived)


def pair_spec(rows):
    return pl.BlockSpec((None, rows, PAIR), lambda i: (i, 0, 0))


def pair_shapes(tokens):
    shape = (HEADS // 2, tokens, PAIR)
    return jax.ShapeDtypeStruct(shape, NARROW), jax.ShapeDtypeStruct(shape, WIDE)


def attention_specs(seqs, context):
    carry = pl.BlockSpec((seqs, 1, HEAD + 8, PAIR), lambda i: (0, i, 0, 0))
    scores = pl.BlockSpec((1, seqs, 2, context, context), lambda i: (i, 0, 0, 0, 0))
    return carry, scores, [whole_spec((3, context, PAIR)), whole_spec((PAIR, PAIR))]


def attention_local(lengths, first, attn_in, weight, bias, tables, mix, wrow):
    seqs, context, tokens = lengths.shape[0], tables.shape[1], attn_in.shape[0]
    pairs = HEADS // 2
    carry, scores, shared = attention_specs(seqs, context)
    narrow, wide = pair_shapes(tokens)
    return pl.pallas_call(
        partial(local_kernel, seqs),
        grid=(pairs,),
        in_specs=[
            SMEM_SPEC,
            SMEM_SPEC,
            whole_spec((tokens, D)),
            pl.BlockSpec((D, 3 * PAIR), lambda i: (0, i)),
            pl.BlockSpec((1, 3 * PAIR), lambda i: (0, i)),
            *shared,
            whole_spec((1, PAIR)),
        ],
        out_specs=[pair_spec(tokens)] * 9 + [scores, carry],
        out_shape=[narrow] * 3
        + [wide] * 6
        + [
            jax.ShapeDtypeStruct((pairs, seqs, 2, context, context), NARROW),
            jax.ShapeDtypeStruct((seqs, pairs, HEAD + 8, PAIR), WIDE),
        ],
        cost_estimate=lasting(14.0),
        name="attention_local",
    )(lengths, first, attn_in, weight, bias, tables, mix, wrow)


def attention_middle(lengths, first, cot, dense_weight, *rest):
    seqs, context, tokens = lengths.shape[0], rest[-2].shape[1], cot.shape[0]
    pairs = HEADS // 2
    carry, scores, shared = attention_specs(seqs, context)
    narrow, wide = pair_shapes(tokens)
    return pl.pallas_call(
        partial(middle_kernel, seqs),
        grid=(pairs,),
        in_specs=[
            SMEM_SPEC,
            SMEM_SPEC,
            whole_spec((tokens, D)),
            pl.BlockSpec((PAIR, D), lambda i: (i, 0)),
        ]
        + [pair_spec(tokens)] * 7
        + [scores, carry, *shared],
        out_specs=[pl.BlockSpec((tokens, PAIR), lambda i: (0, i))]
        + [pair_spec(tokens)] * 3
        + [carry],
        out_shape=[jax.ShapeDtypeStruct((tokens, D), NARROW), narrow, wide, wide]
        + [jax.ShapeDtypeStruct((seqs, pairs, HEAD + 8, PAIR), WIDE)],
        cost_estimate=lasting(20.0),
        name="attention_middle",
    )(lengths, first, cot, dense_weight, *rest)


def attention_last(lengths, first, *rest):
    seqs, context, tokens = lengths.shape[0], rest[-2].shape[1], rest[0].shape[1]
    carry, _, shared = attention_specs(seqs, context)
    return pl.pallas_call(
        partial(last_kernel, seqs),
        grid=(HEADS // 2,),
        in_specs=[SMEM_SPEC, SMEM_SPEC] + [pair_spec(tokens)] * 7 + [carry, *shared],
        out_specs=[pl.BlockSpec((tokens, 3 * PAIR), lambda i: (0, i))] * 2,
        out_shape=[
            jax.ShapeDtypeStruct((tokens, 3 * D), NARROW),
            jax.ShapeDtypeStruct((tokens, 3 * D), WIDE),
        ],
        cost_estimate=lasting(10.0),
        name="attention_last",
    )(lengths, first, *rest)


def shards(
    inputs,
    lengths,
    ln1_gain,
    ln1_bias,
    ln2_gain,
    ln2_bias,
    qkv_weight,
    qkv_bias,
    dense_weight,
    dense_bias,
    up_weight,
    up_bias,
    down_weight,
    down_bias,
    qmc_points,
    qmc_weights,
    cotangent,
):
    seqs, context = inputs.shape[:2]
    tokens = seqs * context
    owners, count, place = lax.axis_size("batch"), lax.axis_size("seq"), lax.axis_index("seq")
    bits = list(range(owners.bit_length() - 2))[::-1]
    across = D // COLUMNS
    hops = max(1, count // 2)

    line = Line()
    me = lax.axis_index("batch").astype(jnp.int32)[None]
    edge = ((place == 0) | (place == count - 1)).astype(jnp.int32)[None]
    if owners == 8 and count == 4:
        reduction = Rounds(line, edge, [2, 2, 2, 2, 1, 1, 1, 1])
    else:
        reduction = Singly(line, bits)

    def group(name, shape, at, left, blocks, right, columns):
        pieces = [
            (*left, block, *right, (row, column))
            for column in range(columns)
            for row, block in enumerate(blocks)
        ]
        size = (len(blocks) * BLOCK_ROWS, columns * COLUMNS // Rounds.PARTS)
        reduction.prepare((name, shape, at, size), pieces)

    BLOCK_ROWS = min(BLOCK, D // owners)
    inputs_flat = inputs.reshape(tokens, D)
    cot = cotangent.reshape(tokens, D)
    cot_in = swap(cot.astype(WIDE), 0)
    row = jnp.concatenate(
        [qkv_bias, up_bias, ln1_gain, ln1_bias, ln2_gain, ln2_bias, dense_bias, down_bias]
    ).astype(WIDE)[None, :]
    attn_in, mlp_in, unit, rate = line.step(
        lambda *a: two_norms(*a, (LN1_GAIN, LN1_BIAS, LN2_GAIN, LN2_BIAS)), inputs_flat, row
    )
    act, slope, act_own, act_send = line.step(mlp_up, mlp_in, up_weight, row, me)
    act_in = swap(act_send, 0)
    norm_own, norm_send = line.step(lambda *a: pick(a[:2], a[2]), attn_in, mlp_in, me)
    subs = act_own.shape[0]

    def down_group(sub):
        shape = (FF // owners, D)
        at = (sub // 2, 0)
        group("down", shape, at, (act_own, act_in), (sub, sub + 1), (cot, cot_in), across)

    down_group(0)
    up_grad, up_send, up_sums, mlp_out, mlp_norm_grad = line.step(
        mlp_back, cot, down_weight, up_weight, act, slope
    )
    for sub in range(2, subs, 2):
        down_group(sub)
    reduction.step()
    up_in = line.send(up_send, lambda a: swap(a, 0))
    norm_in = line.send(norm_send, lambda a: swap(a, 0))

    start, lengths_here = line.wait(place * context, lengths)
    first = jnp.stack([start, jnp.full((), context, jnp.int32)])
    positions = start + jnp.arange(context, dtype=jnp.int32)
    tables, mix, wrow = attention_tables(positions, qmc_points, qmc_weights)
    fq, fk, value, phi_q, phi_k, rot_q, rot_k, num, den, scores, carry = line.step(
        attention_local,
        lengths_here,
        first,
        attn_in,
        qkv_weight,
        row,
        tables,
        mix,
        wrow,
    )
    arrived = shift_rows(carry, "seq", 1)

    def up_group(part):
        shape = (D // owners, FF)
        at = (0, part * Rounds.PARTS)
        columns = FF // COLUMNS // 2
        group("up", shape, at, (norm_own, norm_in), (1,), (up_grad, up_in), columns)

    up_group(0)
    for _ in range(hops - 1):
        passed = line.step(pass_on, carry, arrived, lengths_here, first)
        arrived = shift_rows(passed, "seq", 1)
    reduction.step()
    up_group(1)
    attn_low, grad_q, grad_k, grad_v, carry_back = line.step(
        attention_middle,
        lengths_here,
        first,
        cot,
        dense_weight,
        fq,
        fk,
        value,
        phi_q,
        rot_q,
        num,
        den,
        scores,
        arrived,
        tables,
        mix,
    )
    arrived_back = shift_rows(carry_back, "seq", -1)
    low_own, low_send = line.step(lambda *a: pick(a[:1], a[1]), attn_low, me)
    low_in = swap(low_send, 0)
    reduction.step()
    output = line.step(
        lambda *a: layer_output(*a, (DENSE, DOWN)),
        attn_low,
        dense_weight,
        inputs_flat,
        mlp_out,
        row,
    )
    for _ in range(hops - 1):
        passed = line.step(pass_on, carry_back, arrived_back, lengths_here, first)
        arrived_back = shift_rows(passed, "seq", -1)
    shape = (D // owners, D)
    group("dense", shape, (0, 0), (low_own, low_in), (0,), (cot, cot_in), across)
    qkv_grad, qkv_send = line.step(
        attention_last,
        lengths_here,
        first,
        grad_q,
        grad_k,
        grad_v,
        fk,
        value,
        phi_k,
        rot_k,
        arrived_back,
        tables,
        mix,
    )
    reduction.step()
    qkv_in = line.send(qkv_send, lambda a: swap(a, 0))
    input_grad, sums, qkv_sums = line.step(
        lambda *a: norm_back(*a, (LN1_GAIN, LN2_GAIN)),
        qkv_grad,
        qkv_weight,
        mlp_norm_grad,
        unit,
        rate,
        cot,
        row,
    )

    def qkv_group(part):
        shape = (D // owners, 3 * D)
        at = (0, part * Rounds.PARTS)
        group("qkv", shape, at, (norm_own, norm_in), (0,), (qkv_grad, qkv_in), 2)

    qkv_group(0)
    reduction.step()
    vectors = Vectors(
        line, (sums[0], sums[1], sums[2], sums[3], qkv_sums[0], sums[4], up_sums[0])
    )
    for part in range(1, 3):
        qkv_group(part)
        vectors.take()
        reduction.step()
        vectors.send()
    while not reduction.finished():
        vectors.take()
        reduction.step()
        vectors.send()
    totals = reduction.results()
    (
        attn_gain_total,
        attn_shift_total,
        mlp_gain_total,
        mlp_shift_total,
        qkv_bias_total,
        bias_total,
        up_bias_total,
    ) = vectors.results()

    return (
        output.reshape(inputs.shape),
        input_grad.reshape(inputs.shape),
        attn_gain_total,
        attn_shift_total,
        mlp_gain_total,
        mlp_shift_total,
        totals["qkv"],
        qkv_bias_total,
        totals["dense"],
        bias_total,
        totals["up"],
        up_bias_total,
        totals["down"],
        bias_total,
    )


def solution(mesh):
    placed = (
        P("batch", "seq", None),
        P("batch", None),
        P(),
        P(),
        P(),
        P(),
        P(),
        P(),
        P(),
        P(),
        P(),
        P(),
        P(),
        P(),
        P(),
        P(),
        P("batch", "seq", None),
    )
    return jax.shard_map(
        shards,
        mesh=mesh,
        in_specs=placed,
        out_specs=(
            P("batch", "seq", None),
            P("batch", "seq", None),
            P("batch"),
            P("batch"),
            P("batch"),
            P("batch"),
            P("batch", None),
            P("batch"),
            P("batch", None),
            P("batch"),
            P("batch", None),
            P("batch"),
            P("batch", None),
            P("batch"),
        ),
        check_vma=False,
    )
```

```python
import math
from functools import partial

import jax
import jax.numpy as jnp
import numpy as np
from jax import lax
from jax.experimental import pallas as pl
from jax.experimental.pallas import tpu as pltpu
from jax.sharding import PartitionSpec as P

D = 1024
HEADS = 16
HEAD = 64
ROT = 16
FF = 4096
PAIR = 2 * HEAD
BLOCK = 128
COLUMNS = 512

EPSILON = 1e-05
ROTARY_BASE = 10000.0

def lasting(microseconds):
    return pl.CostEstimate(
        flops=int(microseconds * 1.15e9), transcendentals=0, bytes_accessed=0
    )


ROWS_COLS = ((1,), (0,))
ROWS_ROWS = ((1,), (1,))
COLS_COLS = ((0,), (0,))
NARROW = jnp.bfloat16
WIDE = jnp.float32


def plain_dot(left, right, dims):
    return lax.dot_general(left, right, (dims, ((), ())), preferred_element_type=WIDE)


def whole_spec(shape):
    return pl.BlockSpec(shape, lambda *_: (0,) * len(shape))


def shift_rows(value, axis, by):
    count = lax.axis_size(axis)
    return lax.ppermute(
        value, axis, [(i, i + by) for i in range(count) if 0 <= i + by < count]
    )


def swap(value, bit):
    count = lax.axis_size("batch")
    return lax.ppermute(value, "batch", [(i, i ^ (1 << bit)) for i in range(count)])


def owner_order(bits):
    return sorted(
        range(1 << len(bits)), key=lambda r: tuple(-((r >> bit) & 1) for bit in bits)
    )


def line_rounds(count):
    half = count // 2
    rounds = [("in", [(k, k + 1), (count - 1 - k, count - 2 - k)], k) for k in range(half - 1)]
    rounds.append(("in", [(half - 1, half), (half, half - 1)], -1))
    for k in range(half - 2, -1, -1):
        rounds.append(("out", [(k + 1, k), (count - 2 - k, count - 1 - k)], k))
    return rounds


class Line:
    def __init__(self):
        self.last = None

    def wait(self, *values):
        if self.last is not None:
            values, _ = lax.optimization_barrier((values, self.last))
        return values

    def send(self, value, how):
        return how(*self.wait(value))

    def step(self, function, *values):
        out = function(*self.wait(*values))
        self.last = jax.tree.leaves(out)[0]
        return out


class Vectors:
    def __init__(self, line, vectors):
        owners = lax.axis_size("batch")
        me = lax.axis_index("batch")
        self.line = line
        self.sizes = [v.shape[0] // owners for v in vectors]
        pieces = jnp.concatenate([v.reshape(owners, -1) for v in vectors], axis=1)
        bits = list(range(owners.bit_length() - 1))
        rows = [lax.dynamic_slice_in_dim(pieces, r ^ me, 1, 0) for r in owner_order(bits)]
        self.held = jnp.concatenate(rows)
        count = lax.axis_size("seq")
        self.steps = [("swap", bit, 0) for bit in bits]
        self.steps += line_rounds(count) if count % 2 == 0 else []
        self.moving = None
        self.now = None
        self.send()

    def send(self):
        if self.moving is not None or not self.steps:
            return
        self.now = kind, what, _ = self.steps.pop(0)
        if kind == "swap":
            half = self.held.shape[0] // 2
            self.moving = self.line.send(self.held[:half], lambda a: swap(a, what))
            self.held = self.held[half:]
        else:
            self.moving = self.line.send(self.held, lambda a: lax.ppermute(a, "seq", what))

    def take(self):
        if self.moving is None:
            return
        kind, _, at = self.now
        if kind == "out":
            place, count = lax.axis_index("seq"), lax.axis_size("seq")
            edge = (place == at) | (place == count - 1 - at)
            self.held = self.line.step(
                lambda a, b: jnp.where(edge, b, a), self.held, self.moving
            )
        else:
            self.held = self.line.step(lambda a, b: a + b, self.held, self.moving)
        self.moving = None

    def results(self):
        while self.moving is not None or self.steps:
            self.take()
            self.send()
        if lax.axis_size("seq") % 2 and lax.axis_size("seq") > 1:
            self.held = lax.psum(self.held, "seq")
        out, at = [], 0
        for size in self.sizes:
            out.append(self.held[0, at : at + size])
            at += size
        return out


class Reduction:
    def __init__(self, line, left, right, bits):
        self.line = line
        half = left.shape[1] // 2
        send = line.step(lambda a, b: plain_dot(a, b, COLS_COLS), left[:, :half], right)
        self.held = line.step(lambda a, b: plain_dot(a, b, COLS_COLS), left[:, half:], right)
        count = lax.axis_size("seq")
        self.steps = [("swap", bit + 1, 0) for bit in bits]
        self.steps += line_rounds(count) if count % 2 == 0 else []
        self.moving = swap(send, bits[0] + 1)

    def finish(self):
        place, count = lax.axis_index("seq"), lax.axis_size("seq")
        for i, (kind, _, at) in enumerate(self.steps):
            if kind == "out":
                edge = (place == at) | (place == count - 1 - at)
                self.held = self.line.step(
                    lambda a, b: jnp.where(edge, b, a), self.held, self.moving
                )
            else:
                self.held = self.line.step(lambda a, b: a + b, self.held, self.moving)
            if i + 1 == len(self.steps):
                break
            kind, what, _ = self.steps[i + 1]
            if kind == "swap":
                half = self.held.shape[0] // 2
                self.moving = swap(self.held[:half], what)
                self.held = self.held[half:]
            else:
                self.moving = lax.ppermute(self.held, "seq", what)
        return self.held if count % 2 == 0 or count == 1 else lax.psum(self.held, "seq")


class Singly:
    def __init__(self, line, bits):
        self.line, self.bits = line, bits
        self.pieces, self.outputs = [], {}

    def prepare(self, target, pieces):
        _, _, at, size = target
        for left, left_in, block, right, right_in, (row, column) in pieces:
            wide = COLUMNS // Rounds.PARTS
            across = size[1] // wide
            starts = [((at[1] + i) * across + column) * wide for i in range(Rounds.PARTS)]
            right, right_in = (
                jnp.concatenate([value[:, k : k + wide] for k in starts], axis=1)
                for value in (right, right_in)
            )
            left = jnp.concatenate([left[block], rounded(left_in[block])], axis=0)
            right = jnp.concatenate([right, rounded(right_in)], axis=0)
            done = Reduction(self.line, left, right, self.bits)
            self.pieces.append((target, row, starts, wide, done))

    def step(self):
        pass

    def finished(self):
        return True

    def results(self):
        for (name, shape, at, size), row, starts, wide, piece in self.pieces:
            whole = self.outputs.get(name, jnp.zeros(shape, WIDE))
            total = piece.finish()
            top = at[0] * size[0] + row * total.shape[0]
            for i, k in enumerate(starts):
                whole = lax.dynamic_update_slice(
                    whole, total[:, i * wide : (i + 1) * wide], (top, k)
                )
            self.outputs[name] = whole
        return self.outputs


def rounded(arrived):
    one = jnp.where(lax.axis_index("seq") < lax.axis_size("seq"), 1.0, 0.5)
    return (arrived * one).astype(NARROW)


def product_kernel(count, *refs):
    ins, (to_x, to_y, hold_a, hold_b) = refs[: 8 * count], refs[-4:]
    for p in range(count):
        for i, (to, hold) in enumerate(((to_x, hold_a), (to_y, hold_b))):
            left, left_in, right, right_in = ins[8 * p + 4 * i : 8 * p + 4 * i + 4]
            whole = jnp.concatenate([left[0], left_in[0].astype(NARROW)], axis=0)
            right = jnp.concatenate([right[...], right_in[...].astype(NARROW)], axis=0)

            def product(first, second):
                rows = [whole[:, k * BLOCK : (k + 1) * BLOCK] for k in (first, second)]
                return plain_dot(jnp.concatenate(rows, axis=1), right, COLS_COLS)

            out = pl.ds(p * 2 * BLOCK, 2 * BLOCK)
            to[out, :] = product(0, 1 if i else 2)
            hold[out, :] = product(2 if i else 1, 3)


def round_kernel(counts, places, skip, *refs):
    first, second, inward, middle, outward = counts
    refs = list(refs)
    edge = refs.pop(0)[0] != 0

    def take(flag, count):
        return [refs.pop(0) for _ in range(count)] if flag else [None] * count

    from_x, from_y = take(first or second, 2)
    hold_a, hold_b = take(first, 2)
    kept_a, kept_b = take(second, 2)
    (sums,) = take(inward, 1)
    (from_end,) = take(inward or outward, 1)
    inner, from_middle = take(middle, 2)
    (whole,) = take(outward, 1)
    take(True, skip)
    to_x, to_y, keep_a, keep_b = take(first, 4)
    (new_sums,) = take(second, 1)
    (to_end,) = take(second or middle, 1)
    (new_inner,) = take(inward, 1)
    (new_whole,) = take(middle, 1)
    (final,) = take(outward, 1)
    for p in range(first):
        low = pl.ds(2 * p * BLOCK, BLOCK)
        high = pl.ds((2 * p + 1) * BLOCK, BLOCK)
        out = pl.ds(p * BLOCK, BLOCK)
        to_y[out, :] = hold_a[low, :] + from_x[low, :]
        to_x[out, :] = hold_b[low, :] + from_y[low, :]
        keep_a[out, :] = hold_a[high, :] + from_x[high, :]
        keep_b[out, :] = hold_b[high, :] + from_y[high, :]
    for p in range(max(second, middle)):
        for i, (kept, arrived) in enumerate(((kept_a, from_y), (kept_b, from_x))):
            out = pl.ds((2 * p + i) * BLOCK, BLOCK)
            ends = inners = None
            if p < second:
                come = pl.ds((2 * first + p) * BLOCK, BLOCK)
                ends = kept[pl.ds(p * BLOCK, BLOCK), :] + arrived[come, :]
                new_sums[out, :] = ends
            if p < middle:
                inners = inner[out, :] + from_middle[out, :]
                new_whole[out, :] = inners
            if ends is None:
                to_end[out, :] = inners
            elif inners is None:
                to_end[out, :] = ends
            else:
                to_end[out, :] = jnp.where(edge, ends, inners)
    if inward:
        new_inner[...] = sums[...] + from_end[: 2 * inward * BLOCK, :]
    for k, (row, column) in enumerate(places):
        rows = pl.ds(k * BLOCK, BLOCK)
        wide = whole.shape[1]
        total = jnp.where(edge, from_end[rows, :], whole[rows, :])
        final[row * BLOCK : (row + 1) * BLOCK, column * wide : (column + 1) * wide] = total


class Rounds:
    PARTS = 2

    def __init__(self, line, edge, counts):
        self.line, self.edge, self.counts = line, edge, counts
        self.made = self.at = 0
        self.buffers, self.moving, self.hold, self.kept = {}, {}, {}, {}
        self.sums, self.inner, self.whole, self.targets = {}, {}, {}, []
        self.outputs = {}
        self.end = self.middle = None
        self.wide = COLUMNS // self.PARTS

    def count(self, group):
        return self.counts[group] if 0 <= group < len(self.counts) else 0

    def rows_spec(self, rows, at=0):
        return pl.BlockSpec((rows, self.wide), lambda i: (at, i))

    def prepare(self, target, pieces):
        r = self.made
        self.made += 1
        self.targets.append((target, [piece[5] for piece in pieces]))
        count = len(pieces) // 2
        name, shape, at, size = target
        across = size[1] // self.wide
        args, specs = [], []
        for left, left_in, block, right, right_in, (_, column) in pieces:
            for value in (left, left_in):
                args.append(value)
                specs.append(
                    pl.BlockSpec((1, *value.shape[1:]), lambda i, block=block: (block, 0, 0))
                )
            for value in (right, right_in):
                args.append(value)
                specs.append(
                    pl.BlockSpec(
                        (value.shape[0], self.wide),
                        lambda i, c=column: (0, (at[1] + i) * across + c),
                    )
                )
        rows = 2 * count * BLOCK
        total = rows + self.count(r - 1) * BLOCK
        call = pl.pallas_call(
            partial(product_kernel, count),
            grid=(self.PARTS,),
            in_specs=specs,
            out_specs=[self.rows_spec(rows)] * 4,
            out_shape=[jax.ShapeDtypeStruct((total, COLUMNS), WIDE)] * 2
            + [jax.ShapeDtypeStruct((rows, COLUMNS), WIDE)] * 2,
            cost_estimate=lasting(5.0),
        compiler_params=pltpu.CompilerParams(vmem_limit_bytes=67108864),
        name="piece_products",
        )
        to_x, to_y, hold_a, hold_b = self.line.step(call, *args)
        self.hold[r] = (hold_a, hold_b)
        if r:
            self.buffers[r] = (to_x, to_y)
        else:
            self.moving[r] = (swap(to_x, 1), swap(to_y, 2))

    def step(self):
        r = self.at
        self.at += 1
        counts = [self.count(r - back) for back in (0, 1, 2, 3, 4)]
        first, second, inward, middle, outward = counts
        aliases = {}
        args, specs = [self.edge], [pl.BlockSpec(memory_space=pltpu.SMEM)]

        def add(value):
            args.append(value)
            specs.append(self.rows_spec(value.shape[0]))

        if first or second:
            for value in self.moving.pop(r):
                add(value)
        if first:
            for value in self.hold.pop(r):
                add(value)
        if second:
            for value in self.kept.pop(r - 1):
                add(value)
        if inward:
            add(self.sums.pop(r - 2))
        if inward or outward:
            add(self.end)
        if middle:
            add(self.inner.pop(r - 3))
            add(self.middle)
        if outward:
            add(self.whole.pop(r - 4))
        outs, out_specs = [], []

        def out(rows, at=0, of=None):
            outs.append(jax.ShapeDtypeStruct((of or rows, COLUMNS), WIDE))
            out_specs.append(self.rows_spec(rows, at))

        ahead = self.count(r + 1)
        if ahead:
            aliases = {len(args): 0, len(args) + 1: 1}
            args += list(self.buffers.pop(r + 1))
            specs += [pl.BlockSpec(memory_space=pl.ANY)] * 2
        if first:
            for _ in range(2):
                out(first * BLOCK, 2 * ahead // first, (2 * ahead + first) * BLOCK)
            out(first * BLOCK)
            out(first * BLOCK)
        if second:
            out(2 * second * BLOCK)
        if second or middle:
            out(2 * max(second, middle) * BLOCK)
        for count in (inward, middle):
            if count:
                out(2 * count * BLOCK)
        places = ()
        if outward:
            (name, shape, at, size), places = self.targets[r - 4]
            if name in self.outputs:
                aliases[len(args)] = len(outs)
                args.append(self.outputs[name])
                specs.append(pl.BlockSpec(memory_space=pl.ANY))
            outs.append(jax.ShapeDtypeStruct(shape, WIDE))
            out_specs.append(pl.BlockSpec(size, lambda i: (at[0], at[1] + i)))
        call = pl.pallas_call(
            partial(round_kernel, counts, places, len(aliases)),
            grid=(self.PARTS,),
            in_specs=specs,
            out_specs=out_specs,
            out_shape=outs,
            input_output_aliases=aliases,
            cost_estimate=lasting(5.0),
            compiler_params=pltpu.CompilerParams(vmem_limit_bytes=67108864),
            name="reduce_round",
        )
        got = list(self.line.step(call, *args))
        if first:
            self.moving[r + 1] = (swap(got.pop(0), 1), swap(got.pop(0), 2))
            self.kept[r] = (got.pop(0), got.pop(0))
        if second:
            self.sums[r - 1] = got.pop(0)
        if second or middle:
            self.end = lax.ppermute(got.pop(0), "seq", [(0, 1), (1, 0), (2, 3), (3, 2)])
        if inward:
            self.inner[r - 2] = got.pop(0)
            self.middle = lax.ppermute(self.inner[r - 2], "seq", [(1, 2), (2, 1)])
        if middle:
            self.whole[r - 3] = got.pop(0)
        if outward:
            self.outputs[name] = got.pop(0)

    def finished(self):
        return self.at == len(self.counts) + 4

    def results(self):
        return self.outputs


def pick_kernel(me_ref, *refs):
    ins, (keep_ref, send_ref) = refs[:-2], refs[-2:]
    half = keep_ref.shape[2] // BLOCK
    for i, ref in enumerate(ins):
        for p in range(half):
            for core in range(2):
                owner = (2 * (half - 1 - p) + core) ^ me_ref[0]
                columns = ref[:, pl.ds(pl.multiple_of(owner * BLOCK, BLOCK), BLOCK)]
                at = slice(p * BLOCK, (p + 1) * BLOCK)
                if core:
                    send_ref[i, :, at] = columns.astype(WIDE)
                else:
                    keep_ref[i, :, at] = columns


def pick(arrays, me):
    owners = lax.axis_size("batch")
    half = owners // 2
    tokens, features = arrays[0].shape
    size = features // owners
    if size != BLOCK:

        def columns(value, core):
            return jnp.concatenate(
                [
                    lax.dynamic_slice_in_dim(value, ((2 * r + core) ^ me[0]) * size, size, 1)
                    for r in range(half)[::-1]
                ],
                axis=1,
            )

        return (
            jnp.stack([columns(a, 0) for a in arrays]),
            jnp.stack([columns(a, 1) for a in arrays]).astype(WIDE),
        )
    shape = (len(arrays), tokens, half * size)
    return pl.pallas_call(
        pick_kernel,
        in_specs=[pl.BlockSpec(memory_space=pltpu.SMEM)]
        + [pl.BlockSpec(memory_space=pltpu.VMEM)] * len(arrays),
        out_specs=[pl.BlockSpec(memory_space=pltpu.VMEM)] * 2,
        out_shape=[jax.ShapeDtypeStruct(shape, NARROW), jax.ShapeDtypeStruct(shape, WIDE)],
        cost_estimate=lasting(2.0),
        name="pick_columns",
    )(me, *arrays)


def as_row(ref):
    return ref[...].astype(WIDE)[None, :]


def norm_kernel(x_ref, gain1, bias1, gain2, bias2, attn_ref, mlp_ref, unit_ref, rate_ref):
    x = x_ref[...].astype(WIDE)
    centered = x - jnp.mean(x, axis=-1, keepdims=True)
    rate = lax.rsqrt(jnp.mean(centered * centered, axis=-1, keepdims=True) + EPSILON)
    unit = centered * rate
    unit_ref[...] = unit
    rate_ref[...] = jnp.broadcast_to(rate, rate_ref.shape)
    for gain, bias, out in ((gain1, bias1, attn_ref), (gain2, bias2, mlp_ref)):
        out[...] = (unit * as_row(gain) + as_row(bias)).astype(NARROW)


def two_norms(inputs, *gains):
    tokens = inputs.shape[0]
    rows = tokens // 4
    by_rows = pl.BlockSpec((rows, D), lambda i: (i, 0))
    return pl.pallas_call(
        norm_kernel,
        grid=(4,),
        in_specs=[by_rows] + [whole_spec((D,))] * len(gains),
        out_specs=[by_rows, by_rows, by_rows, pl.BlockSpec((rows, 128), lambda i: (i, 0))],
        out_shape=[
            jax.ShapeDtypeStruct((tokens, D), NARROW),
            jax.ShapeDtypeStruct((tokens, D), NARROW),
            jax.ShapeDtypeStruct((tokens, D), WIDE),
            jax.ShapeDtypeStruct((tokens, 128), WIDE),
        ],
        cost_estimate=lasting(4.0),
        name="two_norms",
    )(inputs, *gains)


def up_kernel(
    half, me_ref, x_ref, weight_ref, bias_ref, act_ref, slope_ref, keep_ref, send_ref
):
    step = pl.program_id(0)
    up = plain_dot(x_ref[...], weight_ref[...], ROWS_COLS) + as_row(bias_ref)
    below = 0.5 * (1.0 + lax.erf(up * (0.5**0.5)))
    act = (up * below).astype(NARROW)
    act_ref[...] = act
    slope_ref[...] = below + up * jnp.exp(-0.5 * up * up) * ((2.0 * math.pi) ** -0.5)

    @pl.when(step < half)
    def _():
        for i in range(keep_ref.shape[0]):
            keep_ref[i] = act[:, i * BLOCK : (i + 1) * BLOCK]

    @pl.when(step >= half)
    def _():
        wide = act.astype(WIDE)
        for i in range(send_ref.shape[0]):
            send_ref[i] = wide[:, i * BLOCK : (i + 1) * BLOCK]


def mlp_up(mlp_in, up_weight, up_bias, me):
    owners = lax.axis_size("batch")
    tokens = mlp_in.shape[0]
    half = owners // 2
    each = FF // owners
    subs = each // BLOCK

    def natural(i, me):
        return (0, (2 * (i % half) + i // half) ^ me[0])

    return pl.pallas_call(
        partial(up_kernel, half),
        grid_spec=pltpu.PrefetchScalarGridSpec(
            num_scalar_prefetch=1,
            grid=(owners,),
            in_specs=[
                pl.BlockSpec((tokens, D), lambda i, me: (0, 0)),
                pl.BlockSpec((D, each), natural),
                pl.BlockSpec((each,), lambda i, me: natural(i, me)[1:]),
            ],
            out_specs=[
                pl.BlockSpec((tokens, each), natural),
                pl.BlockSpec((tokens, each), natural),
                pl.BlockSpec(
                    (subs, tokens, BLOCK),
                    lambda i, me: (0, 0, half - 1 - jnp.minimum(i, half - 1)),
                ),
                pl.BlockSpec(
                    (subs, tokens, BLOCK),
                    lambda i, me: (0, 0, half - 1 - jnp.maximum(i - half, 0)),
                ),
            ],
        ),
        out_shape=[
            jax.ShapeDtypeStruct((tokens, FF), NARROW),
            jax.ShapeDtypeStruct((tokens, FF), WIDE),
            jax.ShapeDtypeStruct((subs, tokens, half * BLOCK), NARROW),
            jax.ShapeDtypeStruct((subs, tokens, half * BLOCK), WIDE),
        ],
        cost_estimate=lasting(11.0),
        name="mlp_up",
    )(me, mlp_in, up_weight, up_bias)


def back_kernel(
    cot_ref, down_ref, up_ref, act_ref, slope_ref, grad_ref, send_ref, sums_ref, out_ref, norm_ref
):
    step = pl.program_id(0)
    down = down_ref[...]
    grad = plain_dot(cot_ref[...], down, ROWS_ROWS) * slope_ref[...]
    grad = grad.astype(NARROW)
    grad_ref[...] = grad
    wide = grad.astype(WIDE)
    send_ref[...] = wide
    sums_ref[...] = jnp.sum(wide, axis=0, keepdims=True)
    out = plain_dot(act_ref[...], down, ROWS_COLS)
    norm = plain_dot(grad, up_ref[...], ROWS_ROWS)

    @pl.when(step == 0)
    def _():
        out_ref[...] = out
        norm_ref[...] = norm

    @pl.when(step > 0)
    def _():
        out_ref[...] += out
        norm_ref[...] += norm


def mlp_back(cot, down_weight, up_weight, act, slope):
    tokens = cot.shape[0]
    each = 1024
    by_column = pl.BlockSpec((tokens, each), lambda i: (0, i))
    total = whole_spec((tokens, D))
    return pl.pallas_call(
        back_kernel,
        grid=(FF // each,),
        in_specs=[
            total,
            pl.BlockSpec((each, D), lambda i: (i, 0)),
            pl.BlockSpec((D, each), lambda i: (0, i)),
            by_column,
            by_column,
        ],
        out_specs=[
            by_column,
            by_column,
            pl.BlockSpec((1, each), lambda i: (0, i)),
            total,
            total,
        ],
        out_shape=[
            jax.ShapeDtypeStruct((tokens, FF), NARROW),
            jax.ShapeDtypeStruct((tokens, FF), WIDE),
            jax.ShapeDtypeStruct((1, FF), WIDE),
            jax.ShapeDtypeStruct((tokens, D), WIDE),
            jax.ShapeDtypeStruct((tokens, D), WIDE),
        ],
        cost_estimate=lasting(16.0),
        compiler_params=pltpu.CompilerParams(vmem_limit_bytes=67108864),
        name="mlp_back",
    )(cot, down_weight, up_weight, act, slope)


def output_kernel(low_ref, weight_ref, x_ref, mlp_ref, dense_ref, down_ref, out_ref):
    attn = plain_dot(low_ref[...], weight_ref[...], ROWS_COLS) + as_row(dense_ref)
    mlp = mlp_ref[...] + as_row(down_ref)
    out_ref[...] = (x_ref[...].astype(WIDE) + attn + mlp).astype(NARROW)


def layer_output(low, dense_weight, inputs, mlp_out, *biases):
    tokens = inputs.shape[0]
    each = 512
    by_column = pl.BlockSpec((tokens, each), lambda i: (0, i))
    return pl.pallas_call(
        output_kernel,
        grid=(D // each,),
        in_specs=[
            whole_spec((tokens, D)),
            pl.BlockSpec((D, each), lambda i: (0, i)),
            by_column,
            by_column,
        ]
        + [pl.BlockSpec((each,), lambda i: (i,))] * len(biases),
        out_specs=by_column,
        out_shape=jax.ShapeDtypeStruct((tokens, D), NARROW),
        cost_estimate=lasting(3.0),
        name="layer_output",
    )(low, dense_weight, inputs, mlp_out, *biases)


def norm_back_kernel(
    qkv_ref,
    weight_ref,
    mlp_ref,
    unit_ref,
    rate_ref,
    cot_ref,
    gain1,
    gain2,
    grad_ref,
    sums_ref,
    qkv_sums,
):
    step = pl.program_id(0)
    qkv = qkv_ref[...]
    qkv_sums[...] = jnp.sum(qkv.astype(WIDE), axis=0, keepdims=True)
    part = plain_dot(qkv, weight_ref[...], ROWS_ROWS)

    @pl.when(step == 0)
    def _():
        grad_ref[...] = part

    @pl.when(step > 0)
    def _():
        grad_ref[...] += part

    @pl.when(step == pl.num_programs(0) - 1)
    def _():
        size = 64
        gain_attn, gain_mlp = as_row(gain1), as_row(gain2)
        totals = [jnp.zeros((1, D), WIDE)] * 5
        for k in range(grad_ref.shape[0] // size):
            rows = pl.ds(k * size, size)
            attn, mlp, unit = grad_ref[rows, :], mlp_ref[rows, :], unit_ref[rows, :]
            cot = cot_ref[rows, :].astype(WIDE)
            together = attn * gain_attn + mlp * gain_mlp
            grad_ref[rows, :] = cot + rate_ref[rows, 0:1] * (
                together
                - jnp.mean(together, axis=-1, keepdims=True)
                - unit * jnp.mean(together * unit, axis=-1, keepdims=True)
            )
            for i, value in enumerate((attn * unit, attn, mlp * unit, mlp, cot)):
                totals[i] = totals[i] + jnp.sum(value, axis=0, keepdims=True)
        for i, value in enumerate(totals):
            sums_ref[i : i + 1, :] = value
        sums_ref[5:8, :] = jnp.zeros((3, D), WIDE)


def norm_back(qkv_grad, qkv_weight, mlp_norm_grad, unit, rate, cot, *gains):
    tokens = cot.shape[0]
    each = 512
    total = whole_spec((tokens, D))
    return pl.pallas_call(
        norm_back_kernel,
        grid=(3 * D // each,),
        in_specs=[
            pl.BlockSpec((tokens, each), lambda i: (0, i)),
            pl.BlockSpec((D, each), lambda i: (0, i)),
            total,
            total,
            whole_spec(rate.shape),
            total,
        ]
        + [whole_spec((D,))] * len(gains),
        out_specs=[total, whole_spec((8, D)), pl.BlockSpec((1, each), lambda i: (0, i))],
        out_shape=[
            jax.ShapeDtypeStruct((tokens, D), WIDE),
            jax.ShapeDtypeStruct((8, D), WIDE),
            jax.ShapeDtypeStruct((1, 3 * D), WIDE),
        ],
        cost_estimate=lasting(9.0),
        compiler_params=pltpu.CompilerParams(vmem_limit_bytes=67108864),
        name="norm_back",
    )(qkv_grad, qkv_weight, mlp_norm_grad, unit, rate, cot, *gains)


def dct_matrix():
    rows = np.arange(HEAD)[:, None]
    columns = np.arange(HEAD)[None, :]
    cosines = np.cos(np.pi * (columns + 0.5) * rows / HEAD) * np.sqrt(2.0 / HEAD)
    return np.where(rows == 0, cosines * np.sqrt(0.5), cosines).astype(np.float32)


def attention_tables(positions, points, weights):
    half_rot = ROT // 2
    lane = jnp.arange(PAIR) % HEAD
    freq = ROTARY_BASE ** (-2.0 * (lane % half_rot).astype(WIDE) / ROT)
    angles = positions.astype(WIDE)[:, None] * freq[None, :]
    sin = jnp.sin(angles)
    tables = jnp.stack(
        [
            jnp.where(lane < ROT, jnp.cos(angles), 1.0),
            jnp.where(lane < half_rot, -sin, 0.0),
            jnp.where((lane >= half_rot) & (lane < ROT), sin, 0.0),
        ]
    )
    mix = HEAD ** (-0.25) * jnp.einsum(
        "kn,km->nm", dct_matrix(), points, precision=lax.Precision.HIGHEST
    )
    side = jnp.arange(PAIR) // HEAD
    mix = jnp.where(side[:, None] == side[None, :], jnp.tile(mix, (2, 2)), 0.0)
    return tables, mix, jnp.tile(weights, 2)[None, :]


def lane_is_low(shape):
    return lax.broadcasted_iota(jnp.int32, shape, len(shape) - 1) % PAIR < HEAD


def halves(full):
    return jnp.where(lane_is_low((HEAD, PAIR)), full[:HEAD], full[HEAD:])


def spread_pair(block):
    low = lane_is_low(block.shape)
    zero = jnp.zeros_like(block)
    return jnp.concatenate([jnp.where(low, block, zero), jnp.where(low, zero, block)], axis=0)


def one_head(tile, head):
    low = lane_is_low(tile.shape)
    zero = jnp.zeros_like(tile)
    return jnp.where(low, tile, zero) if head == 0 else jnp.where(low, zero, tile)


def in_two(value):
    high = value.astype(NARROW)
    return high, (value - high.astype(WIDE)).astype(NARROW)


def fine_dot(left, right, dims):
    left_high, left_low = in_two(left)
    right_high, right_low = in_two(right)
    return (
        plain_dot(left_high, right_high, dims)
        + plain_dot(left_low, right_high, dims)
        + plain_dot(left_high, right_low, dims)
    )


def head_sums(tile):
    rows = lax.broadcasted_iota(jnp.int32, (PAIR, PAIR), 0) // HEAD
    columns = lax.broadcasted_iota(jnp.int32, (PAIR, PAIR), 1) // HEAD
    ones = (rows == columns).astype(WIDE).astype(NARROW)
    high, low = in_two(tile)
    return plain_dot(
        jnp.concatenate([high, low], axis=1), jnp.concatenate([ones, ones], axis=0), ROWS_COLS
    )


def turn(tile, cos, sin_up, sin_down):
    half_rot = ROT // 2
    return (
        tile * cos
        + pltpu.roll(tile, PAIR - half_rot, 1) * sin_up
        + pltpu.roll(tile, half_rot, 1) * sin_down
    )


def turn_back(tile, cos, sin_up, sin_down):
    half_rot = ROT // 2
    return (
        tile * cos
        + pltpu.roll(tile * sin_up, half_rot, 1)
        + pltpu.roll(tile * sin_down, PAIR - half_rot, 1)
    )


def all_rows(tables_ref, seqs):
    return [jnp.concatenate([tables_ref[k]] * seqs, axis=0) for k in range(3)]


def feature_grad(grad, phi, turned, mix, tables):
    weighted = grad * phi
    back = fine_dot(weighted, mix, ROWS_ROWS) - (HEAD**-0.5) * turned * head_sums(weighted)
    return turn_back(back, *tables)


def doc_at(where, lengths_ref, b):
    start, found = 0, jnp.zeros_like(where) - 1
    for k in range(lengths_ref.shape[1]):
        found = found + jnp.where(start <= where, 1, 0)
        start = start + lengths_ref[b, k]
    return found


def same_doc_before(lengths_ref, b, first, context):
    query = first + lax.broadcasted_iota(jnp.int32, (context, context), 0)
    key = first + lax.broadcasted_iota(jnp.int32, (context, context), 1)
    same = doc_at(query, lengths_ref, b) == doc_at(key, lengths_ref, b)
    return jnp.where(same & (key <= query), 1.0, 0.0)


def in_doc_of(lengths_ref, b, first, context, where):
    rows = first + lax.broadcasted_iota(jnp.int32, (context, PAIR), 0)
    return jnp.where(doc_at(rows, lengths_ref, b) == doc_at(where, lengths_ref, b), 1.0, 0.0)


def local_kernel(
    seqs,
    lengths_ref,
    first_ref,
    attn_ref,
    weight_ref,
    bias_ref,
    tables_ref,
    mix_ref,
    wrow_ref,
    fq_ref,
    fk_ref,
    val_ref,
    phiq_ref,
    phik_ref,
    rotq_ref,
    rotk_ref,
    num_ref,
    den_ref,
    score_ref,
    carry_ref,
):
    context = tables_ref.shape[1]
    first = first_ref[0]
    mix, wrow = mix_ref[...], wrow_ref[...]
    tables = all_rows(tables_ref, seqs)
    low = lane_is_low((seqs * context, PAIR))
    block = plain_dot(attn_ref[...], weight_ref[...], ROWS_COLS) + bias_ref[...]
    one, two, three = block[:, :PAIR], block[:, PAIR : 2 * PAIR], block[:, 2 * PAIR :]
    query = jnp.where(low, one, two)
    key = pltpu.roll(jnp.where(low, three, one), HEAD, 1)
    value_all = jnp.where(low, two, three).astype(NARROW)
    val_ref[...] = value_all

    def features(raw):
        turned = turn(raw, *tables)
        power = fine_dot(turned, mix, ROWS_COLS) - (0.5 * HEAD**-0.5) * head_sums(turned * turned)
        return turned, wrow * jnp.exp(power)

    turned_q, phi_q = features(query)
    turned_k, phi_k = features(key)
    rotq_ref[...], rotk_ref[...] = turned_q, turned_k
    phiq_ref[...], phik_ref[...] = phi_q, phi_k
    fq_all, fk_all = phi_q.astype(NARROW), phi_k.astype(NARROW)
    fq_ref[...], fk_ref[...] = fq_all, fk_all
    low = lane_is_low((context, PAIR))
    for b in range(seqs):
        rows = slice(b * context, (b + 1) * context)
        fq, fk, value = fq_all[rows], fk_all[rows], value_all[rows]
        mask = same_doc_before(lengths_ref, b, first, context)
        keep = in_doc_of(lengths_ref, b, first, context, first + context - 1)
        wide_value = jnp.concatenate([value, jnp.ones_like(value)], axis=1)
        sums = []
        for h in range(2):
            scores = (plain_dot(one_head(fq, h), fk, ROWS_ROWS) * mask).astype(NARROW)
            score_ref[0, b, h] = scores
            sums.append(plain_dot(scores, wide_value, ROWS_COLS))
        num_ref[rows, :] = jnp.where(low, sums[0][:, :PAIR], sums[1][:, :PAIR])
        den_ref[rows, :] = jnp.where(low, sums[0][:, PAIR:], sums[1][:, PAIR:])
        kept = fk * keep.astype(NARROW)
        carry_ref[b, 0, :HEAD, :] = halves(plain_dot(kept, value, COLS_COLS))
        norm = jnp.sum(kept.astype(WIDE), axis=0, keepdims=True)
        carry_ref[b, 0, HEAD:, :] = jnp.broadcast_to(norm, (8, PAIR))


def middle_kernel(
    seqs,
    lengths_ref,
    first_ref,
    cot_ref,
    dense_ref,
    fq_ref,
    fk_ref,
    val_ref,
    phiq_ref,
    rotq_ref,
    num_ref,
    den_ref,
    score_ref,
    carry_ref,
    tables_ref,
    mix_ref,
    low_ref,
    gradq_ref,
    gradk_ref,
    gradv_ref,
    out_ref,
):
    context = tables_ref.shape[1]
    first = first_ref[0]
    mix = mix_ref[...]
    tables = all_rows(tables_ref, seqs)
    low = lane_is_low((context, PAIR))
    back_all = plain_dot(cot_ref[...], dense_ref[...], ROWS_ROWS)
    grads_q = []
    for b in range(seqs):
        rows = pl.ds(b * context, context)
        fq, fk, value = fq_ref[rows, :], fk_ref[rows, :], val_ref[rows, :]
        use = in_doc_of(lengths_ref, b, first, context, first - 1)
        state = spread_pair(carry_ref[b, 0, :HEAD, :].astype(NARROW))
        norm = carry_ref[b, 0, HEAD : HEAD + 1, :]
        wide_fq = fq.astype(WIDE)
        num = num_ref[rows, :] + use * plain_dot(fq, state, ROWS_COLS)
        den = den_ref[rows, :] + use * head_sums(wide_fq * norm)
        heads_out = num / den
        low_ref[rows, :] = heads_out.astype(NARROW)
        back = back_all[b * context : (b + 1) * context]
        num_grad = (back / den).astype(NARROW)
        den_grad = -head_sums(back * heads_out) / den
        mask = same_doc_before(lengths_ref, b, first, context)
        parts_q, parts_k, parts_v = [], [], []
        for h in range(2):
            column = den_grad[:, h * HEAD : h * HEAD + 1]
            score_grad = plain_dot(one_head(num_grad, h), value, ROWS_ROWS) + column
            score_grad = (score_grad * mask).astype(NARROW)
            parts_q.append(plain_dot(score_grad, fk, ROWS_COLS))
            parts_k.append(plain_dot(score_grad, fq, COLS_COLS))
            parts_v.append(plain_dot(score_ref[0, b, h], num_grad, COLS_COLS))
        gradk_ref[rows, :] = jnp.where(low, parts_k[0], parts_k[1])
        gradv_ref[rows, :] = jnp.where(low, parts_v[0], parts_v[1])
        num_used = num_grad * use.astype(NARROW)
        den_used = den_grad * use
        grads_q.append(
            jnp.where(low, parts_q[0], parts_q[1])
            + plain_dot(num_used, state, ROWS_ROWS)
            + den_used * norm
        )
        out_ref[b, 0, :HEAD, :] = halves(plain_dot(fq, num_used, COLS_COLS))
        norm_grad = jnp.sum(den_used * wide_fq, axis=0, keepdims=True)
        out_ref[b, 0, HEAD:, :] = jnp.broadcast_to(norm_grad, (8, PAIR))
    gradq_ref[...] = feature_grad(
        jnp.concatenate(grads_q, axis=0), phiq_ref[...], rotq_ref[...], mix, tables
    ).astype(NARROW)


def last_kernel(
    seqs,
    lengths_ref,
    first_ref,
    gradq_ref,
    gradk_ref,
    gradv_ref,
    fk_ref,
    val_ref,
    phik_ref,
    rotk_ref,
    carry_ref,
    tables_ref,
    mix_ref,
    out_ref,
    send_ref,
):
    context = tables_ref.shape[1]
    first = first_ref[0]
    tables = all_rows(tables_ref, seqs)
    grads_k, grads_v = [], []
    for b in range(seqs):
        rows = pl.ds(b * context, context)
        keep = in_doc_of(lengths_ref, b, first, context, first + context - 1)
        state = spread_pair(carry_ref[b, 0, :HEAD, :].astype(NARROW))
        norm = carry_ref[b, 0, HEAD : HEAD + 1, :]
        grads_k.append(
            gradk_ref[rows, :] + keep * (plain_dot(val_ref[rows, :], state, ROWS_ROWS) + norm)
        )
        grads_v.append(gradv_ref[rows, :] + keep * plain_dot(fk_ref[rows, :], state, ROWS_COLS))
    grad_k = feature_grad(
        jnp.concatenate(grads_k, axis=0), phik_ref[...], rotk_ref[...], mix_ref[...], tables
    )
    grad_k = pltpu.roll(grad_k, HEAD, 1)
    grad_v = jnp.concatenate(grads_v, axis=0)
    grad_q = gradq_ref[...].astype(WIDE)
    low = lane_is_low(grad_q.shape)
    grad = jnp.concatenate(
        [
            jnp.where(low, grad_q, grad_k),
            jnp.where(low, grad_v, grad_q),
            jnp.where(low, grad_k, grad_v),
        ],
        axis=1,
    ).astype(NARROW)
    out_ref[...] = grad
    send_ref[...] = grad.astype(WIDE)


def pass_kernel(lengths_ref, first_ref, own_ref, arrived_ref, out_ref):
    context = first_ref[1]
    for b in range(own_ref.shape[0]):
        last = doc_at(first_ref[0] + context - 1, lengths_ref, b)
        through = last == doc_at(first_ref[0] - 1, lengths_ref, b)
        out_ref[b] = own_ref[b] + jnp.where(through, arrived_ref[b], 0.0)


SMEM_SPEC = pl.BlockSpec(memory_space=pltpu.SMEM)


def pass_on(own, arrived, lengths, first):
    seqs, pairs = own.shape[:2]
    spec = pl.BlockSpec((seqs, pairs // 2, *own.shape[2:]), lambda i: (0, i, 0, 0))
    return pl.pallas_call(
        pass_kernel,
        grid=(2,),
        in_specs=[SMEM_SPEC, SMEM_SPEC, spec, spec],
        out_specs=spec,
        out_shape=jax.ShapeDtypeStruct(own.shape, WIDE),
        cost_estimate=lasting(2.0),
        name="pass_carry",
    )(lengths, first, own, arrived)


def pair_spec(rows):
    return pl.BlockSpec((None, rows, PAIR), lambda i: (i, 0, 0))


def pair_shapes(tokens):
    shape = (HEADS // 2, tokens, PAIR)
    return jax.ShapeDtypeStruct(shape, NARROW), jax.ShapeDtypeStruct(shape, WIDE)


def attention_specs(seqs, context):
    carry = pl.BlockSpec((seqs, 1, HEAD + 8, PAIR), lambda i: (0, i, 0, 0))
    scores = pl.BlockSpec((1, seqs, 2, context, context), lambda i: (i, 0, 0, 0, 0))
    return carry, scores, [whole_spec((3, context, PAIR)), whole_spec((PAIR, PAIR))]


def attention_local(lengths, first, attn_in, weight, bias, tables, mix, wrow):
    seqs, context, tokens = lengths.shape[0], tables.shape[1], attn_in.shape[0]
    pairs = HEADS // 2
    carry, scores, shared = attention_specs(seqs, context)
    narrow, wide = pair_shapes(tokens)
    return pl.pallas_call(
        partial(local_kernel, seqs),
        grid=(pairs,),
        in_specs=[
            SMEM_SPEC,
            SMEM_SPEC,
            whole_spec((tokens, D)),
            pl.BlockSpec((D, 3 * PAIR), lambda i: (0, i)),
            pl.BlockSpec((1, 3 * PAIR), lambda i: (0, i)),
            *shared,
            whole_spec((1, PAIR)),
        ],
        out_specs=[pair_spec(tokens)] * 9 + [scores, carry],
        out_shape=[narrow] * 3
        + [wide] * 6
        + [
            jax.ShapeDtypeStruct((pairs, seqs, 2, context, context), NARROW),
            jax.ShapeDtypeStruct((seqs, pairs, HEAD + 8, PAIR), WIDE),
        ],
        cost_estimate=lasting(14.0),
        compiler_params=pltpu.CompilerParams(vmem_limit_bytes=67108864),
        name="attention_local",
    )(lengths, first, attn_in, weight, bias, tables, mix, wrow)


def attention_middle(lengths, first, cot, dense_weight, *rest):
    seqs, context, tokens = lengths.shape[0], rest[-2].shape[1], cot.shape[0]
    pairs = HEADS // 2
    carry, scores, shared = attention_specs(seqs, context)
    narrow, wide = pair_shapes(tokens)
    return pl.pallas_call(
        partial(middle_kernel, seqs),
        grid=(pairs,),
        in_specs=[
            SMEM_SPEC,
            SMEM_SPEC,
            whole_spec((tokens, D)),
            pl.BlockSpec((PAIR, D), lambda i: (i, 0)),
        ]
        + [pair_spec(tokens)] * 7
        + [scores, carry, *shared],
        out_specs=[pl.BlockSpec((tokens, PAIR), lambda i: (0, i))]
        + [pair_spec(tokens)] * 3
        + [carry],
        out_shape=[jax.ShapeDtypeStruct((tokens, D), NARROW), narrow, wide, wide]
        + [jax.ShapeDtypeStruct((seqs, pairs, HEAD + 8, PAIR), WIDE)],
        cost_estimate=lasting(20.0),
        compiler_params=pltpu.CompilerParams(vmem_limit_bytes=67108864),
        name="attention_middle",
    )(lengths, first, cot, dense_weight, *rest)


def attention_last(lengths, first, *rest):
    seqs, context, tokens = lengths.shape[0], rest[-2].shape[1], rest[0].shape[1]
    carry, _, shared = attention_specs(seqs, context)
    return pl.pallas_call(
        partial(last_kernel, seqs),
        grid=(HEADS // 2,),
        in_specs=[SMEM_SPEC, SMEM_SPEC] + [pair_spec(tokens)] * 7 + [carry, *shared],
        out_specs=[pl.BlockSpec((tokens, 3 * PAIR), lambda i: (0, i))] * 2,
        out_shape=[
            jax.ShapeDtypeStruct((tokens, 3 * D), NARROW),
            jax.ShapeDtypeStruct((tokens, 3 * D), WIDE),
        ],
        cost_estimate=lasting(10.0),
        compiler_params=pltpu.CompilerParams(vmem_limit_bytes=67108864),
        name="attention_last",
    )(lengths, first, *rest)


def shards(
    inputs,
    lengths,
    ln1_gain,
    ln1_bias,
    ln2_gain,
    ln2_bias,
    qkv_weight,
    qkv_bias,
    dense_weight,
    dense_bias,
    up_weight,
    up_bias,
    down_weight,
    down_bias,
    qmc_points,
    qmc_weights,
    cotangent,
):
    seqs, context = inputs.shape[:2]
    tokens = seqs * context
    owners, count, place = lax.axis_size("batch"), lax.axis_size("seq"), lax.axis_index("seq")
    bits = list(range(owners.bit_length() - 2))[::-1]
    across = D // COLUMNS
    hops = max(1, count // 2)

    line = Line()
    me = lax.axis_index("batch").astype(jnp.int32)[None]
    edge = ((place == 0) | (place == count - 1)).astype(jnp.int32)[None]
    if owners == 8 and count == 4:
        reduction = Rounds(line, edge, [2, 2, 2, 2, 1, 1, 1, 1])
    else:
        reduction = Singly(line, bits)

    def group(name, shape, at, left, blocks, right, columns):
        pieces = [
            (*left, block, *right, (row, column))
            for column in range(columns)
            for row, block in enumerate(blocks)
        ]
        size = (len(blocks) * BLOCK_ROWS, columns * COLUMNS // Rounds.PARTS)
        reduction.prepare((name, shape, at, size), pieces)

    BLOCK_ROWS = min(BLOCK, D // owners)
    inputs_flat = inputs.reshape(tokens, D)
    cot = cotangent.reshape(tokens, D)
    cot_in = swap(cot.astype(WIDE), 0)
    attn_in, mlp_in, unit, rate = line.step(
        two_norms, inputs_flat, ln1_gain, ln1_bias, ln2_gain, ln2_bias
    )
    act, slope, act_own, act_send = line.step(mlp_up, mlp_in, up_weight, up_bias, me)
    act_in = swap(act_send, 0)
    norm_own, norm_send = line.step(lambda *a: pick(a[:2], a[2]), attn_in, mlp_in, me)
    subs = act_own.shape[0]

    def down_group(sub):
        shape = (FF // owners, D)
        at = (sub // 2, 0)
        group("down", shape, at, (act_own, act_in), (sub, sub + 1), (cot, cot_in), across)

    down_group(0)
    up_grad, up_send, up_sums, mlp_out, mlp_norm_grad = line.step(
        mlp_back, cot, down_weight, up_weight, act, slope
    )
    for sub in range(2, subs, 2):
        down_group(sub)
    reduction.step()
    up_in = line.send(up_send, lambda a: swap(a, 0))
    norm_in = line.send(norm_send, lambda a: swap(a, 0))

    start, lengths_here = line.wait(place * context, lengths)
    first = jnp.stack([start, jnp.full((), context, jnp.int32)])
    positions = start + jnp.arange(context, dtype=jnp.int32)
    tables, mix, wrow = attention_tables(positions, qmc_points, qmc_weights)
    fq, fk, value, phi_q, phi_k, rot_q, rot_k, num, den, scores, carry = line.step(
        attention_local,
        lengths_here,
        first,
        attn_in,
        qkv_weight,
        qkv_bias.astype(WIDE)[None, :],
        tables,
        mix,
        wrow,
    )
    arrived = shift_rows(carry, "seq", 1)

    def up_group(part):
        shape = (D // owners, FF)
        at = (0, part * Rounds.PARTS)
        columns = FF // COLUMNS // 2
        group("up", shape, at, (norm_own, norm_in), (1,), (up_grad, up_in), columns)

    up_group(0)
    for _ in range(hops - 1):
        passed = line.step(pass_on, carry, arrived, lengths_here, first)
        arrived = shift_rows(passed, "seq", 1)
    reduction.step()
    up_group(1)
    attn_low, grad_q, grad_k, grad_v, carry_back = line.step(
        attention_middle,
        lengths_here,
        first,
        cot,
        dense_weight,
        fq,
        fk,
        value,
        phi_q,
        rot_q,
        num,
        den,
        scores,
        arrived,
        tables,
        mix,
    )
    arrived_back = shift_rows(carry_back, "seq", -1)
    low_own, low_send = line.step(lambda *a: pick(a[:1], a[1]), attn_low, me)
    low_in = swap(low_send, 0)
    reduction.step()
    output = line.step(
        layer_output,
        attn_low,
        dense_weight,
        inputs_flat,
        mlp_out,
        dense_bias,
        down_bias,
    )
    for _ in range(hops - 1):
        passed = line.step(pass_on, carry_back, arrived_back, lengths_here, first)
        arrived_back = shift_rows(passed, "seq", -1)
    shape = (D // owners, D)
    group("dense", shape, (0, 0), (low_own, low_in), (0,), (cot, cot_in), across)
    qkv_grad, qkv_send = line.step(
        attention_last,
        lengths_here,
        first,
        grad_q,
        grad_k,
        grad_v,
        fk,
        value,
        phi_k,
        rot_k,
        arrived_back,
        tables,
        mix,
    )
    reduction.step()
    qkv_in = line.send(qkv_send, lambda a: swap(a, 0))
    input_grad, sums, qkv_sums = line.step(
        norm_back,
        qkv_grad,
        qkv_weight,
        mlp_norm_grad,
        unit,
        rate,
        cot,
        ln1_gain,
        ln2_gain,
    )

    def qkv_group(part):
        shape = (D // owners, 3 * D)
        at = (0, part * Rounds.PARTS)
        group("qkv", shape, at, (norm_own, norm_in), (0,), (qkv_grad, qkv_in), 2)

    qkv_group(0)
    reduction.step()
    vectors = Vectors(
        line, (sums[0], sums[1], sums[2], sums[3], qkv_sums[0], sums[4], up_sums[0])
    )
    for part in range(1, 3):
        qkv_group(part)
        vectors.take()
        reduction.step()
        vectors.send()
    while not reduction.finished():
        vectors.take()
        reduction.step()
        vectors.send()
    totals = reduction.results()
    (
        attn_gain_total,
        attn_shift_total,
        mlp_gain_total,
        mlp_shift_total,
        qkv_bias_total,
        bias_total,
        up_bias_total,
    ) = vectors.results()

    return (
        output.reshape(inputs.shape),
        input_grad.reshape(inputs.shape),
        attn_gain_total,
        attn_shift_total,
        mlp_gain_total,
        mlp_shift_total,
        totals["qkv"],
        qkv_bias_total,
        totals["dense"],
        bias_total,
        totals["up"],
        up_bias_total,
        totals["down"],
        bias_total,
    )


def solution(mesh):
    placed = (
        P("batch", "seq", None),
        P("batch", None),
        P(),
        P(),
        P(),
        P(),
        P(),
        P(),
        P(),
        P(),
        P(),
        P(),
        P(),
        P(),
        P(),
        P(),
        P("batch", "seq", None),
    )
    return jax.shard_map(
        shards,
        mesh=mesh,
        in_specs=placed,
        out_specs=(
            P("batch", "seq", None),
            P("batch", "seq", None),
            P("batch"),
            P("batch"),
            P("batch"),
            P("batch"),
            P("batch", None),
            P("batch"),
            P("batch", None),
            P("batch"),
            P("batch", None),
            P("batch"),
            P("batch", None),
            P("batch"),
        ),
        check_vma=False,
    )
```

```python
import math
from functools import partial

import jax
import jax.numpy as jnp
import numpy as np
from jax import lax
from jax.experimental import pallas as pl
from jax.experimental.pallas import tpu as pltpu
from jax.sharding import PartitionSpec as P

D = 1024
HEADS = 16
HEAD = 64
ROT = 16
FF = 4096
PAIR = 2 * HEAD
BLOCK = 128
COLUMNS = 512

EPSILON = 1e-05
ROTARY_BASE = 10000.0

def lasting(microseconds):
    return pl.CostEstimate(
        flops=int(microseconds * 1.15e9), transcendentals=0, bytes_accessed=0
    )


ROWS_COLS = ((1,), (0,))
ROWS_ROWS = ((1,), (1,))
COLS_COLS = ((0,), (0,))
NARROW = jnp.bfloat16
WIDE = jnp.float32


def plain_dot(left, right, dims):
    return lax.dot_general(left, right, (dims, ((), ())), preferred_element_type=WIDE)


def whole_spec(shape):
    return pl.BlockSpec(shape, lambda *_: (0,) * len(shape))


def shift_rows(value, axis, by):
    count = lax.axis_size(axis)
    return lax.ppermute(
        value, axis, [(i, i + by) for i in range(count) if 0 <= i + by < count]
    )


def in_hbm(*values):
    return [
        pltpu.with_memory_space_constraint(v, pltpu.HBM)
        if v.size * v.dtype.itemsize >= 1 << 16
        else v
        for v in values
    ]


def swap(value, bit):
    count = lax.axis_size("batch")
    return lax.ppermute(value, "batch", [(i, i ^ (1 << bit)) for i in range(count)])


def owner_order(bits):
    return sorted(
        range(1 << len(bits)), key=lambda r: tuple(-((r >> bit) & 1) for bit in bits)
    )


def line_rounds(count):
    half = count // 2
    rounds = [("in", [(k, k + 1), (count - 1 - k, count - 2 - k)], k) for k in range(half - 1)]
    rounds.append(("in", [(half - 1, half), (half, half - 1)], -1))
    for k in range(half - 2, -1, -1):
        rounds.append(("out", [(k + 1, k), (count - 2 - k, count - 1 - k)], k))
    return rounds


class Line:
    def __init__(self):
        self.last = None

    def wait(self, *values):
        if self.last is not None:
            values, _ = lax.optimization_barrier((values, self.last))
        return values

    def send(self, value, how):
        return how(*self.wait(value))

    def step(self, function, *values):
        out = function(*self.wait(*values))
        self.last = jax.tree.leaves(out)[0]
        return out


def pack_kernel(order, sizes, me_ref, *refs):
    ins, out_ref = refs[:-1], refs[-1]
    at, sizes = 0, list(sizes)
    for ref in ins:
        count = ref.shape[0]
        size, sizes = sizes[0], sizes[count:]
        for k, relative in enumerate(order):
            start = pl.multiple_of((relative ^ me_ref[0]) * size, BLOCK)
            block = ref[:, pl.ds(start, size)]
            for j in range(count):
                out_ref[k : k + 1, at + j * size : at + (j + 1) * size] = block[j : j + 1]
        at += count * size


def pack(order, sizes, me, *blocks):
    return pl.pallas_call(
        partial(pack_kernel, order, sizes),
        in_specs=[pl.BlockSpec(memory_space=pltpu.SMEM)]
        + [pl.BlockSpec(memory_space=pltpu.VMEM)] * len(blocks),
        out_specs=pl.BlockSpec(memory_space=pltpu.VMEM),
        out_shape=jax.ShapeDtypeStruct((len(order), sum(sizes)), WIDE),
        name="pack_vectors",
    )(me, *blocks)


class Vectors:
    def __init__(self, line, blocks):
        owners = lax.axis_size("batch")
        me = lax.axis_index("batch").astype(jnp.int32)
        self.line = line
        vectors = [v for block in blocks for v in block]
        self.sizes = [v.shape[0] // owners for v in vectors]
        bits = list(range(owners.bit_length() - 1))
        order = owner_order(bits)
        if any(size % BLOCK for size in self.sizes):
            pieces = jnp.concatenate([v.reshape(owners, -1) for v in vectors], axis=1)
            rows = [lax.dynamic_slice_in_dim(pieces, r ^ me, 1, 0) for r in order]
            self.held = jnp.concatenate(rows)
        else:
            self.held = line.step(lambda *a: pack(order, self.sizes, *a), me[None], *blocks)
        count = lax.axis_size("seq")
        self.steps = [("swap", bit, 0) for bit in bits]
        self.steps += line_rounds(count) if count % 2 == 0 else []
        self.moving = None
        self.now = None
        self.send()

    def send(self):
        if self.moving is not None or not self.steps:
            return
        self.now = kind, what, _ = self.steps.pop(0)
        if kind == "swap":
            half = self.held.shape[0] // 2
            self.moving = self.line.send(self.held[:half], lambda a: swap(a, what))
            self.held = self.held[half:]
        else:
            self.moving = self.line.send(self.held, lambda a: lax.ppermute(a, "seq", what))

    def take(self):
        if self.moving is None:
            return
        kind, _, at = self.now
        if kind == "out":
            place, count = lax.axis_index("seq"), lax.axis_size("seq")
            edge = (place == at) | (place == count - 1 - at)
            self.held = self.line.step(
                lambda a, b: jnp.where(edge, b, a), self.held, self.moving
            )
        else:
            self.held = self.line.step(lambda a, b: a + b, self.held, self.moving)
        self.moving = None

    def results(self):
        while self.moving is not None or self.steps:
            self.take()
            self.send()
        if lax.axis_size("seq") % 2 and lax.axis_size("seq") > 1:
            self.held = lax.psum(self.held, "seq")
        out, at = [], 0
        for size in self.sizes:
            out.append(self.held[0, at : at + size])
            at += size
        return out


class Reduction:
    def __init__(self, line, left, right, bits):
        self.line = line
        half = left.shape[1] // 2
        send = line.step(lambda a, b: plain_dot(a, b, COLS_COLS), left[:, :half], right)
        self.held = line.step(lambda a, b: plain_dot(a, b, COLS_COLS), left[:, half:], right)
        count = lax.axis_size("seq")
        self.steps = [("swap", bit + 1, 0) for bit in bits]
        self.steps += line_rounds(count) if count % 2 == 0 else []
        self.moving = swap(send, bits[0] + 1)

    def finish(self):
        place, count = lax.axis_index("seq"), lax.axis_size("seq")
        for i, (kind, _, at) in enumerate(self.steps):
            if kind == "out":
                edge = (place == at) | (place == count - 1 - at)
                self.held = self.line.step(
                    lambda a, b: jnp.where(edge, b, a), self.held, self.moving
                )
            else:
                self.held = self.line.step(lambda a, b: a + b, self.held, self.moving)
            if i + 1 == len(self.steps):
                break
            kind, what, _ = self.steps[i + 1]
            if kind == "swap":
                half = self.held.shape[0] // 2
                self.moving = swap(self.held[:half], what)
                self.held = self.held[half:]
            else:
                self.moving = lax.ppermute(self.held, "seq", what)
        return self.held if count % 2 == 0 or count == 1 else lax.psum(self.held, "seq")


class Singly:
    def __init__(self, line, bits):
        self.line, self.bits = line, bits
        self.pieces, self.outputs = [], {}

    def prepare(self, target, pieces):
        _, _, at, size = target
        for left, left_in, block, right, right_in, (row, column) in pieces:
            wide = COLUMNS // Rounds.PARTS
            across = size[1] // wide
            starts = [((at[1] + i) * across + column) * wide for i in range(Rounds.PARTS)]
            right, right_in = (
                jnp.concatenate([value[:, k : k + wide] for k in starts], axis=1)
                for value in (right, right_in)
            )
            left = jnp.concatenate([left[block], rounded(left_in[block])], axis=0)
            right = jnp.concatenate([right, rounded(right_in)], axis=0)
            done = Reduction(self.line, left, right, self.bits)
            self.pieces.append((target, row, starts, wide, done))

    def step(self, *arrived):
        pass

    def finished(self):
        return True

    def results(self):
        for (name, shape, at, size), row, starts, wide, piece in self.pieces:
            whole = self.outputs.get(name, jnp.zeros(shape, WIDE))
            total = piece.finish()
            top = at[0] * size[0] + row * total.shape[0]
            for i, k in enumerate(starts):
                whole = lax.dynamic_update_slice(
                    whole, total[:, i * wide : (i + 1) * wide], (top, k)
                )
            self.outputs[name] = whole
        return self.outputs


def rounded(arrived):
    one = jnp.where(lax.axis_index("seq") < lax.axis_size("seq"), 1.0, 0.5)
    return (arrived * one).astype(NARROW)


def product_kernel(count, *refs):
    ins, (to_x, to_y, hold_a, hold_b) = refs[: 8 * count], refs[-4:]
    for p in range(count):
        for i, (to, hold) in enumerate(((to_x, hold_a), (to_y, hold_b))):
            left, left_in, right, right_in = ins[8 * p + 4 * i : 8 * p + 4 * i + 4]
            whole = jnp.concatenate([left[0], left_in[0].astype(NARROW)], axis=0)
            right = jnp.concatenate([right[...], right_in[...].astype(NARROW)], axis=0)

            def product(first, second):
                rows = [whole[:, k * BLOCK : (k + 1) * BLOCK] for k in (first, second)]
                return plain_dot(jnp.concatenate(rows, axis=1), right, COLS_COLS)

            out = pl.ds(p * 2 * BLOCK, 2 * BLOCK)
            to[out, :] = product(0, 1 if i else 2)
            hold[out, :] = product(2 if i else 1, 3)


def round_kernel(counts, places, skip, *refs):
    first, second, inward, middle, outward = counts
    refs = list(refs)
    edge = refs.pop(0)[0] != 0

    def take(flag, count):
        return [refs.pop(0) for _ in range(count)] if flag else [None] * count

    from_x, from_y = take(first or second, 2)
    hold_a, hold_b = take(first, 2)
    kept_a, kept_b = take(second, 2)
    (sums,) = take(inward, 1)
    (from_end,) = take(inward or outward, 1)
    inner, from_middle = take(middle, 2)
    (whole,) = take(outward, 1)
    take(True, skip)
    to_x, to_y, keep_a, keep_b = take(first, 4)
    (new_sums,) = take(second, 1)
    (to_end,) = take(second or middle, 1)
    (new_inner,) = take(inward, 1)
    (final,) = take(outward, 1)
    for p in range(first):
        low = pl.ds(2 * p * BLOCK, BLOCK)
        high = pl.ds((2 * p + 1) * BLOCK, BLOCK)
        out = pl.ds(p * BLOCK, BLOCK)
        to_y[out, :] = hold_a[low, :] + from_x[low, :]
        to_x[out, :] = hold_b[low, :] + from_y[low, :]
        keep_a[out, :] = hold_a[high, :] + from_x[high, :]
        keep_b[out, :] = hold_b[high, :] + from_y[high, :]
    for p in range(max(second, middle)):
        for i, (kept, arrived) in enumerate(((kept_a, from_y), (kept_b, from_x))):
            out = pl.ds((2 * p + i) * BLOCK, BLOCK)
            ends = inners = None
            if p < second:
                come = pl.ds((2 * first + p) * BLOCK, BLOCK)
                ends = kept[pl.ds(p * BLOCK, BLOCK), :] + arrived[come, :]
                new_sums[out, :] = ends
            if p < middle:
                inners = inner[out, :] + from_middle[out, :]
            if ends is None:
                to_end[out, :] = inners
            elif inners is None:
                to_end[out, :] = ends
            else:
                to_end[out, :] = jnp.where(edge, ends, inners)
    if inward:
        new_inner[...] = sums[...] + from_end[: 2 * inward * BLOCK, :]
    for k, (row, column) in enumerate(places):
        rows = pl.ds(k * BLOCK, BLOCK)
        wide = final.shape[1] // (1 + max(column for _, column in places))
        total = jnp.where(edge, from_end[rows, :], whole[rows, :])
        final[row * BLOCK : (row + 1) * BLOCK, column * wide : (column + 1) * wide] = total


class Rounds:
    PARTS = 2

    def __init__(self, line, edge, counts):
        self.line, self.edge, self.counts = line, edge, counts
        self.made = self.at = 0
        self.buffers, self.moving, self.hold, self.kept = {}, {}, {}, {}
        self.sums, self.inner, self.whole, self.targets = {}, {}, None, []
        self.outputs = {}
        self.end = self.middle = None
        self.wide = COLUMNS // self.PARTS

    def count(self, group):
        return self.counts[group] if 0 <= group < len(self.counts) else 0

    def place(self, value, local, sent):
        if local:
            return pltpu.with_memory_space_constraint(value, pltpu.HBM)
        return pltpu.with_memory_space_constraint(value, pltpu.HBM) if sent else value

    def rows_spec(self, rows, at=0):
        return pl.BlockSpec((rows, self.wide), lambda i: (at, i))

    def prepare(self, target, pieces):
        r = self.made
        self.made += 1
        self.targets.append((target, [piece[5] for piece in pieces]))
        count = len(pieces) // 2
        name, shape, at, size = target
        across = size[1] // self.wide
        args, specs = [], []
        for left, left_in, block, right, right_in, (_, column) in pieces:
            for value in (left, left_in):
                args += in_hbm(value) if value is left else [value]
                specs.append(
                    pl.BlockSpec((1, *value.shape[1:]), lambda i, block=block: (block, 0, 0))
                )
            for value in (right, right_in):
                args += in_hbm(value) if value is right else [value]
                specs.append(
                    pl.BlockSpec(
                        (value.shape[0], self.wide),
                        lambda i, c=column: (0, (at[1] + i) * across + c),
                    )
                )
        rows = 2 * count * BLOCK
        total = rows + self.count(r - 1) * BLOCK
        call = pl.pallas_call(
            partial(product_kernel, count),
            grid=(self.PARTS,),
            in_specs=specs,
            out_specs=[self.rows_spec(rows)] * 4,
            out_shape=[pltpu.HBM((total, COLUMNS), WIDE)] * 2
            + [pltpu.HBM((rows, COLUMNS), WIDE)] * 2,
            cost_estimate=lasting(5.0),
        compiler_params=pltpu.CompilerParams(vmem_limit_bytes=25165824),
        name="piece_products",
        )
        to_x, to_y, hold_a, hold_b = self.line.step(call, *args)
        self.hold[r] = (hold_a, hold_b)
        if r:
            self.buffers[r] = (to_x, to_y)
        else:
            self.moving[r] = (swap(to_x, 1), swap(to_y, 2))

    def step(self, *arrived):
        r = self.at
        self.at += 1
        counts = [self.count(r - back) for back in (0, 1, 2, 3, 4)]
        first, second, inward, middle, outward = counts
        aliases = {}
        args, specs = [self.edge], [pl.BlockSpec(memory_space=pltpu.SMEM)]

        def add(value, local=False, sent=False):
            args.append(self.place(value, local, sent))
            specs.append(self.rows_spec(value.shape[0]))

        if first or second:
            for value in self.moving.pop(r):
                add(value)
        if first:
            for value in self.hold.pop(r):
                add(value, local=True)
        if second:
            for value in self.kept.pop(r - 1):
                add(value, local=True)
        if inward:
            add(self.sums.pop(r - 2), local=True)
        if inward or outward:
            add(self.end)
        if middle:
            add(self.inner.pop(r - 3), sent=True)
            add(self.middle)
        if outward:
            add(self.whole, sent=True)
        outs, out_specs = [], []

        def out(rows, at=0, of=None, sent=False):
            kind = pltpu.HBM if sent else pltpu.HBM
            outs.append(kind((of or rows, COLUMNS), WIDE))
            out_specs.append(self.rows_spec(rows, at))

        ahead = self.count(r + 1)
        if ahead:
            aliases = {len(args): 0, len(args) + 1: 1}
            args += list(self.buffers.pop(r + 1))
            specs += [pl.BlockSpec(memory_space=pl.ANY)] * 2
        if first:
            for _ in range(2):
                out(first * BLOCK, 2 * ahead // first, (2 * ahead + first) * BLOCK, sent=True)
            out(first * BLOCK)
            out(first * BLOCK)
        if second:
            out(2 * second * BLOCK)
        if second or middle:
            out(2 * max(second, middle) * BLOCK, sent=True)
        if inward:
            out(2 * inward * BLOCK, sent=True)
        places = ()
        if outward:
            (name, shape, at, size), places = self.targets[r - 4]
            if name in self.outputs:
                aliases[len(args)] = len(outs)
                args.append(self.outputs[name])
                specs.append(pl.BlockSpec(memory_space=pl.ANY))
            outs.append(pltpu.HBM(shape, WIDE))
            out_specs.append(pl.BlockSpec(size, lambda i: (at[0], at[1] + i)))
        args += arrived
        specs += [pl.BlockSpec(memory_space=pl.ANY)] * len(arrived)
        call = pl.pallas_call(
            partial(round_kernel, counts, places, len(aliases) + len(arrived)),
            grid=(self.PARTS,),
            in_specs=specs,
            out_specs=out_specs,
            out_shape=outs,
            input_output_aliases=aliases,
            cost_estimate=lasting(5.0),
            compiler_params=pltpu.CompilerParams(vmem_limit_bytes=25165824),
            name="reduce_round",
        )
        got = list(self.line.step(call, *args))
        if first:
            self.moving[r + 1] = (swap(got.pop(0), 1), swap(got.pop(0), 2))
            self.kept[r] = (got.pop(0), got.pop(0))
        if second:
            self.sums[r - 1] = got.pop(0)
        self.whole = None
        if second or middle:
            self.whole = got.pop(0)
            self.end = lax.ppermute(self.whole, "seq", [(0, 1), (1, 0), (2, 3), (3, 2)])
        if inward:
            self.inner[r - 2] = got.pop(0)
            self.middle = lax.ppermute(self.inner[r - 2], "seq", [(1, 2), (2, 1)])
        if outward:
            self.outputs[name] = got.pop(0)

    def finished(self):
        return self.at == len(self.counts) + 4

    def results(self):
        return self.outputs


def pick_kernel(me_ref, *refs):
    ins, (keep_ref, send_ref) = refs[:-2], refs[-2:]
    half = keep_ref.shape[2] // BLOCK
    for i, ref in enumerate(ins):
        for p in range(half):
            for core in range(2):
                owner = (2 * (half - 1 - p) + core) ^ me_ref[0]
                columns = ref[:, pl.ds(pl.multiple_of(owner * BLOCK, BLOCK), BLOCK)]
                at = slice(p * BLOCK, (p + 1) * BLOCK)
                if core:
                    send_ref[i, :, at] = columns.astype(WIDE)
                else:
                    keep_ref[i, :, at] = columns


def pick(arrays, me):
    owners = lax.axis_size("batch")
    half = owners // 2
    tokens, features = arrays[0].shape
    size = features // owners
    if size != BLOCK:

        def columns(value, core):
            return jnp.concatenate(
                [
                    lax.dynamic_slice_in_dim(value, ((2 * r + core) ^ me[0]) * size, size, 1)
                    for r in range(half)[::-1]
                ],
                axis=1,
            )

        return (
            jnp.stack([columns(a, 0) for a in arrays]),
            jnp.stack([columns(a, 1) for a in arrays]).astype(WIDE),
        )
    shape = (len(arrays), tokens, half * size)
    return pl.pallas_call(
        pick_kernel,
        in_specs=[pl.BlockSpec(memory_space=pltpu.SMEM)]
        + [pl.BlockSpec(memory_space=pltpu.VMEM)] * len(arrays),
        out_specs=[pl.BlockSpec(memory_space=pltpu.VMEM)] * 2,
        out_shape=[pltpu.HBM(shape, NARROW), pltpu.HBM(shape, WIDE)],
        cost_estimate=lasting(2.0),
        name="pick_columns",
    )(*in_hbm(me, *arrays))


def as_row(ref):
    return ref[...].astype(WIDE)[None, :]


def norm_kernel(x_ref, gain1, bias1, gain2, bias2, attn_ref, mlp_ref, unit_ref, rate_ref):
    x = x_ref[...].astype(WIDE)
    centered = x - jnp.mean(x, axis=-1, keepdims=True)
    rate = lax.rsqrt(jnp.mean(centered * centered, axis=-1, keepdims=True) + EPSILON)
    unit = centered * rate
    unit_ref[...] = unit
    rate_ref[...] = jnp.broadcast_to(rate, rate_ref.shape)
    for gain, bias, out in ((gain1, bias1, attn_ref), (gain2, bias2, mlp_ref)):
        out[...] = (unit * as_row(gain) + as_row(bias)).astype(NARROW)


def two_norms(inputs, *gains):
    tokens = inputs.shape[0]
    rows = tokens // 4
    by_rows = pl.BlockSpec((rows, D), lambda i: (i, 0))
    return pl.pallas_call(
        norm_kernel,
        grid=(4,),
        in_specs=[by_rows] + [whole_spec((D,))] * len(gains),
        out_specs=[by_rows, by_rows, by_rows, pl.BlockSpec((rows, 128), lambda i: (i, 0))],
        out_shape=[
            pltpu.HBM((tokens, D), NARROW),
            pltpu.HBM((tokens, D), NARROW),
            pltpu.HBM((tokens, D), WIDE),
            pltpu.HBM((tokens, 128), WIDE),
        ],
        cost_estimate=lasting(4.0),
        name="two_norms",
    )(*in_hbm(inputs, *gains))


def up_kernel(
    half, me_ref, x_ref, weight_ref, bias_ref, act_ref, slope_ref, keep_ref, send_ref
):
    step = pl.program_id(0)
    up = plain_dot(x_ref[...], weight_ref[...], ROWS_COLS) + as_row(bias_ref)
    below = 0.5 * (1.0 + lax.erf(up * (0.5**0.5)))
    act = (up * below).astype(NARROW)
    act_ref[...] = act
    slope_ref[...] = below + up * jnp.exp(-0.5 * up * up) * ((2.0 * math.pi) ** -0.5)

    @pl.when(step < half)
    def _():
        for i in range(keep_ref.shape[0]):
            keep_ref[i] = act[:, i * BLOCK : (i + 1) * BLOCK]

    @pl.when(step >= half)
    def _():
        wide = act.astype(WIDE)
        for i in range(send_ref.shape[0]):
            send_ref[i] = wide[:, i * BLOCK : (i + 1) * BLOCK]


def mlp_up(mlp_in, up_weight, up_bias, me):
    owners = lax.axis_size("batch")
    tokens = mlp_in.shape[0]
    half = owners // 2
    each = FF // owners
    subs = each // BLOCK

    def natural(i, me):
        return (0, (2 * (i % half) + i // half) ^ me[0])

    return pl.pallas_call(
        partial(up_kernel, half),
        grid_spec=pltpu.PrefetchScalarGridSpec(
            num_scalar_prefetch=1,
            grid=(owners,),
            in_specs=[
                pl.BlockSpec((tokens, D), lambda i, me: (0, 0)),
                pl.BlockSpec((D, each), natural),
                pl.BlockSpec((each,), lambda i, me: natural(i, me)[1:]),
            ],
            out_specs=[
                pl.BlockSpec((tokens, each), natural),
                pl.BlockSpec((tokens, each), natural),
                pl.BlockSpec(
                    (subs, tokens, BLOCK),
                    lambda i, me: (0, 0, half - 1 - jnp.minimum(i, half - 1)),
                ),
                pl.BlockSpec(
                    (subs, tokens, BLOCK),
                    lambda i, me: (0, 0, half - 1 - jnp.maximum(i - half, 0)),
                ),
            ],
        ),
        out_shape=[
            pltpu.HBM((tokens, FF), NARROW),
            pltpu.HBM((tokens, FF), WIDE),
            pltpu.HBM((subs, tokens, half * BLOCK), NARROW),
            pltpu.HBM((subs, tokens, half * BLOCK), WIDE),
        ],
        cost_estimate=lasting(11.0),
        name="mlp_up",
    )(*in_hbm(me, mlp_in, up_weight, up_bias))


def back_kernel(
    cot_ref, down_ref, up_ref, act_ref, slope_ref, grad_ref, send_ref, sums_ref, out_ref, norm_ref
):
    step = pl.program_id(0)
    down = down_ref[...]
    grad = plain_dot(cot_ref[...], down, ROWS_ROWS) * slope_ref[...]
    grad = grad.astype(NARROW)
    grad_ref[...] = grad
    wide = grad.astype(WIDE)
    send_ref[...] = wide
    sums_ref[...] = jnp.sum(wide, axis=0, keepdims=True)
    out = plain_dot(act_ref[...], down, ROWS_COLS)
    norm = plain_dot(grad, up_ref[...], ROWS_ROWS)

    @pl.when(step == 0)
    def _():
        out_ref[...] = out
        norm_ref[...] = norm

    @pl.when(step > 0)
    def _():
        out_ref[...] += out
        norm_ref[...] += norm


def mlp_back(cot, down_weight, up_weight, act, slope):
    tokens = cot.shape[0]
    each = 1024
    by_column = pl.BlockSpec((tokens, each), lambda i: (0, i))
    total = whole_spec((tokens, D))
    return pl.pallas_call(
        back_kernel,
        grid=(FF // each,),
        in_specs=[
            total,
            pl.BlockSpec((each, D), lambda i: (i, 0)),
            pl.BlockSpec((D, each), lambda i: (0, i)),
            by_column,
            by_column,
        ],
        out_specs=[
            by_column,
            by_column,
            pl.BlockSpec((1, each), lambda i: (0, i)),
            total,
            total,
        ],
        out_shape=[
            pltpu.HBM((tokens, FF), NARROW),
            pltpu.HBM((tokens, FF), WIDE),
            pltpu.HBM((1, FF), WIDE),
            pltpu.HBM((tokens, D), WIDE),
            pltpu.HBM((tokens, D), WIDE),
        ],
        cost_estimate=lasting(16.0),
        compiler_params=pltpu.CompilerParams(vmem_limit_bytes=25165824),
        name="mlp_back",
    )(*in_hbm(cot, down_weight, up_weight, act, slope))


def output_kernel(low_ref, weight_ref, x_ref, mlp_ref, dense_ref, down_ref, out_ref):
    attn = plain_dot(low_ref[...], weight_ref[...], ROWS_COLS) + as_row(dense_ref)
    mlp = mlp_ref[...] + as_row(down_ref)
    out_ref[...] = (x_ref[...].astype(WIDE) + attn + mlp).astype(NARROW)


def layer_output(low, dense_weight, inputs, mlp_out, *biases):
    tokens = inputs.shape[0]
    each = 512
    by_column = pl.BlockSpec((tokens, each), lambda i: (0, i))
    return pl.pallas_call(
        output_kernel,
        grid=(D // each,),
        in_specs=[
            whole_spec((tokens, D)),
            pl.BlockSpec((D, each), lambda i: (0, i)),
            by_column,
            by_column,
        ]
        + [pl.BlockSpec((each,), lambda i: (i,))] * len(biases),
        out_specs=by_column,
        out_shape=pltpu.HBM((tokens, D), NARROW),
        cost_estimate=lasting(3.0),
        name="layer_output",
    )(*in_hbm(low, dense_weight, inputs, mlp_out, *biases))


def norm_back_kernel(
    qkv_ref,
    weight_ref,
    mlp_ref,
    unit_ref,
    rate_ref,
    cot_ref,
    gain1,
    gain2,
    grad_ref,
    sums_ref,
    qkv_sums,
):
    step = pl.program_id(0)
    qkv = qkv_ref[...]
    qkv_sums[...] = jnp.sum(qkv.astype(WIDE), axis=0, keepdims=True)
    part = plain_dot(qkv, weight_ref[...], ROWS_ROWS)

    @pl.when(step == 0)
    def _():
        grad_ref[...] = part

    @pl.when(step > 0)
    def _():
        grad_ref[...] += part

    @pl.when(step == pl.num_programs(0) - 1)
    def _():
        size = 64
        gain_attn, gain_mlp = as_row(gain1), as_row(gain2)
        totals = [jnp.zeros((1, D), WIDE)] * 5
        for k in range(grad_ref.shape[0] // size):
            rows = pl.ds(k * size, size)
            attn, mlp, unit = grad_ref[rows, :], mlp_ref[rows, :], unit_ref[rows, :]
            cot = cot_ref[rows, :].astype(WIDE)
            together = attn * gain_attn + mlp * gain_mlp
            grad_ref[rows, :] = cot + rate_ref[rows, 0:1] * (
                together
                - jnp.mean(together, axis=-1, keepdims=True)
                - unit * jnp.mean(together * unit, axis=-1, keepdims=True)
            )
            for i, value in enumerate((attn * unit, attn, mlp * unit, mlp, cot)):
                totals[i] = totals[i] + jnp.sum(value, axis=0, keepdims=True)
        for i, value in enumerate(totals):
            sums_ref[i : i + 1, :] = value


def norm_back(qkv_grad, qkv_weight, mlp_norm_grad, unit, rate, cot, *gains):
    tokens = cot.shape[0]
    each = 512
    total = whole_spec((tokens, D))
    return pl.pallas_call(
        norm_back_kernel,
        grid=(3 * D // each,),
        in_specs=[
            pl.BlockSpec((tokens, each), lambda i: (0, i)),
            pl.BlockSpec((D, each), lambda i: (0, i)),
            total,
            total,
            whole_spec(rate.shape),
            total,
        ]
        + [whole_spec((D,))] * len(gains),
        out_specs=[total, whole_spec((5, D)), pl.BlockSpec((1, each), lambda i: (0, i))],
        out_shape=[
            pltpu.HBM((tokens, D), WIDE),
            pltpu.HBM((5, D), WIDE),
            pltpu.HBM((1, 3 * D), WIDE),
        ],
        cost_estimate=lasting(9.0),
        compiler_params=pltpu.CompilerParams(vmem_limit_bytes=25165824),
        name="norm_back",
    )(*in_hbm(qkv_grad, qkv_weight, mlp_norm_grad, unit, rate, cot, *gains))


def dct_matrix():
    rows = np.arange(HEAD)[:, None]
    columns = np.arange(HEAD)[None, :]
    cosines = np.cos(np.pi * (columns + 0.5) * rows / HEAD) * np.sqrt(2.0 / HEAD)
    return np.where(rows == 0, cosines * np.sqrt(0.5), cosines).astype(np.float32)


def attention_tables(place, context, count):
    half_rot = ROT // 2
    lane = np.arange(PAIR) % HEAD
    freq = ROTARY_BASE ** (-2.0 * (lane % half_rot) / ROT)
    angles = np.arange(count * context)[:, None] * freq[None, :]
    tables = np.stack(
        [
            np.where(lane < ROT, np.cos(angles), 1.0),
            np.where(lane < half_rot, -np.sin(angles), 0.0),
            np.where((lane >= half_rot) & (lane < ROT), np.sin(angles), 0.0),
        ]
    )
    return lax.dynamic_slice_in_dim(
        jnp.asarray(tables.astype(np.float32)), place * context, context, 1
    )


def lane_is_low(shape):
    return lax.broadcasted_iota(jnp.int32, shape, len(shape) - 1) % PAIR < HEAD


def halves(full):
    return jnp.where(lane_is_low((HEAD, PAIR)), full[:HEAD], full[HEAD:])


def spread_pair(block):
    low = lane_is_low(block.shape)
    zero = jnp.zeros_like(block)
    return jnp.concatenate([jnp.where(low, block, zero), jnp.where(low, zero, block)], axis=0)


def one_head(tile, head):
    low = lane_is_low(tile.shape)
    zero = jnp.zeros_like(tile)
    return jnp.where(low, tile, zero) if head == 0 else jnp.where(low, zero, tile)


def in_two(value):
    high = value.astype(NARROW)
    return high, (value - high.astype(WIDE)).astype(NARROW)


def fine_dot(left, right, dims):
    left_high, left_low = in_two(left)
    right_high, right_low = in_two(right)
    return (
        plain_dot(left_high, right_high, dims)
        + plain_dot(left_low, right_high, dims)
        + plain_dot(left_high, right_low, dims)
    )


def head_sums(tile):
    rows = lax.broadcasted_iota(jnp.int32, (PAIR, PAIR), 0) // HEAD
    columns = lax.broadcasted_iota(jnp.int32, (PAIR, PAIR), 1) // HEAD
    ones = (rows == columns).astype(WIDE).astype(NARROW)
    high, low = in_two(tile)
    return plain_dot(
        jnp.concatenate([high, low], axis=1), jnp.concatenate([ones, ones], axis=0), ROWS_COLS
    )


def turn(tile, cos, sin_up, sin_down):
    half_rot = ROT // 2
    return (
        tile * cos
        + pltpu.roll(tile, PAIR - half_rot, 1) * sin_up
        + pltpu.roll(tile, half_rot, 1) * sin_down
    )


def turn_back(tile, cos, sin_up, sin_down):
    half_rot = ROT // 2
    return (
        tile * cos
        + pltpu.roll(tile * sin_up, half_rot, 1)
        + pltpu.roll(tile * sin_down, PAIR - half_rot, 1)
    )


def all_rows(tables_ref, seqs):
    return [jnp.concatenate([tables_ref[k]] * seqs, axis=0) for k in range(3)]


def feature_grad(grad, phi, turned, mix, tables):
    weighted = grad * phi
    back = fine_dot(weighted, mix, ROWS_ROWS) - (HEAD**-0.5) * turned * head_sums(weighted)
    return turn_back(back, *tables)


def doc_at(where, lengths_ref, b):
    start, found = 0, jnp.zeros_like(where) - 1
    for k in range(lengths_ref.shape[1]):
        found = found + jnp.where(start <= where, 1, 0)
        start = start + lengths_ref[b, k]
    return found


def same_doc_before(lengths_ref, b, first, context):
    query = first + lax.broadcasted_iota(jnp.int32, (context, context), 0)
    key = first + lax.broadcasted_iota(jnp.int32, (context, context), 1)
    same = doc_at(query, lengths_ref, b) == doc_at(key, lengths_ref, b)
    return jnp.where(same & (key <= query), 1.0, 0.0)


def in_doc_of(lengths_ref, b, first, context, where):
    rows = first + lax.broadcasted_iota(jnp.int32, (context, PAIR), 0)
    return jnp.where(doc_at(rows, lengths_ref, b) == doc_at(where, lengths_ref, b), 1.0, 0.0)


def local_kernel(
    seqs,
    lengths_ref,
    first_ref,
    attn_ref,
    weight_ref,
    bias_ref,
    tables_ref,
    dct_ref,
    points_ref,
    weights_ref,
    fq_ref,
    fk_ref,
    val_ref,
    phiq_ref,
    phik_ref,
    rotq_ref,
    rotk_ref,
    num_ref,
    den_ref,
    score_ref,
    carry_ref,
    mix_ref,
):
    context = tables_ref.shape[1]
    first = first_ref[0]

    @pl.when(pl.program_id(0) == 0)
    def _():
        both = lax.dot_general(
            dct_ref[...],
            points_ref[...],
            (COLS_COLS, ((), ())),
            precision=lax.Precision.HIGHEST,
            preferred_element_type=WIDE,
        )
        mix_ref[...] = spread_pair(jnp.concatenate([both, both], axis=1) * HEAD ** (-0.25))

    mix = mix_ref[...]
    weights = as_row(weights_ref)
    wrow = jnp.concatenate([weights, weights], axis=1)
    tables = all_rows(tables_ref, seqs)
    low = lane_is_low((seqs * context, PAIR))
    block = plain_dot(attn_ref[...], weight_ref[...], ROWS_COLS) + bias_ref[...]
    one, two, three = block[:, :PAIR], block[:, PAIR : 2 * PAIR], block[:, 2 * PAIR :]
    query = jnp.where(low, one, two)
    key = pltpu.roll(jnp.where(low, three, one), HEAD, 1)
    value_all = jnp.where(low, two, three).astype(NARROW)
    val_ref[...] = value_all

    def features(raw):
        turned = turn(raw, *tables)
        power = fine_dot(turned, mix, ROWS_COLS) - (0.5 * HEAD**-0.5) * head_sums(turned * turned)
        return turned, wrow * jnp.exp(power)

    turned_q, phi_q = features(query)
    turned_k, phi_k = features(key)
    rotq_ref[...], rotk_ref[...] = turned_q, turned_k
    phiq_ref[...], phik_ref[...] = phi_q, phi_k
    fq_all, fk_all = phi_q.astype(NARROW), phi_k.astype(NARROW)
    fq_ref[...], fk_ref[...] = fq_all, fk_all
    low = lane_is_low((context, PAIR))
    for b in range(seqs):
        rows = slice(b * context, (b + 1) * context)
        fq, fk, value = fq_all[rows], fk_all[rows], value_all[rows]
        mask = same_doc_before(lengths_ref, b, first, context)
        keep = in_doc_of(lengths_ref, b, first, context, first + context - 1)
        wide_value = jnp.concatenate([value, jnp.ones_like(value)], axis=1)
        sums = []
        for h in range(2):
            scores = (plain_dot(one_head(fq, h), fk, ROWS_ROWS) * mask).astype(NARROW)
            score_ref[0, b, h] = scores
            sums.append(plain_dot(scores, wide_value, ROWS_COLS))
        num_ref[rows, :] = jnp.where(low, sums[0][:, :PAIR], sums[1][:, :PAIR])
        den_ref[rows, :] = jnp.where(low, sums[0][:, PAIR:], sums[1][:, PAIR:])
        kept = fk * keep.astype(NARROW)
        carry_ref[b, 0, :HEAD, :] = halves(plain_dot(kept, value, COLS_COLS))
        norm = jnp.sum(kept.astype(WIDE), axis=0, keepdims=True)
        carry_ref[b, 0, HEAD:, :] = jnp.broadcast_to(norm, (8, PAIR))


def middle_kernel(
    seqs,
    lengths_ref,
    first_ref,
    cot_ref,
    dense_ref,
    fq_ref,
    fk_ref,
    val_ref,
    phiq_ref,
    rotq_ref,
    num_ref,
    den_ref,
    score_ref,
    carry_ref,
    tables_ref,
    mix_ref,
    low_ref,
    gradq_ref,
    gradk_ref,
    gradv_ref,
    out_ref,
):
    context = tables_ref.shape[1]
    first = first_ref[0]
    mix = mix_ref[...]
    tables = all_rows(tables_ref, seqs)
    low = lane_is_low((context, PAIR))
    back_all = plain_dot(cot_ref[...], dense_ref[...], ROWS_ROWS)
    grads_q = []
    for b in range(seqs):
        rows = pl.ds(b * context, context)
        fq, fk, value = fq_ref[rows, :], fk_ref[rows, :], val_ref[rows, :]
        use = in_doc_of(lengths_ref, b, first, context, first - 1)
        state = spread_pair(carry_ref[b, 0, :HEAD, :].astype(NARROW))
        norm = carry_ref[b, 0, HEAD : HEAD + 1, :]
        wide_fq = fq.astype(WIDE)
        num = num_ref[rows, :] + use * plain_dot(fq, state, ROWS_COLS)
        den = den_ref[rows, :] + use * head_sums(wide_fq * norm)
        heads_out = num / den
        low_ref[rows, :] = heads_out.astype(NARROW)
        back = back_all[b * context : (b + 1) * context]
        num_grad = (back / den).astype(NARROW)
        den_grad = -head_sums(back * heads_out) / den
        mask = same_doc_before(lengths_ref, b, first, context)
        parts_q, parts_k, parts_v = [], [], []
        for h in range(2):
            column = den_grad[:, h * HEAD : h * HEAD + 1]
            score_grad = plain_dot(one_head(num_grad, h), value, ROWS_ROWS) + column
            score_grad = (score_grad * mask).astype(NARROW)
            parts_q.append(plain_dot(score_grad, fk, ROWS_COLS))
            parts_k.append(plain_dot(score_grad, fq, COLS_COLS))
            parts_v.append(plain_dot(score_ref[0, b, h], num_grad, COLS_COLS))
        gradk_ref[rows, :] = jnp.where(low, parts_k[0], parts_k[1])
        gradv_ref[rows, :] = jnp.where(low, parts_v[0], parts_v[1])
        num_used = num_grad * use.astype(NARROW)
        den_used = den_grad * use
        grads_q.append(
            jnp.where(low, parts_q[0], parts_q[1])
            + plain_dot(num_used, state, ROWS_ROWS)
            + den_used * norm
        )
        out_ref[b, 0, :HEAD, :] = halves(plain_dot(fq, num_used, COLS_COLS))
        norm_grad = jnp.sum(den_used * wide_fq, axis=0, keepdims=True)
        out_ref[b, 0, HEAD:, :] = jnp.broadcast_to(norm_grad, (8, PAIR))
    gradq_ref[...] = feature_grad(
        jnp.concatenate(grads_q, axis=0), phiq_ref[...], rotq_ref[...], mix, tables
    ).astype(NARROW)


def last_kernel(
    seqs,
    lengths_ref,
    first_ref,
    gradq_ref,
    gradk_ref,
    gradv_ref,
    fk_ref,
    val_ref,
    phik_ref,
    rotk_ref,
    carry_ref,
    tables_ref,
    mix_ref,
    out_ref,
    send_ref,
):
    context = tables_ref.shape[1]
    first = first_ref[0]
    tables = all_rows(tables_ref, seqs)
    grads_k, grads_v = [], []
    for b in range(seqs):
        rows = pl.ds(b * context, context)
        keep = in_doc_of(lengths_ref, b, first, context, first + context - 1)
        state = spread_pair(carry_ref[b, 0, :HEAD, :].astype(NARROW))
        norm = carry_ref[b, 0, HEAD : HEAD + 1, :]
        grads_k.append(
            gradk_ref[rows, :] + keep * (plain_dot(val_ref[rows, :], state, ROWS_ROWS) + norm)
        )
        grads_v.append(gradv_ref[rows, :] + keep * plain_dot(fk_ref[rows, :], state, ROWS_COLS))
    grad_k = feature_grad(
        jnp.concatenate(grads_k, axis=0), phik_ref[...], rotk_ref[...], mix_ref[...], tables
    )
    grad_k = pltpu.roll(grad_k, HEAD, 1)
    grad_v = jnp.concatenate(grads_v, axis=0)
    grad_q = gradq_ref[...].astype(WIDE)
    low = lane_is_low(grad_q.shape)
    grad = jnp.concatenate(
        [
            jnp.where(low, grad_q, grad_k),
            jnp.where(low, grad_v, grad_q),
            jnp.where(low, grad_k, grad_v),
        ],
        axis=1,
    ).astype(NARROW)
    out_ref[...] = grad
    send_ref[...] = grad.astype(WIDE)


def pass_kernel(lengths_ref, first_ref, own_ref, arrived_ref, out_ref):
    context = first_ref[1]
    for b in range(own_ref.shape[0]):
        last = doc_at(first_ref[0] + context - 1, lengths_ref, b)
        through = last == doc_at(first_ref[0] - 1, lengths_ref, b)
        out_ref[b] = own_ref[b] + jnp.where(through, arrived_ref[b], 0.0)


SMEM_SPEC = pl.BlockSpec(memory_space=pltpu.SMEM)


def pass_on(own, arrived, lengths, first):
    seqs, pairs = own.shape[:2]
    spec = pl.BlockSpec((seqs, pairs // 2, *own.shape[2:]), lambda i: (0, i, 0, 0))
    return pl.pallas_call(
        pass_kernel,
        grid=(2,),
        in_specs=[SMEM_SPEC, SMEM_SPEC, spec, spec],
        out_specs=spec,
        out_shape=pltpu.HBM(own.shape, WIDE),
        cost_estimate=lasting(2.0),
        name="pass_carry",
    )(*in_hbm(lengths, first, own, arrived))


def pair_spec(rows):
    return pl.BlockSpec((None, rows, PAIR), lambda i: (i, 0, 0))


def pair_shapes(tokens):
    shape = (HEADS // 2, tokens, PAIR)
    return pltpu.HBM(shape, NARROW), pltpu.HBM(shape, WIDE)


def attention_specs(seqs, context):
    carry = pl.BlockSpec((seqs, 1, HEAD + 8, PAIR), lambda i: (0, i, 0, 0))
    scores = pl.BlockSpec((1, seqs, 2, context, context), lambda i: (i, 0, 0, 0, 0))
    return carry, scores, [whole_spec((3, context, PAIR)), whole_spec((PAIR, PAIR))]


def attention_local(lengths, first, attn_in, weight, bias, tables, points, weights):
    seqs, context, tokens = lengths.shape[0], tables.shape[1], attn_in.shape[0]
    pairs = HEADS // 2
    carry, scores, shared = attention_specs(seqs, context)
    narrow, wide = pair_shapes(tokens)
    return pl.pallas_call(
        partial(local_kernel, seqs),
        grid=(pairs,),
        in_specs=[
            SMEM_SPEC,
            SMEM_SPEC,
            whole_spec((tokens, D)),
            pl.BlockSpec((D, 3 * PAIR), lambda i: (0, i)),
            pl.BlockSpec((1, 3 * PAIR), lambda i: (0, i)),
            shared[0],
            whole_spec((HEAD, HEAD)),
            whole_spec((HEAD, HEAD)),
            whole_spec((HEAD,)),
        ],
        out_specs=[pair_spec(tokens)] * 9 + [scores, carry, shared[1]],
        out_shape=[narrow] * 3
        + [wide] * 6
        + [
            pltpu.HBM((pairs, seqs, 2, context, context), NARROW),
            pltpu.HBM((seqs, pairs, HEAD + 8, PAIR), WIDE),
            pltpu.HBM((PAIR, PAIR), WIDE),
        ],
        cost_estimate=lasting(14.0),
        compiler_params=pltpu.CompilerParams(vmem_limit_bytes=25165824),
        name="attention_local",
    )(*in_hbm(lengths, first, attn_in, weight, bias, tables, dct_matrix(), points, weights))


def attention_middle(lengths, first, cot, dense_weight, *rest):
    seqs, context, tokens = lengths.shape[0], rest[-2].shape[1], cot.shape[0]
    pairs = HEADS // 2
    carry, scores, shared = attention_specs(seqs, context)
    narrow, wide = pair_shapes(tokens)
    return pl.pallas_call(
        partial(middle_kernel, seqs),
        grid=(pairs,),
        in_specs=[
            SMEM_SPEC,
            SMEM_SPEC,
            whole_spec((tokens, D)),
            pl.BlockSpec((PAIR, D), lambda i: (i, 0)),
        ]
        + [pair_spec(tokens)] * 7
        + [scores, carry, *shared],
        out_specs=[pl.BlockSpec((tokens, PAIR), lambda i: (0, i))]
        + [pair_spec(tokens)] * 3
        + [carry],
        out_shape=[pltpu.HBM((tokens, D), NARROW), narrow, wide, wide]
        + [pltpu.HBM((seqs, pairs, HEAD + 8, PAIR), WIDE)],
        cost_estimate=lasting(20.0),
        compiler_params=pltpu.CompilerParams(vmem_limit_bytes=25165824),
        name="attention_middle",
    )(*in_hbm(lengths, first, cot, dense_weight, *rest))


def attention_last(lengths, first, *rest):
    seqs, context, tokens = lengths.shape[0], rest[-2].shape[1], rest[0].shape[1]
    carry, _, shared = attention_specs(seqs, context)
    return pl.pallas_call(
        partial(last_kernel, seqs),
        grid=(HEADS // 2,),
        in_specs=[SMEM_SPEC, SMEM_SPEC] + [pair_spec(tokens)] * 7 + [carry, *shared],
        out_specs=[pl.BlockSpec((tokens, 3 * PAIR), lambda i: (0, i))] * 2,
        out_shape=[
            pltpu.HBM((tokens, 3 * D), NARROW),
            pltpu.HBM((tokens, 3 * D), WIDE),
        ],
        cost_estimate=lasting(10.0),
        compiler_params=pltpu.CompilerParams(vmem_limit_bytes=25165824),
        name="attention_last",
    )(*in_hbm(lengths, first, *rest))


def shards(
    inputs,
    lengths,
    ln1_gain,
    ln1_bias,
    ln2_gain,
    ln2_bias,
    qkv_weight,
    qkv_bias,
    dense_weight,
    dense_bias,
    up_weight,
    up_bias,
    down_weight,
    down_bias,
    qmc_points,
    qmc_weights,
    cotangent,
):
    seqs, context = inputs.shape[:2]
    tokens = seqs * context
    owners, count, place = lax.axis_size("batch"), lax.axis_size("seq"), lax.axis_index("seq")
    bits = list(range(owners.bit_length() - 2))[::-1]
    across = D // COLUMNS
    hops = max(1, count // 2)

    line = Line()
    me = lax.axis_index("batch").astype(jnp.int32)[None]
    edge = ((place == 0) | (place == count - 1)).astype(jnp.int32)[None]
    if owners == 8 and count == 4:
        reduction = Rounds(line, edge, [2, 2, 2, 2, 1, 1, 1, 1])
    else:
        reduction = Singly(line, bits)

    def group(name, shape, at, left, blocks, right, columns):
        pieces = [
            (*left, block, *right, (row, column))
            for column in range(columns)
            for row, block in enumerate(blocks)
        ]
        size = (len(blocks) * BLOCK_ROWS, columns * COLUMNS // Rounds.PARTS)
        reduction.prepare((name, shape, at, size), pieces)

    BLOCK_ROWS = min(BLOCK, D // owners)
    inputs_flat = inputs.reshape(tokens, D)
    cot = cotangent.reshape(tokens, D)
    cot_in = swap(cot.astype(WIDE), 0)
    start = place * context
    first = jnp.stack([start, jnp.full((), context, jnp.int32)])
    qkv_row = qkv_bias.astype(WIDE)[None, :]
    tables = attention_tables(place, context, count)
    attn_in, mlp_in, unit, rate = line.step(
        two_norms, inputs_flat, ln1_gain, ln1_bias, ln2_gain, ln2_bias
    )
    act, slope, act_own, act_send = line.step(mlp_up, mlp_in, up_weight, up_bias, me)
    act_in = swap(act_send, 0)
    norm_own, norm_send = line.step(lambda *a: pick(a[:2], a[2]), attn_in, mlp_in, me)
    subs = act_own.shape[0]

    def down_group(sub):
        shape = (FF // owners, D)
        at = (sub // 2, 0)
        group("down", shape, at, (act_own, act_in), (sub, sub + 1), (cot, cot_in), across)

    down_group(0)
    up_grad, up_send, up_sums, mlp_out, mlp_norm_grad = line.step(
        mlp_back, cot, down_weight, up_weight, act, slope
    )
    for sub in range(2, subs, 2):
        down_group(sub)
    reduction.step(tables, qkv_row, first)
    up_in = line.send(up_send, lambda a: swap(a, 0))
    norm_in = line.send(norm_send, lambda a: swap(a, 0))

    fq, fk, value, phi_q, phi_k, rot_q, rot_k, num, den, scores, carry, mix = line.step(
        attention_local,
        lengths,
        first,
        attn_in,
        qkv_weight,
        qkv_row,
        tables,
        qmc_points,
        qmc_weights,
    )
    arrived = shift_rows(carry, "seq", 1)

    def up_group(part):
        shape = (D // owners, FF)
        at = (0, part * Rounds.PARTS)
        columns = FF // COLUMNS // 2
        group("up", shape, at, (norm_own, norm_in), (1,), (up_grad, up_in), columns)

    up_group(0)
    for _ in range(hops - 1):
        passed = line.step(pass_on, carry, arrived, lengths, first)
        arrived = shift_rows(passed, "seq", 1)
    reduction.step()
    up_group(1)
    attn_low, grad_q, grad_k, grad_v, carry_back = line.step(
        attention_middle,
        lengths,
        first,
        cot,
        dense_weight,
        fq,
        fk,
        value,
        phi_q,
        rot_q,
        num,
        den,
        scores,
        arrived,
        tables,
        mix,
    )
    arrived_back = shift_rows(carry_back, "seq", -1)
    low_own, low_send = line.step(lambda *a: pick(a[:1], a[1]), attn_low, me)
    low_in = swap(low_send, 0)
    reduction.step()
    output = line.step(
        layer_output,
        attn_low,
        dense_weight,
        inputs_flat,
        mlp_out,
        dense_bias,
        down_bias,
    )
    for _ in range(hops - 1):
        passed = line.step(pass_on, carry_back, arrived_back, lengths, first)
        arrived_back = shift_rows(passed, "seq", -1)
    shape = (D // owners, D)
    group("dense", shape, (0, 0), (low_own, low_in), (0,), (cot, cot_in), across)
    qkv_grad, qkv_send = line.step(
        attention_last,
        lengths,
        first,
        grad_q,
        grad_k,
        grad_v,
        fk,
        value,
        phi_k,
        rot_k,
        arrived_back,
        tables,
        mix,
    )
    reduction.step()
    qkv_in = line.send(qkv_send, lambda a: swap(a, 0))
    input_grad, sums, qkv_sums = line.step(
        norm_back,
        qkv_grad,
        qkv_weight,
        mlp_norm_grad,
        unit,
        rate,
        cot,
        ln1_gain,
        ln2_gain,
    )

    def qkv_group(part):
        shape = (D // owners, 3 * D)
        at = (0, part * Rounds.PARTS)
        group("qkv", shape, at, (norm_own, norm_in), (0,), (qkv_grad, qkv_in), 2)

    qkv_group(0)
    reduction.step()
    qkv_group(1)
    vectors = Vectors(line, (sums, qkv_sums, up_sums))
    reduction.step()
    qkv_group(2)
    vectors.take()
    vectors.send()
    while not reduction.finished():
        reduction.step()
        vectors.take()
        vectors.send()
    totals = reduction.results()
    (
        attn_gain_total,
        attn_shift_total,
        mlp_gain_total,
        mlp_shift_total,
        bias_total,
        qkv_bias_total,
        up_bias_total,
    ) = vectors.results()

    return (
        output.reshape(inputs.shape),
        input_grad.reshape(inputs.shape),
        attn_gain_total,
        attn_shift_total,
        mlp_gain_total,
        mlp_shift_total,
        totals["qkv"],
        qkv_bias_total,
        totals["dense"],
        bias_total,
        totals["up"],
        up_bias_total,
        totals["down"],
        bias_total,
    )


def solution(mesh):
    placed = (
        P("batch", "seq", None),
        P("batch", None),
        P(),
        P(),
        P(),
        P(),
        P(),
        P(),
        P(),
        P(),
        P(),
        P(),
        P(),
        P(),
        P(),
        P(),
        P("batch", "seq", None),
    )
    return jax.shard_map(
        shards,
        mesh=mesh,
        in_specs=placed,
        out_specs=(
            P("batch", "seq", None),
            P("batch", "seq", None),
            P("batch"),
            P("batch"),
            P("batch"),
            P("batch"),
            P("batch", None),
            P("batch"),
            P("batch", None),
            P("batch"),
            P("batch", None),
            P("batch"),
            P("batch", None),
            P("batch"),
        ),
        check_vma=False,
    )
```

```python
import math
from functools import partial

import jax
import jax.numpy as jnp
import numpy as np
from jax import lax
from jax.experimental import pallas as pl
from jax.experimental.pallas import tpu as pltpu
from jax.sharding import PartitionSpec as P

D = 1024
HEADS = 16
HEAD = 64
ROT = 16
FF = 4096
PAIR = 2 * HEAD
BLOCK = 128
COLUMNS = 512

EPSILON = 1e-05
ROTARY_BASE = 10000.0

def lasting(microseconds):
    return pl.CostEstimate(
        flops=int(microseconds * 1.15e9), transcendentals=0, bytes_accessed=0
    )


ROWS_COLS = ((1,), (0,))
ROWS_ROWS = ((1,), (1,))
COLS_COLS = ((0,), (0,))
NARROW = jnp.bfloat16
WIDE = jnp.float32


def plain_dot(left, right, dims):
    return lax.dot_general(left, right, (dims, ((), ())), preferred_element_type=WIDE)


def whole_spec(shape):
    return pl.BlockSpec(shape, lambda *_: (0,) * len(shape))


def shift_rows(value, axis, by):
    count = lax.axis_size(axis)
    return lax.ppermute(
        value, axis, [(i, i + by) for i in range(count) if 0 <= i + by < count]
    )


def in_hbm(*values):
    return [
        pltpu.with_memory_space_constraint(v, pltpu.HBM)
        if v.size * v.dtype.itemsize >= 1 << 16
        else v
        for v in values
    ]


def swap(value, bit):
    count = lax.axis_size("batch")
    return lax.ppermute(value, "batch", [(i, i ^ (1 << bit)) for i in range(count)])


def owner_order(bits):
    return sorted(
        range(1 << len(bits)), key=lambda r: tuple(-((r >> bit) & 1) for bit in bits)
    )


def line_rounds(count):
    half = count // 2
    rounds = [("in", [(k, k + 1), (count - 1 - k, count - 2 - k)], k) for k in range(half - 1)]
    rounds.append(("in", [(half - 1, half), (half, half - 1)], -1))
    for k in range(half - 2, -1, -1):
        rounds.append(("out", [(k + 1, k), (count - 2 - k, count - 1 - k)], k))
    return rounds


class Line:
    def __init__(self):
        self.last = None

    def wait(self, *values):
        if self.last is not None:
            values, _ = lax.optimization_barrier((values, self.last))
        return values

    def send(self, value, how):
        return how(*self.wait(value))

    def step(self, function, *values):
        out = function(*self.wait(*values))
        self.last = jax.tree.leaves(out)[0]
        return out


def pack_kernel(order, sizes, count, me_ref, *refs):
    ins, out_ref = refs[:count], refs[-1]
    at, sizes = 0, list(sizes)
    for ref in ins:
        count = ref.shape[0]
        size, sizes = sizes[0], sizes[count:]
        for k, relative in enumerate(order):
            start = pl.multiple_of((relative ^ me_ref[0]) * size, BLOCK)
            block = ref[:, pl.ds(start, size)]
            for j in range(count):
                out_ref[k : k + 1, at + j * size : at + (j + 1) * size] = block[j : j + 1]
        at += count * size


def pack(order, sizes, arriving, me, *blocks):
    return pl.pallas_call(
        partial(pack_kernel, order, sizes, len(blocks)),
        in_specs=[pl.BlockSpec(memory_space=pltpu.SMEM)]
        + [pl.BlockSpec(memory_space=pltpu.VMEM)] * len(blocks)
        + [pl.BlockSpec(memory_space=pl.ANY)] * len(arriving),
        out_specs=pl.BlockSpec(memory_space=pltpu.VMEM),
        out_shape=jax.ShapeDtypeStruct((len(order), sum(sizes)), WIDE),
        name="pack_vectors",
    )(me, *blocks, *arriving)


class Vectors:
    def __init__(self, line, blocks, arriving):
        owners = lax.axis_size("batch")
        me = lax.axis_index("batch").astype(jnp.int32)
        self.line = line
        vectors = [v for block in blocks for v in block]
        self.sizes = [v.shape[0] // owners for v in vectors]
        bits = list(range(owners.bit_length() - 1))
        order = owner_order(bits)
        if any(size % BLOCK for size in self.sizes):
            pieces = jnp.concatenate([v.reshape(owners, -1) for v in vectors], axis=1)
            rows = [lax.dynamic_slice_in_dim(pieces, r ^ me, 1, 0) for r in order]
            self.held = jnp.concatenate(rows)
        else:
            self.held = line.step(
                lambda *a: pack(order, self.sizes, arriving, *a), me[None], *blocks
            )
        count = lax.axis_size("seq")
        self.steps = [("swap", bit, 0) for bit in bits]
        self.steps += line_rounds(count) if count % 2 == 0 else []
        self.moving = None
        self.now = None

    def send(self):
        if self.moving is not None or not self.steps:
            return
        self.now = kind, what, _ = self.steps.pop(0)
        if kind == "swap":
            half = self.held.shape[0] // 2
            self.moving = self.line.send(self.held[:half], lambda a: swap(a, what))
            self.held = self.held[half:]
        else:
            self.moving = self.line.send(self.held, lambda a: lax.ppermute(a, "seq", what))

    def take(self):
        if self.moving is None:
            return
        kind, _, at = self.now
        if kind == "out":
            place, count = lax.axis_index("seq"), lax.axis_size("seq")
            edge = (place == at) | (place == count - 1 - at)
            self.held = self.line.step(
                lambda a, b: jnp.where(edge, b, a), self.held, self.moving
            )
        else:
            self.held = self.line.step(lambda a, b: a + b, self.held, self.moving)
        self.moving = None

    def results(self):
        while self.moving is not None or self.steps:
            self.take()
            self.send()
        if lax.axis_size("seq") % 2 and lax.axis_size("seq") > 1:
            self.held = lax.psum(self.held, "seq")
        out, at = [], 0
        for size in self.sizes:
            out.append(self.held[0, at : at + size])
            at += size
        return out


class Reduction:
    def __init__(self, line, left, right, bits):
        self.line = line
        half = left.shape[1] // 2
        send = line.step(lambda a, b: plain_dot(a, b, COLS_COLS), left[:, :half], right)
        self.held = line.step(lambda a, b: plain_dot(a, b, COLS_COLS), left[:, half:], right)
        count = lax.axis_size("seq")
        self.steps = [("swap", bit + 1, 0) for bit in bits]
        self.steps += line_rounds(count) if count % 2 == 0 else []
        self.moving = swap(send, bits[0] + 1)

    def finish(self):
        place, count = lax.axis_index("seq"), lax.axis_size("seq")
        for i, (kind, _, at) in enumerate(self.steps):
            if kind == "out":
                edge = (place == at) | (place == count - 1 - at)
                self.held = self.line.step(
                    lambda a, b: jnp.where(edge, b, a), self.held, self.moving
                )
            else:
                self.held = self.line.step(lambda a, b: a + b, self.held, self.moving)
            if i + 1 == len(self.steps):
                break
            kind, what, _ = self.steps[i + 1]
            if kind == "swap":
                half = self.held.shape[0] // 2
                self.moving = swap(self.held[:half], what)
                self.held = self.held[half:]
            else:
                self.moving = lax.ppermute(self.held, "seq", what)
        return self.held if count % 2 == 0 or count == 1 else lax.psum(self.held, "seq")


class Singly:
    def __init__(self, line, bits):
        self.line, self.bits = line, bits
        self.pieces, self.outputs = [], {}

    def prepare(self, target, pieces, *arrived):
        _, _, at, size = target
        for left, left_in, block, right, right_in, (begin, each), (row, column) in pieces:
            wide = COLUMNS // Rounds.PARTS
            across = size[1] // wide
            starts = [((at[1] + i) * across + column) * wide for i in range(Rounds.PARTS)]
            starts_in = [(begin + i * each) * wide for i in range(Rounds.PARTS)]
            right, right_in = (
                jnp.concatenate([value[:, k : k + wide] for k in places], axis=1)
                for value, places in ((right, starts), (right_in, starts_in))
            )
            left = jnp.concatenate([left[block], rounded(left_in[block])], axis=0)
            right = jnp.concatenate([right, rounded(right_in)], axis=0)
            done = Reduction(self.line, left, right, self.bits)
            self.pieces.append((target, row, starts, wide, done))

    def step(self, *arrived):
        pass

    def arriving(self):
        return []

    def finished(self):
        return True

    def results(self):
        for (name, shape, at, size), row, starts, wide, piece in self.pieces:
            whole = self.outputs.get(name, jnp.zeros(shape, WIDE))
            total = piece.finish()
            top = at[0] * size[0] + row * total.shape[0]
            for i, k in enumerate(starts):
                whole = lax.dynamic_update_slice(
                    whole, total[:, i * wide : (i + 1) * wide], (top, k)
                )
            self.outputs[name] = whole
        return self.outputs


def rounded(arrived):
    one = jnp.where(lax.axis_index("seq") < lax.axis_size("seq"), 1.0, 0.5)
    return (arrived * one).astype(NARROW)


def product_kernel(count, *refs):
    ins, (to_x, to_y, hold_a, hold_b) = refs[: 8 * count], refs[-4:]
    for p in range(count):
        for i, (to, hold) in enumerate(((to_x, hold_a), (to_y, hold_b))):
            left, left_in, right, right_in = ins[8 * p + 4 * i : 8 * p + 4 * i + 4]
            whole = jnp.concatenate([left[0], left_in[0].astype(NARROW)], axis=0)
            right = jnp.concatenate([right[...], right_in[...].astype(NARROW)], axis=0)

            def product(first, second):
                rows = [whole[:, k * BLOCK : (k + 1) * BLOCK] for k in (first, second)]
                return plain_dot(jnp.concatenate(rows, axis=1), right, COLS_COLS)

            out = pl.ds(p * 2 * BLOCK, 2 * BLOCK)
            to[out, :] = product(0, 1 if i else 2)
            hold[out, :] = product(2 if i else 1, 3)


def round_kernel(counts, places, skip, *refs):
    first, second, inward, middle, outward = counts
    refs = list(refs)
    edge = refs.pop(0)[0] != 0

    def take(flag, count):
        return [refs.pop(0) for _ in range(count)] if flag else [None] * count

    from_x, from_y = take(first or second, 2)
    hold_a, hold_b = take(first, 2)
    kept_a, kept_b = take(second, 2)
    (sums,) = take(inward, 1)
    (from_end,) = take(inward or outward, 1)
    inner, from_middle = take(middle, 2)
    (whole,) = take(outward, 1)
    take(True, skip)
    to_x, to_y, keep_a, keep_b = take(first, 4)
    (new_sums,) = take(second, 1)
    (to_end,) = take(second or middle, 1)
    (new_inner,) = take(inward, 1)
    (final,) = take(outward, 1)
    for p in range(first):
        low = pl.ds(2 * p * BLOCK, BLOCK)
        high = pl.ds((2 * p + 1) * BLOCK, BLOCK)
        out = pl.ds(p * BLOCK, BLOCK)
        to_y[out, :] = hold_a[low, :] + from_x[low, :]
        to_x[out, :] = hold_b[low, :] + from_y[low, :]
        keep_a[out, :] = hold_a[high, :] + from_x[high, :]
        keep_b[out, :] = hold_b[high, :] + from_y[high, :]
    for p in range(max(second, middle)):
        for i, (kept, arrived) in enumerate(((kept_a, from_y), (kept_b, from_x))):
            out = pl.ds((2 * p + i) * BLOCK, BLOCK)
            ends = inners = None
            if p < second:
                come = pl.ds((2 * first + p) * BLOCK, BLOCK)
                ends = kept[pl.ds(p * BLOCK, BLOCK), :] + arrived[come, :]
                new_sums[out, :] = ends
            if p < middle:
                inners = inner[out, :] + from_middle[out, :]
            if ends is None:
                to_end[out, :] = inners
            elif inners is None:
                to_end[out, :] = ends
            else:
                to_end[out, :] = jnp.where(edge, ends, inners)
    if inward:
        new_inner[...] = sums[...] + from_end[: 2 * inward * BLOCK, :]
    for k, (row, column) in enumerate(places):
        rows = pl.ds(k * BLOCK, BLOCK)
        wide = final.shape[1] // (1 + max(column for _, column in places))
        total = jnp.where(edge, from_end[rows, :], whole[rows, :])
        final[row * BLOCK : (row + 1) * BLOCK, column * wide : (column + 1) * wide] = total


class Rounds:
    PARTS = 2

    def __init__(self, line, edge, counts):
        self.line, self.edge, self.counts = line, edge, counts
        self.made = self.at = 0
        self.buffers, self.moving, self.hold, self.kept = {}, {}, {}, {}
        self.sums, self.inner, self.whole, self.targets = {}, {}, None, []
        self.outputs = {}
        self.end = self.middle = None
        self.wide = COLUMNS // self.PARTS

    def count(self, group):
        return self.counts[group] if 0 <= group < len(self.counts) else 0

    def place(self, value, local, sent):
        if local:
            return pltpu.with_memory_space_constraint(value, pltpu.HBM)
        return pltpu.with_memory_space_constraint(value, pltpu.HBM) if sent else value

    def rows_spec(self, rows, at=0):
        return pl.BlockSpec((rows, self.wide), lambda i: (at, i))

    def prepare(self, target, pieces, *arrived):
        r = self.made
        self.made += 1
        self.targets.append((target, [piece[-1] for piece in pieces]))
        count = len(pieces) // 2
        name, shape, at, size = target
        across = size[1] // self.wide
        args, specs = [], []
        for left, left_in, block, right, right_in, (begin, each), (_, column) in pieces:
            for value in (left, left_in):
                args += in_hbm(value) if value is left else [value]
                specs.append(
                    pl.BlockSpec((1, *value.shape[1:]), lambda i, block=block: (block, 0, 0))
                )
            mine = (at[1] * across + column, across)
            for value, (begin, each) in ((right, mine), (right_in, (begin, each))):
                args += in_hbm(value) if value is right else [value]
                specs.append(
                    pl.BlockSpec(
                        (value.shape[0], self.wide),
                        lambda i, begin=begin, each=each: (0, begin + i * each),
                    )
                )
        args += arrived
        specs += [pl.BlockSpec(memory_space=pl.ANY)] * len(arrived)
        rows = 2 * count * BLOCK
        total = rows + self.count(r - 1) * BLOCK
        call = pl.pallas_call(
            partial(product_kernel, count),
            grid=(self.PARTS,),
            in_specs=specs,
            out_specs=[self.rows_spec(rows)] * 4,
            out_shape=[pltpu.HBM((total, COLUMNS), WIDE)] * 2
            + [pltpu.HBM((rows, COLUMNS), WIDE)] * 2,
            cost_estimate=lasting(5),
        compiler_params=pltpu.CompilerParams(vmem_limit_bytes=25165824),
        name="piece_products",
        )
        to_x, to_y, hold_a, hold_b = self.line.step(call, *args)
        self.hold[r] = (hold_a, hold_b)
        if r:
            self.buffers[r] = (to_x, to_y)
        else:
            self.moving[r] = (swap(to_x, 1), swap(to_y, 2))

    def step(self, *arrived):
        r = self.at
        self.at += 1
        counts = [self.count(r - back) for back in (0, 1, 2, 3, 4)]
        first, second, inward, middle, outward = counts
        aliases = {}
        args, specs = [self.edge], [pl.BlockSpec(memory_space=pltpu.SMEM)]

        def add(value, local=False, sent=False):
            args.append(self.place(value, local, sent))
            specs.append(self.rows_spec(value.shape[0]))

        if first or second:
            for value in self.moving.pop(r):
                add(value)
        if first:
            for value in self.hold.pop(r):
                add(value, local=True)
        if second:
            for value in self.kept.pop(r - 1):
                add(value, local=True)
        if inward:
            add(self.sums.pop(r - 2), local=True)
        if inward or outward:
            add(self.end)
        if middle:
            add(self.inner.pop(r - 3), sent=True)
            add(self.middle)
        if outward:
            add(self.whole, sent=True)
        outs, out_specs = [], []

        def out(rows, at=0, of=None, sent=False):
            kind = pltpu.HBM if sent else pltpu.HBM
            outs.append(kind((of or rows, COLUMNS), WIDE))
            out_specs.append(self.rows_spec(rows, at))

        ahead = self.count(r + 1)
        if ahead:
            aliases = {len(args): 0, len(args) + 1: 1}
            args += list(self.buffers.pop(r + 1))
            specs += [pl.BlockSpec(memory_space=pl.ANY)] * 2
        if first:
            for _ in range(2):
                out(first * BLOCK, 2 * ahead // first, (2 * ahead + first) * BLOCK, sent=True)
            out(first * BLOCK)
            out(first * BLOCK)
        if second:
            out(2 * second * BLOCK)
        if second or middle:
            out(2 * max(second, middle) * BLOCK, sent=True)
        if inward:
            out(2 * inward * BLOCK, sent=True)
        places = ()
        if outward:
            (name, shape, at, size), places = self.targets[r - 4]
            if name in self.outputs:
                aliases[len(args)] = len(outs)
                args.append(self.outputs[name])
                specs.append(pl.BlockSpec(memory_space=pl.ANY))
            outs.append(pltpu.HBM(shape, WIDE))
            out_specs.append(pl.BlockSpec(size, lambda i: (at[0], at[1] + i)))
        args += arrived
        specs += [pl.BlockSpec(memory_space=pl.ANY)] * len(arrived)
        call = pl.pallas_call(
            partial(round_kernel, counts, places, len(aliases) + len(arrived)),
            grid=(self.PARTS,),
            in_specs=specs,
            out_specs=out_specs,
            out_shape=outs,
            input_output_aliases=aliases,
            cost_estimate=lasting(5.0),
            compiler_params=pltpu.CompilerParams(vmem_limit_bytes=25165824),
            name="reduce_round",
        )
        got = list(self.line.step(call, *args))
        if first:
            self.moving[r + 1] = (swap(got.pop(0), 1), swap(got.pop(0), 2))
            self.kept[r] = (got.pop(0), got.pop(0))
        if second:
            self.sums[r - 1] = got.pop(0)
        self.whole = None
        if second or middle:
            self.whole = got.pop(0)
            self.end = lax.ppermute(self.whole, "seq", [(0, 1), (1, 0), (2, 3), (3, 2)])
        if inward:
            self.inner[r - 2] = got.pop(0)
            self.middle = lax.ppermute(self.inner[r - 2], "seq", [(1, 2), (2, 1)])
        if outward:
            self.outputs[name] = got.pop(0)

    def arriving(self):
        return [*self.moving[self.at], self.end, self.middle]

    def finished(self):
        return self.at == len(self.counts) + 4

    def results(self):
        return self.outputs


def settle_kernel(*refs):
    refs[-1][...] = jnp.zeros_like(refs[-1])


def settle(arriving):
    return pl.pallas_call(
        settle_kernel,
        in_specs=[pl.BlockSpec(memory_space=pl.ANY)] * len(arriving),
        out_specs=pl.BlockSpec(memory_space=pltpu.VMEM),
        out_shape=jax.ShapeDtypeStruct((8, 128), WIDE),
        cost_estimate=lasting(12),
        name="settle",
    )(*arriving)


def pick_kernel(me_ref, *refs):
    ins, (keep_ref, send_ref) = refs[:-2], refs[-2:]
    half = keep_ref.shape[2] // BLOCK
    for i, ref in enumerate(ins):
        for p in range(half):
            for core in range(2):
                owner = (2 * (half - 1 - p) + core) ^ me_ref[0]
                columns = ref[:, pl.ds(pl.multiple_of(owner * BLOCK, BLOCK), BLOCK)]
                at = slice(p * BLOCK, (p + 1) * BLOCK)
                if core:
                    send_ref[i, :, at] = columns.astype(WIDE)
                else:
                    keep_ref[i, :, at] = columns


def pick(arrays, me):
    owners = lax.axis_size("batch")
    half = owners // 2
    tokens, features = arrays[0].shape
    size = features // owners
    if size != BLOCK:

        def columns(value, core):
            return jnp.concatenate(
                [
                    lax.dynamic_slice_in_dim(value, ((2 * r + core) ^ me[0]) * size, size, 1)
                    for r in range(half)[::-1]
                ],
                axis=1,
            )

        return (
            jnp.stack([columns(a, 0) for a in arrays]),
            jnp.stack([columns(a, 1) for a in arrays]).astype(WIDE),
        )
    shape = (len(arrays), tokens, half * size)
    return pl.pallas_call(
        pick_kernel,
        in_specs=[pl.BlockSpec(memory_space=pltpu.SMEM)]
        + [pl.BlockSpec(memory_space=pltpu.VMEM)] * len(arrays),
        out_specs=[pl.BlockSpec(memory_space=pltpu.VMEM)] * 2,
        out_shape=[pltpu.HBM(shape, NARROW), pltpu.HBM(shape, WIDE)],
        cost_estimate=lasting(2.0),
        name="pick_columns",
    )(*in_hbm(me, *arrays))


def as_row(ref):
    return ref[...].astype(WIDE)[None, :]


def norm_kernel(x_ref, gain1, bias1, gain2, bias2, attn_ref, mlp_ref, unit_ref, rate_ref):
    x = x_ref[...].astype(WIDE)
    centered = x - jnp.mean(x, axis=-1, keepdims=True)
    rate = lax.rsqrt(jnp.mean(centered * centered, axis=-1, keepdims=True) + EPSILON)
    unit = centered * rate
    unit_ref[...] = unit
    rate_ref[...] = jnp.broadcast_to(rate, rate_ref.shape)
    for gain, bias, out in ((gain1, bias1, attn_ref), (gain2, bias2, mlp_ref)):
        out[...] = (unit * as_row(gain) + as_row(bias)).astype(NARROW)


def two_norms(inputs, *gains):
    tokens = inputs.shape[0]
    rows = tokens // 4
    by_rows = pl.BlockSpec((rows, D), lambda i: (i, 0))
    return pl.pallas_call(
        norm_kernel,
        grid=(4,),
        in_specs=[by_rows] + [whole_spec((D,))] * len(gains),
        out_specs=[by_rows, by_rows, by_rows, pl.BlockSpec((rows, 128), lambda i: (i, 0))],
        out_shape=[
            pltpu.HBM((tokens, D), NARROW),
            pltpu.HBM((tokens, D), NARROW),
            pltpu.HBM((tokens, D), WIDE),
            pltpu.HBM((tokens, 128), WIDE),
        ],
        cost_estimate=lasting(4.0),
        name="two_norms",
    )(*in_hbm(inputs, *gains))


def up_kernel(
    half, me_ref, x_ref, weight_ref, bias_ref, act_ref, slope_ref, keep_ref, send_ref
):
    step = pl.program_id(0)
    up = plain_dot(x_ref[...], weight_ref[...], ROWS_COLS) + as_row(bias_ref)
    below = 0.5 * (1.0 + lax.erf(up * (0.5**0.5)))
    act = (up * below).astype(NARROW)
    act_ref[...] = act
    slope_ref[...] = below + up * jnp.exp(-0.5 * up * up) * ((2.0 * math.pi) ** -0.5)

    @pl.when(step < half)
    def _():
        for i in range(keep_ref.shape[0]):
            keep_ref[i] = act[:, i * BLOCK : (i + 1) * BLOCK]

    @pl.when(step >= half)
    def _():
        wide = act.astype(WIDE)
        for i in range(send_ref.shape[0]):
            send_ref[i] = wide[:, i * BLOCK : (i + 1) * BLOCK]


def mlp_up(mlp_in, up_weight, up_bias, me):
    owners = lax.axis_size("batch")
    tokens = mlp_in.shape[0]
    half = owners // 2
    each = FF // owners
    subs = each // BLOCK

    def natural(i, me):
        return (0, (2 * (i % half) + i // half) ^ me[0])

    return pl.pallas_call(
        partial(up_kernel, half),
        grid_spec=pltpu.PrefetchScalarGridSpec(
            num_scalar_prefetch=1,
            grid=(owners,),
            in_specs=[
                pl.BlockSpec((tokens, D), lambda i, me: (0, 0)),
                pl.BlockSpec((D, each), natural),
                pl.BlockSpec((each,), lambda i, me: natural(i, me)[1:]),
            ],
            out_specs=[
                pl.BlockSpec((tokens, each), natural),
                pl.BlockSpec((tokens, each), natural),
                pl.BlockSpec(
                    (subs, tokens, BLOCK),
                    lambda i, me: (0, 0, half - 1 - jnp.minimum(i, half - 1)),
                ),
                pl.BlockSpec(
                    (subs, tokens, BLOCK),
                    lambda i, me: (0, 0, half - 1 - jnp.maximum(i - half, 0)),
                ),
            ],
        ),
        out_shape=[
            pltpu.HBM((tokens, FF), NARROW),
            pltpu.HBM((tokens, FF), WIDE),
            pltpu.HBM((subs, tokens, half * BLOCK), NARROW),
            pltpu.HBM((subs, tokens, half * BLOCK), WIDE),
        ],
        cost_estimate=lasting(11.0),
        name="mlp_up",
    )(*in_hbm(me, mlp_in, up_weight, up_bias))


def back_kernel(
    cot_ref, down_ref, up_ref, act_ref, slope_ref, grad_ref, send_ref, sums_ref, out_ref, norm_ref
):
    step = pl.program_id(0)
    down = down_ref[...]
    grad = plain_dot(cot_ref[...], down, ROWS_ROWS) * slope_ref[...]
    grad = grad.astype(NARROW)
    grad_ref[...] = grad
    wide = grad.astype(WIDE)
    send_ref[...] = wide
    sums_ref[...] = jnp.sum(wide, axis=0, keepdims=True)
    out = plain_dot(act_ref[...], down, ROWS_COLS)
    norm = plain_dot(grad, up_ref[...], ROWS_ROWS)

    @pl.when(step == 0)
    def _():
        out_ref[...] = out
        norm_ref[...] = norm

    @pl.when(step > 0)
    def _():
        out_ref[...] += out
        norm_ref[...] += norm


def mlp_back(cot, down_weight, up_weight, act, slope):
    tokens = cot.shape[0]
    each = 1024
    by_column = pl.BlockSpec((tokens, each), lambda i: (0, i))
    total = whole_spec((tokens, D))
    return pl.pallas_call(
        back_kernel,
        grid=(FF // each,),
        in_specs=[
            total,
            pl.BlockSpec((each, D), lambda i: (i, 0)),
            pl.BlockSpec((D, each), lambda i: (0, i)),
            by_column,
            by_column,
        ],
        out_specs=[
            by_column,
            by_column,
            pl.BlockSpec((1, each), lambda i: (0, i)),
            total,
            total,
        ],
        out_shape=[
            pltpu.HBM((tokens, FF), NARROW),
            pltpu.HBM((tokens, FF), WIDE),
            pltpu.HBM((1, FF), WIDE),
            pltpu.HBM((tokens, D), WIDE),
            pltpu.HBM((tokens, D), WIDE),
        ],
        cost_estimate=lasting(16.0),
        compiler_params=pltpu.CompilerParams(vmem_limit_bytes=25165824),
        name="mlp_back",
    )(*in_hbm(cot, down_weight, up_weight, act, slope))


def output_kernel(low_ref, weight_ref, x_ref, mlp_ref, dense_ref, down_ref, out_ref):
    attn = plain_dot(low_ref[...], weight_ref[...], ROWS_COLS) + as_row(dense_ref)
    mlp = mlp_ref[...] + as_row(down_ref)
    out_ref[...] = (x_ref[...].astype(WIDE) + attn + mlp).astype(NARROW)


def layer_output(low, dense_weight, inputs, mlp_out, *biases):
    tokens = inputs.shape[0]
    each = 512
    by_column = pl.BlockSpec((tokens, each), lambda i: (0, i))
    return pl.pallas_call(
        output_kernel,
        grid=(D // each,),
        in_specs=[
            whole_spec((tokens, D)),
            pl.BlockSpec((D, each), lambda i: (0, i)),
            by_column,
            by_column,
        ]
        + [pl.BlockSpec((each,), lambda i: (i,))] * len(biases),
        out_specs=by_column,
        out_shape=pltpu.HBM((tokens, D), NARROW),
        cost_estimate=lasting(3.0),
        name="layer_output",
    )(*in_hbm(low, dense_weight, inputs, mlp_out, *biases))


def norm_back_kernel(
    qkv_ref,
    weight_ref,
    mlp_ref,
    unit_ref,
    rate_ref,
    cot_ref,
    gain1,
    gain2,
    grad_ref,
    sums_ref,
    qkv_sums,
):
    step = pl.program_id(0)
    qkv = qkv_ref[...]
    qkv_sums[...] = jnp.sum(qkv.astype(WIDE), axis=0, keepdims=True)
    part = plain_dot(qkv, weight_ref[...], ROWS_ROWS)

    @pl.when(step == 0)
    def _():
        grad_ref[...] = part

    @pl.when(step > 0)
    def _():
        grad_ref[...] += part

    @pl.when(step == pl.num_programs(0) - 1)
    def _():
        size = 64
        gain_attn, gain_mlp = as_row(gain1), as_row(gain2)
        totals = [jnp.zeros((1, D), WIDE)] * 5
        for k in range(grad_ref.shape[0] // size):
            rows = pl.ds(k * size, size)
            attn, mlp, unit = grad_ref[rows, :], mlp_ref[rows, :], unit_ref[rows, :]
            cot = cot_ref[rows, :].astype(WIDE)
            together = attn * gain_attn + mlp * gain_mlp
            grad_ref[rows, :] = cot + rate_ref[rows, 0:1] * (
                together
                - jnp.mean(together, axis=-1, keepdims=True)
                - unit * jnp.mean(together * unit, axis=-1, keepdims=True)
            )
            for i, value in enumerate((attn * unit, attn, mlp * unit, mlp, cot)):
                totals[i] = totals[i] + jnp.sum(value, axis=0, keepdims=True)
        for i, value in enumerate(totals):
            sums_ref[i : i + 1, :] = value


def norm_back(qkv_grad, qkv_weight, mlp_norm_grad, unit, rate, cot, *gains):
    tokens = cot.shape[0]
    each = 512
    total = whole_spec((tokens, D))
    return pl.pallas_call(
        norm_back_kernel,
        grid=(3 * D // each,),
        in_specs=[
            pl.BlockSpec((tokens, each), lambda i: (0, i)),
            pl.BlockSpec((D, each), lambda i: (0, i)),
            total,
            total,
            whole_spec(rate.shape),
            total,
        ]
        + [whole_spec((D,))] * len(gains),
        out_specs=[total, whole_spec((5, D)), pl.BlockSpec((1, each), lambda i: (0, i))],
        out_shape=[
            pltpu.HBM((tokens, D), WIDE),
            pltpu.HBM((5, D), WIDE),
            pltpu.HBM((1, 3 * D), WIDE),
        ],
        compiler_params=pltpu.CompilerParams(vmem_limit_bytes=25165824),
        name="norm_back",
    )(*in_hbm(qkv_grad, qkv_weight, mlp_norm_grad, unit, rate, cot, *gains))


def dct_matrix():
    rows = np.arange(HEAD)[:, None]
    columns = np.arange(HEAD)[None, :]
    cosines = np.cos(np.pi * (columns + 0.5) * rows / HEAD) * np.sqrt(2.0 / HEAD)
    return np.where(rows == 0, cosines * np.sqrt(0.5), cosines).astype(np.float32)


def attention_tables(place, context, count):
    half_rot = ROT // 2
    lane = np.arange(PAIR) % HEAD
    freq = ROTARY_BASE ** (-2.0 * (lane % half_rot) / ROT)
    angles = np.arange(count * context)[:, None] * freq[None, :]
    tables = np.stack(
        [
            np.where(lane < ROT, np.cos(angles), 1.0),
            np.where(lane < half_rot, -np.sin(angles), 0.0),
            np.where((lane >= half_rot) & (lane < ROT), np.sin(angles), 0.0),
        ]
    )
    return lax.dynamic_slice_in_dim(
        jnp.asarray(tables.astype(np.float32)), place * context, context, 1
    )


def lane_is_low(shape):
    return lax.broadcasted_iota(jnp.int32, shape, len(shape) - 1) % PAIR < HEAD


def halves(full):
    return jnp.where(lane_is_low((HEAD, PAIR)), full[:HEAD], full[HEAD:])


def spread_pair(block):
    low = lane_is_low(block.shape)
    zero = jnp.zeros_like(block)
    return jnp.concatenate([jnp.where(low, block, zero), jnp.where(low, zero, block)], axis=0)


def one_head(tile, head):
    low = lane_is_low(tile.shape)
    zero = jnp.zeros_like(tile)
    return jnp.where(low, tile, zero) if head == 0 else jnp.where(low, zero, tile)


def in_two(value):
    high = value.astype(NARROW)
    return high, (value - high.astype(WIDE)).astype(NARROW)


def fine_dot(left, right, dims):
    left_high, left_low = in_two(left)
    right_high, right_low = in_two(right)
    return (
        plain_dot(left_high, right_high, dims)
        + plain_dot(left_low, right_high, dims)
        + plain_dot(left_high, right_low, dims)
    )


def head_sums(tile):
    rows = lax.broadcasted_iota(jnp.int32, (PAIR, PAIR), 0) // HEAD
    columns = lax.broadcasted_iota(jnp.int32, (PAIR, PAIR), 1) // HEAD
    ones = (rows == columns).astype(WIDE).astype(NARROW)
    high, low = in_two(tile)
    return plain_dot(
        jnp.concatenate([high, low], axis=1), jnp.concatenate([ones, ones], axis=0), ROWS_COLS
    )


def turn(tile, cos, sin_up, sin_down):
    half_rot = ROT // 2
    return (
        tile * cos
        + pltpu.roll(tile, PAIR - half_rot, 1) * sin_up
        + pltpu.roll(tile, half_rot, 1) * sin_down
    )


def turn_back(tile, cos, sin_up, sin_down):
    half_rot = ROT // 2
    return (
        tile * cos
        + pltpu.roll(tile * sin_up, half_rot, 1)
        + pltpu.roll(tile * sin_down, PAIR - half_rot, 1)
    )


def all_rows(tables_ref, seqs):
    return [jnp.concatenate([tables_ref[k]] * seqs, axis=0) for k in range(3)]


def feature_grad(grad, phi, turned, mix, tables):
    weighted = grad * phi
    back = fine_dot(weighted, mix, ROWS_ROWS) - (HEAD**-0.5) * turned * head_sums(weighted)
    return turn_back(back, *tables)


def doc_at(where, lengths_ref, b):
    start, found = 0, jnp.zeros_like(where) - 1
    for k in range(lengths_ref.shape[1]):
        found = found + jnp.where(start <= where, 1, 0)
        start = start + lengths_ref[b, k]
    return found


def same_doc_before(lengths_ref, b, first, context):
    query = first + lax.broadcasted_iota(jnp.int32, (context, context), 0)
    key = first + lax.broadcasted_iota(jnp.int32, (context, context), 1)
    same = doc_at(query, lengths_ref, b) == doc_at(key, lengths_ref, b)
    return jnp.where(same & (key <= query), 1.0, 0.0)


def in_doc_of(lengths_ref, b, first, context, where):
    rows = first + lax.broadcasted_iota(jnp.int32, (context, PAIR), 0)
    return jnp.where(doc_at(rows, lengths_ref, b) == doc_at(where, lengths_ref, b), 1.0, 0.0)


def local_kernel(
    seqs,
    lengths_ref,
    first_ref,
    attn_ref,
    weight_ref,
    bias_ref,
    tables_ref,
    dct_ref,
    points_ref,
    weights_ref,
    fq_ref,
    fk_ref,
    val_ref,
    phiq_ref,
    phik_ref,
    rotq_ref,
    rotk_ref,
    num_ref,
    den_ref,
    score_ref,
    carry_ref,
    mix_ref,
):
    context = tables_ref.shape[1]
    first = first_ref[0]

    @pl.when(pl.program_id(0) == 0)
    def _():
        both = lax.dot_general(
            dct_ref[...],
            points_ref[...],
            (COLS_COLS, ((), ())),
            precision=lax.Precision.HIGHEST,
            preferred_element_type=WIDE,
        )
        mix_ref[...] = spread_pair(jnp.concatenate([both, both], axis=1) * HEAD ** (-0.25))

    mix = mix_ref[...]
    weights = as_row(weights_ref)
    wrow = jnp.concatenate([weights, weights], axis=1)
    tables = all_rows(tables_ref, seqs)
    low = lane_is_low((seqs * context, PAIR))
    block = plain_dot(attn_ref[...], weight_ref[...], ROWS_COLS) + bias_ref[...]
    one, two, three = block[:, :PAIR], block[:, PAIR : 2 * PAIR], block[:, 2 * PAIR :]
    query = jnp.where(low, one, two)
    key = pltpu.roll(jnp.where(low, three, one), HEAD, 1)
    value_all = jnp.where(low, two, three).astype(NARROW)
    val_ref[...] = value_all

    def features(raw):
        turned = turn(raw, *tables)
        power = fine_dot(turned, mix, ROWS_COLS) - (0.5 * HEAD**-0.5) * head_sums(turned * turned)
        return turned, wrow * jnp.exp(power)

    turned_q, phi_q = features(query)
    turned_k, phi_k = features(key)
    rotq_ref[...], rotk_ref[...] = turned_q, turned_k
    phiq_ref[...], phik_ref[...] = phi_q, phi_k
    fq_all, fk_all = phi_q.astype(NARROW), phi_k.astype(NARROW)
    fq_ref[...], fk_ref[...] = fq_all, fk_all
    low = lane_is_low((context, PAIR))
    for b in range(seqs):
        rows = slice(b * context, (b + 1) * context)
        fq, fk, value = fq_all[rows], fk_all[rows], value_all[rows]
        mask = same_doc_before(lengths_ref, b, first, context)
        keep = in_doc_of(lengths_ref, b, first, context, first + context - 1)
        wide_value = jnp.concatenate([value, jnp.ones_like(value)], axis=1)
        sums = []
        for h in range(2):
            scores = (plain_dot(one_head(fq, h), fk, ROWS_ROWS) * mask).astype(NARROW)
            score_ref[0, b, h] = scores
            sums.append(plain_dot(scores, wide_value, ROWS_COLS))
        num_ref[rows, :] = jnp.where(low, sums[0][:, :PAIR], sums[1][:, :PAIR])
        den_ref[rows, :] = jnp.where(low, sums[0][:, PAIR:], sums[1][:, PAIR:])
        kept = fk * keep.astype(NARROW)
        carry_ref[b, 0, :HEAD, :] = halves(plain_dot(kept, value, COLS_COLS))
        norm = jnp.sum(kept.astype(WIDE), axis=0, keepdims=True)
        carry_ref[b, 0, HEAD:, :] = jnp.broadcast_to(norm, (8, PAIR))


def middle_kernel(
    seqs,
    lengths_ref,
    first_ref,
    cot_ref,
    dense_ref,
    fq_ref,
    fk_ref,
    val_ref,
    phiq_ref,
    rotq_ref,
    num_ref,
    den_ref,
    score_ref,
    carry_ref,
    tables_ref,
    mix_ref,
    low_ref,
    gradq_ref,
    gradk_ref,
    gradv_ref,
    out_ref,
):
    context = tables_ref.shape[1]
    first = first_ref[0]
    mix = mix_ref[...]
    tables = all_rows(tables_ref, seqs)
    low = lane_is_low((context, PAIR))
    back_all = plain_dot(cot_ref[...], dense_ref[...], ROWS_ROWS)
    grads_q = []
    for b in range(seqs):
        rows = pl.ds(b * context, context)
        fq, fk, value = fq_ref[rows, :], fk_ref[rows, :], val_ref[rows, :]
        use = in_doc_of(lengths_ref, b, first, context, first - 1)
        state = spread_pair(carry_ref[b, 0, :HEAD, :].astype(NARROW))
        norm = carry_ref[b, 0, HEAD : HEAD + 1, :]
        wide_fq = fq.astype(WIDE)
        num = num_ref[rows, :] + use * plain_dot(fq, state, ROWS_COLS)
        den = den_ref[rows, :] + use * head_sums(wide_fq * norm)
        heads_out = num / den
        low_ref[rows, :] = heads_out.astype(NARROW)
        back = back_all[b * context : (b + 1) * context]
        num_grad = (back / den).astype(NARROW)
        den_grad = -head_sums(back * heads_out) / den
        mask = same_doc_before(lengths_ref, b, first, context)
        parts_q, parts_k, parts_v = [], [], []
        for h in range(2):
            column = den_grad[:, h * HEAD : h * HEAD + 1]
            score_grad = plain_dot(one_head(num_grad, h), value, ROWS_ROWS) + column
            score_grad = (score_grad * mask).astype(NARROW)
            parts_q.append(plain_dot(score_grad, fk, ROWS_COLS))
            parts_k.append(plain_dot(score_grad, fq, COLS_COLS))
            parts_v.append(plain_dot(score_ref[0, b, h], num_grad, COLS_COLS))
        gradk_ref[rows, :] = jnp.where(low, parts_k[0], parts_k[1])
        gradv_ref[rows, :] = jnp.where(low, parts_v[0], parts_v[1])
        num_used = num_grad * use.astype(NARROW)
        den_used = den_grad * use
        grads_q.append(
            jnp.where(low, parts_q[0], parts_q[1])
            + plain_dot(num_used, state, ROWS_ROWS)
            + den_used * norm
        )
        out_ref[b, 0, :HEAD, :] = halves(plain_dot(fq, num_used, COLS_COLS))
        norm_grad = jnp.sum(den_used * wide_fq, axis=0, keepdims=True)
        out_ref[b, 0, HEAD:, :] = jnp.broadcast_to(norm_grad, (8, PAIR))
    gradq_ref[...] = feature_grad(
        jnp.concatenate(grads_q, axis=0), phiq_ref[...], rotq_ref[...], mix, tables
    ).astype(NARROW)


def last_kernel(
    seqs,
    lengths_ref,
    first_ref,
    gradq_ref,
    gradk_ref,
    gradv_ref,
    fk_ref,
    val_ref,
    phik_ref,
    rotk_ref,
    carry_ref,
    tables_ref,
    mix_ref,
    out_ref,
    *send_refs,
):
    context = tables_ref.shape[1]
    first = first_ref[0]
    tables = all_rows(tables_ref, seqs)
    grads_k, grads_v = [], []
    for b in range(seqs):
        rows = pl.ds(b * context, context)
        keep = in_doc_of(lengths_ref, b, first, context, first + context - 1)
        state = spread_pair(carry_ref[b, 0, :HEAD, :].astype(NARROW))
        norm = carry_ref[b, 0, HEAD : HEAD + 1, :]
        grads_k.append(
            gradk_ref[rows, :] + keep * (plain_dot(val_ref[rows, :], state, ROWS_ROWS) + norm)
        )
        grads_v.append(gradv_ref[rows, :] + keep * plain_dot(fk_ref[rows, :], state, ROWS_COLS))
    grad_k = feature_grad(
        jnp.concatenate(grads_k, axis=0), phik_ref[...], rotk_ref[...], mix_ref[...], tables
    )
    grad_k = pltpu.roll(grad_k, HEAD, 1)
    grad_v = jnp.concatenate(grads_v, axis=0)
    grad_q = gradq_ref[...].astype(WIDE)
    low = lane_is_low(grad_q.shape)
    grad = jnp.concatenate(
        [
            jnp.where(low, grad_q, grad_k),
            jnp.where(low, grad_v, grad_q),
            jnp.where(low, grad_k, grad_v),
        ],
        axis=1,
    ).astype(NARROW)
    out_ref[...] = grad
    wide = grad.astype(WIDE)
    for step in range(HEADS // 2):

        @pl.when(pl.program_id(0) == step)
        def _(step=step):
            for k in range(3):
                at = (3 * step + k) * PAIR
                ref, at = (send_refs[0], at) if at < D else (send_refs[1], at - D)
                ref[:, at : at + PAIR] = wide[:, k * PAIR : (k + 1) * PAIR]


def pass_kernel(lengths_ref, first_ref, own_ref, arrived_ref, out_ref):
    context = first_ref[1]
    for b in range(own_ref.shape[0]):
        last = doc_at(first_ref[0] + context - 1, lengths_ref, b)
        through = last == doc_at(first_ref[0] - 1, lengths_ref, b)
        out_ref[b] = own_ref[b] + jnp.where(through, arrived_ref[b], 0.0)


SMEM_SPEC = pl.BlockSpec(memory_space=pltpu.SMEM)


def pass_on(own, arrived, lengths, first):
    seqs, pairs = own.shape[:2]
    spec = pl.BlockSpec((seqs, pairs // 2, *own.shape[2:]), lambda i: (0, i, 0, 0))
    return pl.pallas_call(
        pass_kernel,
        grid=(2,),
        in_specs=[SMEM_SPEC, SMEM_SPEC, spec, spec],
        out_specs=spec,
        out_shape=pltpu.HBM(own.shape, WIDE),
        cost_estimate=lasting(2.0),
        name="pass_carry",
    )(*in_hbm(lengths, first, own, arrived))


def pair_spec(rows):
    return pl.BlockSpec((None, rows, PAIR), lambda i: (i, 0, 0))


def pair_shapes(tokens):
    shape = (HEADS // 2, tokens, PAIR)
    return pltpu.HBM(shape, NARROW), pltpu.HBM(shape, WIDE)


def attention_specs(seqs, context):
    carry = pl.BlockSpec((seqs, 1, HEAD + 8, PAIR), lambda i: (0, i, 0, 0))
    scores = pl.BlockSpec((1, seqs, 2, context, context), lambda i: (i, 0, 0, 0, 0))
    return carry, scores, [whole_spec((3, context, PAIR)), whole_spec((PAIR, PAIR))]


def attention_local(lengths, first, attn_in, weight, bias, tables, points, weights):
    seqs, context, tokens = lengths.shape[0], tables.shape[1], attn_in.shape[0]
    pairs = HEADS // 2
    carry, scores, shared = attention_specs(seqs, context)
    narrow, wide = pair_shapes(tokens)
    return pl.pallas_call(
        partial(local_kernel, seqs),
        grid=(pairs,),
        in_specs=[
            SMEM_SPEC,
            SMEM_SPEC,
            whole_spec((tokens, D)),
            pl.BlockSpec((D, 3 * PAIR), lambda i: (0, i)),
            pl.BlockSpec((1, 3 * PAIR), lambda i: (0, i)),
            shared[0],
            whole_spec((HEAD, HEAD)),
            whole_spec((HEAD, HEAD)),
            whole_spec((HEAD,)),
        ],
        out_specs=[pair_spec(tokens)] * 9 + [scores, carry, shared[1]],
        out_shape=[narrow] * 3
        + [wide] * 6
        + [
            pltpu.HBM((pairs, seqs, 2, context, context), NARROW),
            pltpu.HBM((seqs, pairs, HEAD + 8, PAIR), WIDE),
            pltpu.HBM((PAIR, PAIR), WIDE),
        ],
        cost_estimate=lasting(14.0),
        compiler_params=pltpu.CompilerParams(vmem_limit_bytes=25165824),
        name="attention_local",
    )(*in_hbm(lengths, first, attn_in, weight, bias, tables, dct_matrix(), points, weights))


def attention_middle(lengths, first, cot, dense_weight, *rest):
    seqs, context, tokens = lengths.shape[0], rest[-2].shape[1], cot.shape[0]
    pairs = HEADS // 2
    carry, scores, shared = attention_specs(seqs, context)
    narrow, wide = pair_shapes(tokens)
    return pl.pallas_call(
        partial(middle_kernel, seqs),
        grid=(pairs,),
        in_specs=[
            SMEM_SPEC,
            SMEM_SPEC,
            whole_spec((tokens, D)),
            pl.BlockSpec((PAIR, D), lambda i: (i, 0)),
        ]
        + [pair_spec(tokens)] * 7
        + [scores, carry, *shared],
        out_specs=[pl.BlockSpec((tokens, PAIR), lambda i: (0, i))]
        + [pair_spec(tokens)] * 3
        + [carry],
        out_shape=[pltpu.HBM((tokens, D), NARROW), narrow, wide, wide]
        + [pltpu.HBM((seqs, pairs, HEAD + 8, PAIR), WIDE)],
        cost_estimate=lasting(20.0),
        compiler_params=pltpu.CompilerParams(vmem_limit_bytes=25165824),
        name="attention_middle",
    )(*in_hbm(lengths, first, cot, dense_weight, *rest))


def attention_last(lengths, first, *rest):
    seqs, context, tokens = lengths.shape[0], rest[-2].shape[1], rest[0].shape[1]
    carry, _, shared = attention_specs(seqs, context)
    return pl.pallas_call(
        partial(last_kernel, seqs),
        grid=(HEADS // 2,),
        in_specs=[SMEM_SPEC, SMEM_SPEC] + [pair_spec(tokens)] * 7 + [carry, *shared],
        out_specs=[pl.BlockSpec((tokens, 3 * PAIR), lambda i: (0, i))]
        + [whole_spec((tokens, D)), whole_spec((tokens, 2 * D))],
        out_shape=[
            pltpu.HBM((tokens, 3 * D), NARROW),
        ]
        + [pltpu.HBM((tokens, D), WIDE), pltpu.HBM((tokens, 2 * D), WIDE)],
        cost_estimate=lasting(10),
        compiler_params=pltpu.CompilerParams(vmem_limit_bytes=25165824),
        name="attention_last",
    )(*in_hbm(lengths, first, *rest))


def shards(
    inputs,
    lengths,
    ln1_gain,
    ln1_bias,
    ln2_gain,
    ln2_bias,
    qkv_weight,
    qkv_bias,
    dense_weight,
    dense_bias,
    up_weight,
    up_bias,
    down_weight,
    down_bias,
    qmc_points,
    qmc_weights,
    cotangent,
):
    seqs, context = inputs.shape[:2]
    tokens = seqs * context
    owners, count, place = lax.axis_size("batch"), lax.axis_size("seq"), lax.axis_index("seq")
    bits = list(range(owners.bit_length() - 2))[::-1]
    across = D // COLUMNS
    hops = max(1, count // 2)

    line = Line()
    me = lax.axis_index("batch").astype(jnp.int32)[None]
    edge = ((place == 0) | (place == count - 1)).astype(jnp.int32)[None]
    if owners == 8 and count == 4:
        reduction = Rounds(line, edge, [2, 2, 2, 2, 1, 1, 1, 1])
    else:
        reduction = Singly(line, bits)

    def group(name, shape, at, left, blocks, right, rights_in, columns, begin=0, arrived=()):
        many = len(rights_in)
        pieces = [
            (*left, block, right, rights_in[column % many], place, (row, column))
            for column in range(columns)
            for row, block in enumerate(blocks)
            for place in [(begin + column, columns) if many == 1 else (0, 1)]
        ]
        size = (len(blocks) * BLOCK_ROWS, columns * COLUMNS // Rounds.PARTS)
        reduction.prepare((name, shape, at, size), pieces, *arrived)

    BLOCK_ROWS = min(BLOCK, D // owners)
    inputs_flat = inputs.reshape(tokens, D)
    cot = cotangent.reshape(tokens, D)
    cot_in = swap(cot.astype(WIDE), 0)
    start = place * context
    first = jnp.stack([start, jnp.full((), context, jnp.int32)])
    qkv_row = qkv_bias.astype(WIDE)[None, :]
    tables = attention_tables(place, context, count)
    attn_in, mlp_in, unit, rate = line.step(
        two_norms, inputs_flat, ln1_gain, ln1_bias, ln2_gain, ln2_bias
    )
    act, slope, act_own, act_send = line.step(mlp_up, mlp_in, up_weight, up_bias, me)
    act_in = swap(act_send, 0)
    norm_own, norm_send = line.step(lambda *a: pick(a[:2], a[2]), attn_in, mlp_in, me)
    subs = act_own.shape[0]

    def down_group(sub):
        shape = (FF // owners, D)
        at = (sub // 2, 0)
        group("down", shape, at, (act_own, act_in), (sub, sub + 1), cot, [cot_in], across)

    down_group(0)
    up_grad, up_send, up_sums, mlp_out, mlp_norm_grad = line.step(
        mlp_back, cot, down_weight, up_weight, act, slope
    )
    for sub in range(2, subs, 2):
        down_group(sub)
    reduction.step(tables, qkv_row, first)
    up_in = line.send(up_send, lambda a: swap(a, 0))
    norm_in = line.send(norm_send, lambda a: swap(a, 0))

    fq, fk, value, phi_q, phi_k, rot_q, rot_k, num, den, scores, carry, mix = line.step(
        attention_local,
        lengths,
        first,
        attn_in,
        qkv_weight,
        qkv_row,
        tables,
        qmc_points,
        qmc_weights,
    )
    arrived = shift_rows(carry, "seq", 1)

    def up_group(part):
        shape = (D // owners, FF)
        at = (0, part * Rounds.PARTS)
        columns = FF // COLUMNS // 2
        group("up", shape, at, (norm_own, norm_in), (1,), up_grad, [up_in], columns, part * Rounds.PARTS * columns)

    up_group(0)
    for _ in range(hops - 1):
        passed = line.step(pass_on, carry, arrived, lengths, first)
        arrived = shift_rows(passed, "seq", 1)
    reduction.step()
    up_group(1)
    attn_low, grad_q, grad_k, grad_v, carry_back = line.step(
        attention_middle,
        lengths,
        first,
        cot,
        dense_weight,
        fq,
        fk,
        value,
        phi_q,
        rot_q,
        num,
        den,
        scores,
        arrived,
        tables,
        mix,
    )
    arrived_back = shift_rows(carry_back, "seq", -1)
    low_own, low_send = line.step(lambda *a: pick(a[:1], a[1]), attn_low, me)
    low_in = swap(low_send, 0)
    reduction.step()
    output = line.step(
        layer_output,
        attn_low,
        dense_weight,
        inputs_flat,
        mlp_out,
        dense_bias,
        down_bias,
    )
    for _ in range(hops - 1):
        passed = line.step(pass_on, carry_back, arrived_back, lengths, first)
        arrived_back = shift_rows(passed, "seq", -1)
    shape = (D // owners, D)
    group("dense", shape, (0, 0), (low_own, low_in), (0,), cot, [cot_in], across)
    reduction.step()
    qkv_grad, *qkv_send = line.step(
        attention_last,
        lengths,
        first,
        grad_q,
        grad_k,
        grad_v,
        fk,
        value,
        phi_k,
        rot_k,
        arrived_back,
        tables,
        mix,
    )
    qkv_in = [swap(qkv_send[0], 0)]
    qkv_rest = swap(qkv_send[1], 0)
    def qkv_group(part, *arrived):
        shape = (D // owners, 3 * D)
        at = (0, part * Rounds.PARTS)
        left = (norm_own, norm_in)
        group("qkv", shape, at, left, (0,), qkv_grad, qkv_in, 2, max(part - 1, 0) * 4, arrived)

    arriving = reduction.arriving()
    qkv_group(0, *([line.step(lambda *a: settle(a), *arriving)] if arriving else []))
    reduction.step()
    qkv_in = [qkv_rest]
    qkv_group(1)
    input_grad, sums, qkv_sums = line.step(
        norm_back,
        qkv_grad,
        qkv_weight,
        mlp_norm_grad,
        unit,
        rate,
        cot,
        ln1_gain,
        ln2_gain,
    )

    vectors = Vectors(line, (sums, qkv_sums, up_sums), [])
    vectors.send()
    reduction.step()
    qkv_group(2)
    vectors.take()
    vectors.send()
    while not reduction.finished():
        reduction.step()
        vectors.take()
        vectors.send()
    totals = reduction.results()
    (
        attn_gain_total,
        attn_shift_total,
        mlp_gain_total,
        mlp_shift_total,
        bias_total,
        qkv_bias_total,
        up_bias_total,
    ) = vectors.results()

    return (
        output.reshape(inputs.shape),
        input_grad.reshape(inputs.shape),
        attn_gain_total,
        attn_shift_total,
        mlp_gain_total,
        mlp_shift_total,
        totals["qkv"],
        qkv_bias_total,
        totals["dense"],
        bias_total,
        totals["up"],
        up_bias_total,
        totals["down"],
        bias_total,
    )


def solution(mesh):
    placed = (
        P("batch", "seq", None),
        P("batch", None),
        P(),
        P(),
        P(),
        P(),
        P(),
        P(),
        P(),
        P(),
        P(),
        P(),
        P(),
        P(),
        P(),
        P(),
        P("batch", "seq", None),
    )
    return jax.shard_map(
        shards,
        mesh=mesh,
        in_specs=placed,
        out_specs=(
            P("batch", "seq", None),
            P("batch", "seq", None),
            P("batch"),
            P("batch"),
            P("batch"),
            P("batch"),
            P("batch", None),
            P("batch"),
            P("batch", None),
            P("batch"),
            P("batch", None),
            P("batch"),
            P("batch", None),
            P("batch"),
        ),
        check_vma=False,
    )
```

```python
import math
from functools import partial

import jax
import jax.numpy as jnp
import numpy as np
from jax import lax
from jax.experimental import pallas as pl
from jax.experimental.pallas import tpu as pltpu
from jax.sharding import PartitionSpec as P

D = 1024
HEADS = 16
HEAD = 64
ROT = 16
FF = 4096
PAIR = 2 * HEAD
BLOCK = 128
COLUMNS = 512

EPSILON = 1e-05
ROTARY_BASE = 10000.0

def lasting(microseconds):
    return pl.CostEstimate(
        flops=int(microseconds * 1.15e9), transcendentals=0, bytes_accessed=0
    )


ROWS_COLS = ((1,), (0,))
ROWS_ROWS = ((1,), (1,))
COLS_COLS = ((0,), (0,))
NARROW = jnp.bfloat16
WIDE = jnp.float32


def plain_dot(left, right, dims):
    return lax.dot_general(left, right, (dims, ((), ())), preferred_element_type=WIDE)


def whole_spec(shape):
    return pl.BlockSpec(shape, lambda *_: (0,) * len(shape))


def shift_rows(value, axis, by):
    count = lax.axis_size(axis)
    return lax.ppermute(
        value, axis, [(i, i + by) for i in range(count) if 0 <= i + by < count]
    )


def in_hbm(*values):
    return [
        pltpu.with_memory_space_constraint(v, pltpu.HBM)
        if v.size * v.dtype.itemsize >= 1 << 16
        else v
        for v in values
    ]


def swap(value, bit):
    count = lax.axis_size("batch")
    return lax.ppermute(value, "batch", [(i, i ^ (1 << bit)) for i in range(count)])


def owner_order(bits):
    return sorted(
        range(1 << len(bits)), key=lambda r: tuple(-((r >> bit) & 1) for bit in bits)
    )


def line_rounds(count):
    half = count // 2
    rounds = [("in", [(k, k + 1), (count - 1 - k, count - 2 - k)], k) for k in range(half - 1)]
    rounds.append(("in", [(half - 1, half), (half, half - 1)], -1))
    for k in range(half - 2, -1, -1):
        rounds.append(("out", [(k + 1, k), (count - 2 - k, count - 1 - k)], k))
    return rounds


class Line:
    def __init__(self):
        self.last = None

    def wait(self, *values):
        if self.last is not None:
            values, _ = lax.optimization_barrier((values, self.last))
        return values

    def send(self, value, how):
        return how(*self.wait(value))

    def step(self, function, *values):
        out = function(*self.wait(*values))
        self.last = jax.tree.leaves(out)[0]
        return out


def pack_kernel(order, sizes, count, me_ref, *refs):
    ins, out_ref = refs[:count], refs[-1]
    at, sizes = 0, list(sizes)
    for ref in ins:
        count = ref.shape[0]
        size, sizes = sizes[0], sizes[count:]
        for k, relative in enumerate(order):
            start = pl.multiple_of((relative ^ me_ref[0]) * size, BLOCK)
            block = ref[:, pl.ds(start, size)]
            for j in range(count):
                out_ref[k : k + 1, at + j * size : at + (j + 1) * size] = block[j : j + 1]
        at += count * size


def pack(order, sizes, arriving, me, *blocks):
    return pl.pallas_call(
        partial(pack_kernel, order, sizes, len(blocks)),
        in_specs=[pl.BlockSpec(memory_space=pltpu.SMEM)]
        + [pl.BlockSpec(memory_space=pltpu.VMEM)] * len(blocks)
        + [pl.BlockSpec(memory_space=pl.ANY)] * len(arriving),
        out_specs=pl.BlockSpec(memory_space=pltpu.VMEM),
        out_shape=jax.ShapeDtypeStruct((len(order), sum(sizes)), WIDE),
        name="pack_vectors",
    )(me, *blocks, *arriving)


class Vectors:
    def __init__(self, line, blocks, arriving):
        owners = lax.axis_size("batch")
        me = lax.axis_index("batch").astype(jnp.int32)
        self.line = line
        vectors = [v for block in blocks for v in block]
        self.sizes = [v.shape[0] // owners for v in vectors]
        bits = list(range(owners.bit_length() - 1))
        order = owner_order(bits)
        if any(size % BLOCK for size in self.sizes):
            pieces = jnp.concatenate([v.reshape(owners, -1) for v in vectors], axis=1)
            rows = [lax.dynamic_slice_in_dim(pieces, r ^ me, 1, 0) for r in order]
            self.held = jnp.concatenate(rows)
        else:
            self.held = line.step(
                lambda *a: pack(order, self.sizes, arriving, *a), me[None], *blocks
            )
        count = lax.axis_size("seq")
        self.steps = [("swap", bit, 0) for bit in bits]
        self.steps += line_rounds(count) if count % 2 == 0 else []
        self.moving = None
        self.now = None

    def send(self):
        if self.moving is not None or not self.steps:
            return
        self.now = kind, what, _ = self.steps.pop(0)
        if kind == "swap":
            half = self.held.shape[0] // 2
            self.moving = self.line.send(self.held[:half], lambda a: swap(a, what))
            self.held = self.held[half:]
        else:
            self.moving = self.line.send(self.held, lambda a: lax.ppermute(a, "seq", what))

    def take(self):
        if self.moving is None:
            return
        kind, _, at = self.now
        if kind == "out":
            place, count = lax.axis_index("seq"), lax.axis_size("seq")
            edge = (place == at) | (place == count - 1 - at)
            self.held = self.line.step(
                lambda a, b: jnp.where(edge, b, a), self.held, self.moving
            )
        else:
            self.held = self.line.step(lambda a, b: a + b, self.held, self.moving)
        self.moving = None

    def results(self):
        while self.moving is not None or self.steps:
            self.take()
            self.send()
        if lax.axis_size("seq") % 2 and lax.axis_size("seq") > 1:
            self.held = lax.psum(self.held, "seq")
        out, at = [], 0
        for size in self.sizes:
            out.append(self.held[0, at : at + size])
            at += size
        return out


class Reduction:
    def __init__(self, line, left, right, bits):
        self.line = line
        half = left.shape[1] // 2
        send = line.step(lambda a, b: plain_dot(a, b, COLS_COLS), left[:, :half], right)
        self.held = line.step(lambda a, b: plain_dot(a, b, COLS_COLS), left[:, half:], right)
        count = lax.axis_size("seq")
        self.steps = [("swap", bit + 1, 0) for bit in bits]
        self.steps += line_rounds(count) if count % 2 == 0 else []
        self.moving = swap(send, bits[0] + 1)

    def finish(self):
        place, count = lax.axis_index("seq"), lax.axis_size("seq")
        for i, (kind, _, at) in enumerate(self.steps):
            if kind == "out":
                edge = (place == at) | (place == count - 1 - at)
                self.held = self.line.step(
                    lambda a, b: jnp.where(edge, b, a), self.held, self.moving
                )
            else:
                self.held = self.line.step(lambda a, b: a + b, self.held, self.moving)
            if i + 1 == len(self.steps):
                break
            kind, what, _ = self.steps[i + 1]
            if kind == "swap":
                half = self.held.shape[0] // 2
                self.moving = swap(self.held[:half], what)
                self.held = self.held[half:]
            else:
                self.moving = lax.ppermute(self.held, "seq", what)
        return self.held if count % 2 == 0 or count == 1 else lax.psum(self.held, "seq")


class Singly:
    def __init__(self, line, bits):
        self.line, self.bits = line, bits
        self.pieces, self.outputs = [], {}

    def prepare(self, target, pieces, *arrived):
        _, _, at, size = target
        for left, left_in, block, right, right_in, (begin, each), (row, column) in pieces:
            wide = COLUMNS // Rounds.PARTS
            across = size[1] // wide
            starts = [((at[1] + i) * across + column) * wide for i in range(Rounds.PARTS)]
            starts_in = [(begin + i * each) * wide for i in range(Rounds.PARTS)]
            right, right_in = (
                jnp.concatenate([value[:, k : k + wide] for k in places], axis=1)
                for value, places in ((right, starts), (right_in, starts_in))
            )
            left = jnp.concatenate([left[block], rounded(left_in[block])], axis=0)
            right = jnp.concatenate([right, rounded(right_in)], axis=0)
            done = Reduction(self.line, left, right, self.bits)
            self.pieces.append((target, row, starts, wide, done))

    def step(self, *arrived):
        pass

    def arriving(self):
        return []

    def finished(self):
        return True

    def results(self):
        for (name, shape, at, size), row, starts, wide, piece in self.pieces:
            whole = self.outputs.get(name, jnp.zeros(shape, WIDE))
            total = piece.finish()
            top = at[0] * size[0] + row * total.shape[0]
            for i, k in enumerate(starts):
                whole = lax.dynamic_update_slice(
                    whole, total[:, i * wide : (i + 1) * wide], (top, k)
                )
            self.outputs[name] = whole
        return self.outputs


def rounded(arrived):
    one = jnp.where(lax.axis_index("seq") < lax.axis_size("seq"), 1.0, 0.5)
    return (arrived * one).astype(NARROW)


def product_kernel(count, *refs):
    ins, (to_x, to_y, hold_a, hold_b) = refs[: 8 * count], refs[-4:]
    for p in range(count):
        for i, (to, hold) in enumerate(((to_x, hold_a), (to_y, hold_b))):
            left, left_in, right, right_in = ins[8 * p + 4 * i : 8 * p + 4 * i + 4]
            whole = jnp.concatenate([left[0], left_in[0].astype(NARROW)], axis=0)
            right = jnp.concatenate([right[...], right_in[...].astype(NARROW)], axis=0)

            def product(first, second):
                rows = [whole[:, k * BLOCK : (k + 1) * BLOCK] for k in (first, second)]
                return plain_dot(jnp.concatenate(rows, axis=1), right, COLS_COLS)

            out = pl.ds(p * 2 * BLOCK, 2 * BLOCK)
            to[out, :] = product(0, 1 if i else 2)
            hold[out, :] = product(2 if i else 1, 3)


def round_kernel(counts, places, skip, *refs):
    first, second, inward, middle, outward = counts
    refs = list(refs)
    edge = refs.pop(0)[0] != 0

    def take(flag, count):
        return [refs.pop(0) for _ in range(count)] if flag else [None] * count

    from_x, from_y = take(first or second, 2)
    hold_a, hold_b = take(first, 2)
    kept_a, kept_b = take(second, 2)
    (sums,) = take(inward, 1)
    (from_end,) = take(inward or outward, 1)
    inner, from_middle = take(middle, 2)
    (whole,) = take(outward, 1)
    take(True, skip)
    to_x, to_y, keep_a, keep_b = take(first, 4)
    (new_sums,) = take(second, 1)
    (to_end,) = take(second or middle, 1)
    (new_inner,) = take(inward, 1)
    (final,) = take(outward, 1)
    for p in range(first):
        low = pl.ds(2 * p * BLOCK, BLOCK)
        high = pl.ds((2 * p + 1) * BLOCK, BLOCK)
        out = pl.ds(p * BLOCK, BLOCK)
        to_y[out, :] = hold_a[low, :] + from_x[low, :]
        to_x[out, :] = hold_b[low, :] + from_y[low, :]
        keep_a[out, :] = hold_a[high, :] + from_x[high, :]
        keep_b[out, :] = hold_b[high, :] + from_y[high, :]
    for p in range(max(second, middle)):
        for i, (kept, arrived) in enumerate(((kept_a, from_y), (kept_b, from_x))):
            out = pl.ds((2 * p + i) * BLOCK, BLOCK)
            ends = inners = None
            if p < second:
                come = pl.ds((2 * first + p) * BLOCK, BLOCK)
                ends = kept[pl.ds(p * BLOCK, BLOCK), :] + arrived[come, :]
                new_sums[out, :] = ends
            if p < middle:
                inners = inner[out, :] + from_middle[out, :]
            if ends is None:
                to_end[out, :] = inners
            elif inners is None:
                to_end[out, :] = ends
            else:
                to_end[out, :] = jnp.where(edge, ends, inners)
    if inward:
        new_inner[...] = sums[...] + from_end[: 2 * inward * BLOCK, :]
    for k, (row, column) in enumerate(places):
        rows = pl.ds(k * BLOCK, BLOCK)
        wide = final.shape[1] // (1 + max(column for _, column in places))
        total = jnp.where(edge, from_end[rows, :], whole[rows, :])
        final[row * BLOCK : (row + 1) * BLOCK, column * wide : (column + 1) * wide] = total


class Rounds:
    PARTS = 2

    def __init__(self, line, edge, counts):
        self.line, self.edge, self.counts = line, edge, counts
        self.made = self.at = 0
        self.buffers, self.moving, self.hold, self.kept = {}, {}, {}, {}
        self.sums, self.inner, self.whole, self.targets = {}, {}, None, []
        self.outputs = {}
        self.end = self.middle = None
        self.wide = COLUMNS // self.PARTS

    def count(self, group):
        return self.counts[group] if 0 <= group < len(self.counts) else 0

    def place(self, value, local, sent):
        if local:
            return pltpu.with_memory_space_constraint(value, pltpu.HBM)
        return pltpu.with_memory_space_constraint(value, pltpu.HBM) if sent else value

    def rows_spec(self, rows, at=0):
        return pl.BlockSpec((rows, self.wide), lambda i: (at, i))

    def prepare(self, target, pieces, *arrived):
        r = self.made
        self.made += 1
        self.targets.append((target, [piece[-1] for piece in pieces]))
        count = len(pieces) // 2
        name, shape, at, size = target
        across = size[1] // self.wide
        args, specs = [], []
        for left, left_in, block, right, right_in, (begin, each), (_, column) in pieces:
            for value in (left, left_in):
                args += in_hbm(value) if value is left else [value]
                specs.append(
                    pl.BlockSpec((1, *value.shape[1:]), lambda i, block=block: (block, 0, 0))
                )
            mine = (at[1] * across + column, across)
            for value, (begin, each) in ((right, mine), (right_in, (begin, each))):
                args += in_hbm(value) if value is right else [value]
                specs.append(
                    pl.BlockSpec(
                        (value.shape[0], self.wide),
                        lambda i, begin=begin, each=each: (0, begin + i * each),
                    )
                )
        args += arrived
        specs += [pl.BlockSpec(memory_space=pl.ANY)] * len(arrived)
        rows = 2 * count * BLOCK
        total = rows + self.count(r - 1) * BLOCK
        call = pl.pallas_call(
            partial(product_kernel, count),
            grid=(self.PARTS,),
            in_specs=specs,
            out_specs=[self.rows_spec(rows)] * 4,
            out_shape=[pltpu.HBM((total, COLUMNS), WIDE)] * 2
            + [pltpu.HBM((rows, COLUMNS), WIDE)] * 2,
            cost_estimate=lasting(5),
        compiler_params=pltpu.CompilerParams(vmem_limit_bytes=25165824),
        name="piece_products",
        )
        to_x, to_y, hold_a, hold_b = self.line.step(call, *args)
        self.hold[r] = (hold_a, hold_b)
        if r:
            self.buffers[r] = (to_x, to_y)
        else:
            self.moving[r] = (swap(to_x, 1), swap(to_y, 2))

    def step(self, *arrived):
        r = self.at
        self.at += 1
        counts = [self.count(r - back) for back in (0, 1, 2, 3, 4)]
        first, second, inward, middle, outward = counts
        aliases = {}
        args, specs = [self.edge], [pl.BlockSpec(memory_space=pltpu.SMEM)]

        def add(value, local=False, sent=False):
            args.append(self.place(value, local, sent))
            specs.append(self.rows_spec(value.shape[0]))

        if first or second:
            for value in self.moving.pop(r):
                add(value)
        if first:
            for value in self.hold.pop(r):
                add(value, local=True)
        if second:
            for value in self.kept.pop(r - 1):
                add(value, local=True)
        if inward:
            add(self.sums.pop(r - 2), local=True)
        if inward or outward:
            add(self.end)
        if middle:
            add(self.inner.pop(r - 3), sent=True)
            add(self.middle)
        if outward:
            add(self.whole, sent=True)
        outs, out_specs = [], []

        def out(rows, at=0, of=None, sent=False):
            kind = pltpu.HBM if sent else pltpu.HBM
            outs.append(kind((of or rows, COLUMNS), WIDE))
            out_specs.append(self.rows_spec(rows, at))

        ahead = self.count(r + 1)
        if ahead:
            aliases = {len(args): 0, len(args) + 1: 1}
            args += list(self.buffers.pop(r + 1))
            specs += [pl.BlockSpec(memory_space=pl.ANY)] * 2
        if first:
            for _ in range(2):
                out(first * BLOCK, 2 * ahead // first, (2 * ahead + first) * BLOCK, sent=True)
            out(first * BLOCK)
            out(first * BLOCK)
        if second:
            out(2 * second * BLOCK)
        if second or middle:
            out(2 * max(second, middle) * BLOCK, sent=True)
        if inward:
            out(2 * inward * BLOCK, sent=True)
        places = ()
        if outward:
            (name, shape, at, size), places = self.targets[r - 4]
            if name in self.outputs:
                aliases[len(args)] = len(outs)
                args.append(self.outputs[name])
                specs.append(pl.BlockSpec(memory_space=pl.ANY))
            outs.append(pltpu.HBM(shape, WIDE))
            out_specs.append(pl.BlockSpec(size, lambda i: (at[0], at[1] + i)))
        args += arrived
        specs += [pl.BlockSpec(memory_space=pl.ANY)] * len(arrived)
        call = pl.pallas_call(
            partial(round_kernel, counts, places, len(aliases) + len(arrived)),
            grid=(self.PARTS,),
            in_specs=specs,
            out_specs=out_specs,
            out_shape=outs,
            input_output_aliases=aliases,
            cost_estimate=lasting(5.0),
            compiler_params=pltpu.CompilerParams(vmem_limit_bytes=25165824),
            name="reduce_round",
        )
        got = list(self.line.step(call, *args))
        if first:
            self.moving[r + 1] = (swap(got.pop(0), 1), swap(got.pop(0), 2))
            self.kept[r] = (got.pop(0), got.pop(0))
        if second:
            self.sums[r - 1] = got.pop(0)
        self.whole = None
        if second or middle:
            self.whole = got.pop(0)
            self.end = lax.ppermute(self.whole, "seq", [(0, 1), (1, 0), (2, 3), (3, 2)])
        if inward:
            self.inner[r - 2] = got.pop(0)
            self.middle = lax.ppermute(self.inner[r - 2], "seq", [(1, 2), (2, 1)])
        if outward:
            self.outputs[name] = got.pop(0)

    def arriving(self):
        return [*self.moving[self.at], self.end, self.middle]

    def finished(self):
        return self.at == len(self.counts) + 4

    def results(self):
        return self.outputs


def settle_kernel(*refs):
    refs[-1][...] = jnp.zeros_like(refs[-1])


def settle(arriving):
    return pl.pallas_call(
        settle_kernel,
        in_specs=[pl.BlockSpec(memory_space=pl.ANY)] * len(arriving),
        out_specs=pl.BlockSpec(memory_space=pltpu.VMEM),
        out_shape=jax.ShapeDtypeStruct((8, 128), WIDE),
        cost_estimate=lasting(12),
        name="settle",
    )(*arriving)


def pick_kernel(me_ref, *refs):
    ins, (keep_ref, send_ref) = refs[:-2], refs[-2:]
    half = keep_ref.shape[2] // BLOCK
    for i, ref in enumerate(ins):
        for p in range(half):
            for core in range(2):
                owner = (2 * (half - 1 - p) + core) ^ me_ref[0]
                columns = ref[:, pl.ds(pl.multiple_of(owner * BLOCK, BLOCK), BLOCK)]
                at = slice(p * BLOCK, (p + 1) * BLOCK)
                if core:
                    send_ref[i, :, at] = columns.astype(WIDE)
                else:
                    keep_ref[i, :, at] = columns


def pick(arrays, me):
    owners = lax.axis_size("batch")
    half = owners // 2
    tokens, features = arrays[0].shape
    size = features // owners
    if size != BLOCK:

        def columns(value, core):
            return jnp.concatenate(
                [
                    lax.dynamic_slice_in_dim(value, ((2 * r + core) ^ me[0]) * size, size, 1)
                    for r in range(half)[::-1]
                ],
                axis=1,
            )

        return (
            jnp.stack([columns(a, 0) for a in arrays]),
            jnp.stack([columns(a, 1) for a in arrays]).astype(WIDE),
        )
    shape = (len(arrays), tokens, half * size)
    return pl.pallas_call(
        pick_kernel,
        in_specs=[pl.BlockSpec(memory_space=pltpu.SMEM)]
        + [pl.BlockSpec(memory_space=pltpu.VMEM)] * len(arrays),
        out_specs=[pl.BlockSpec(memory_space=pltpu.VMEM)] * 2,
        out_shape=[pltpu.HBM(shape, NARROW), pltpu.HBM(shape, WIDE)],
        cost_estimate=lasting(2.0),
        name="pick_columns",
    )(*in_hbm(me, *arrays))


def as_row(ref):
    return ref[...].astype(WIDE)[None, :]


def norm_kernel(x_ref, gain1, bias1, gain2, bias2, attn_ref, mlp_ref, unit_ref, rate_ref):
    x = x_ref[...].astype(WIDE)
    centered = x - jnp.mean(x, axis=-1, keepdims=True)
    rate = lax.rsqrt(jnp.mean(centered * centered, axis=-1, keepdims=True) + EPSILON)
    unit = centered * rate
    unit_ref[...] = unit
    rate_ref[...] = jnp.broadcast_to(rate, rate_ref.shape)
    for gain, bias, out in ((gain1, bias1, attn_ref), (gain2, bias2, mlp_ref)):
        out[...] = (unit * as_row(gain) + as_row(bias)).astype(NARROW)


def two_norms(inputs, *gains):
    tokens = inputs.shape[0]
    rows = tokens // 4
    by_rows = pl.BlockSpec((rows, D), lambda i: (i, 0))
    return pl.pallas_call(
        norm_kernel,
        grid=(4,),
        in_specs=[by_rows] + [whole_spec((D,))] * len(gains),
        out_specs=[by_rows, by_rows, by_rows, pl.BlockSpec((rows, 128), lambda i: (i, 0))],
        out_shape=[
            pltpu.HBM((tokens, D), NARROW),
            pltpu.HBM((tokens, D), NARROW),
            pltpu.HBM((tokens, D), WIDE),
            pltpu.HBM((tokens, 128), WIDE),
        ],
        cost_estimate=lasting(4.0),
        name="two_norms",
    )(*in_hbm(inputs, *gains))


def up_kernel(
    half, me_ref, x_ref, weight_ref, bias_ref, act_ref, slope_ref, keep_ref, send_ref
):
    step = pl.program_id(0)
    up = plain_dot(x_ref[...], weight_ref[...], ROWS_COLS) + as_row(bias_ref)
    below = 0.5 * (1.0 + lax.erf(up * (0.5**0.5)))
    act = (up * below).astype(NARROW)
    act_ref[...] = act
    slope_ref[...] = below + up * jnp.exp(-0.5 * up * up) * ((2.0 * math.pi) ** -0.5)

    @pl.when(step < half)
    def _():
        for i in range(keep_ref.shape[0]):
            keep_ref[i] = act[:, i * BLOCK : (i + 1) * BLOCK]

    @pl.when(step >= half)
    def _():
        wide = act.astype(WIDE)
        for i in range(send_ref.shape[0]):
            send_ref[i] = wide[:, i * BLOCK : (i + 1) * BLOCK]


def mlp_up(mlp_in, up_weight, up_bias, me):
    owners = lax.axis_size("batch")
    tokens = mlp_in.shape[0]
    half = owners // 2
    each = FF // owners
    subs = each // BLOCK

    def natural(i, me):
        return (0, (2 * (i % half) + i // half) ^ me[0])

    return pl.pallas_call(
        partial(up_kernel, half),
        grid_spec=pltpu.PrefetchScalarGridSpec(
            num_scalar_prefetch=1,
            grid=(owners,),
            in_specs=[
                pl.BlockSpec((tokens, D), lambda i, me: (0, 0)),
                pl.BlockSpec((D, each), natural),
                pl.BlockSpec((each,), lambda i, me: natural(i, me)[1:]),
            ],
            out_specs=[
                pl.BlockSpec((tokens, each), natural),
                pl.BlockSpec((tokens, each), natural),
                pl.BlockSpec(
                    (subs, tokens, BLOCK),
                    lambda i, me: (0, 0, half - 1 - jnp.minimum(i, half - 1)),
                ),
                pl.BlockSpec(
                    (subs, tokens, BLOCK),
                    lambda i, me: (0, 0, half - 1 - jnp.maximum(i - half, 0)),
                ),
            ],
        ),
        out_shape=[
            pltpu.HBM((tokens, FF), NARROW),
            pltpu.HBM((tokens, FF), WIDE),
            pltpu.HBM((subs, tokens, half * BLOCK), NARROW),
            pltpu.HBM((subs, tokens, half * BLOCK), WIDE),
        ],
        cost_estimate=lasting(11.0),
        name="mlp_up",
    )(*in_hbm(me, mlp_in, up_weight, up_bias))


def back_kernel(
    cot_ref, down_ref, up_ref, act_ref, slope_ref, grad_ref, send_ref, sums_ref, out_ref, norm_ref
):
    step = pl.program_id(0)
    down = down_ref[...]
    grad = plain_dot(cot_ref[...], down, ROWS_ROWS) * slope_ref[...]
    grad = grad.astype(NARROW)
    grad_ref[...] = grad
    wide = grad.astype(WIDE)
    send_ref[...] = wide
    sums_ref[...] = jnp.sum(wide, axis=0, keepdims=True)
    out = plain_dot(act_ref[...], down, ROWS_COLS)
    norm = plain_dot(grad, up_ref[...], ROWS_ROWS)

    @pl.when(step == 0)
    def _():
        out_ref[...] = out
        norm_ref[...] = norm

    @pl.when(step > 0)
    def _():
        out_ref[...] += out
        norm_ref[...] += norm


def mlp_back(cot, down_weight, up_weight, act, slope):
    tokens = cot.shape[0]
    each = 1024
    by_column = pl.BlockSpec((tokens, each), lambda i: (0, i))
    total = whole_spec((tokens, D))
    return pl.pallas_call(
        back_kernel,
        grid=(FF // each,),
        in_specs=[
            total,
            pl.BlockSpec((each, D), lambda i: (i, 0)),
            pl.BlockSpec((D, each), lambda i: (0, i)),
            by_column,
            by_column,
        ],
        out_specs=[
            by_column,
            by_column,
            pl.BlockSpec((1, each), lambda i: (0, i)),
            total,
            total,
        ],
        out_shape=[
            pltpu.HBM((tokens, FF), NARROW),
            pltpu.HBM((tokens, FF), WIDE),
            pltpu.HBM((1, FF), WIDE),
            pltpu.HBM((tokens, D), WIDE),
            pltpu.HBM((tokens, D), WIDE),
        ],
        cost_estimate=lasting(16.0),
        compiler_params=pltpu.CompilerParams(vmem_limit_bytes=25165824),
        name="mlp_back",
    )(*in_hbm(cot, down_weight, up_weight, act, slope))


def output_kernel(low_ref, weight_ref, x_ref, mlp_ref, dense_ref, down_ref, out_ref):
    attn = plain_dot(low_ref[...], weight_ref[...], ROWS_COLS) + as_row(dense_ref)
    mlp = mlp_ref[...] + as_row(down_ref)
    out_ref[...] = (x_ref[...].astype(WIDE) + attn + mlp).astype(NARROW)


def layer_output(low, dense_weight, inputs, mlp_out, *biases):
    tokens = inputs.shape[0]
    each = 512
    by_column = pl.BlockSpec((tokens, each), lambda i: (0, i))
    return pl.pallas_call(
        output_kernel,
        grid=(D // each,),
        in_specs=[
            whole_spec((tokens, D)),
            pl.BlockSpec((D, each), lambda i: (0, i)),
            by_column,
            by_column,
        ]
        + [pl.BlockSpec((each,), lambda i: (i,))] * len(biases),
        out_specs=by_column,
        out_shape=pltpu.HBM((tokens, D), NARROW),
        cost_estimate=lasting(3.0),
        name="layer_output",
    )(*in_hbm(low, dense_weight, inputs, mlp_out, *biases))


def norm_back_kernel(
    qkv_ref,
    weight_ref,
    mlp_ref,
    unit_ref,
    rate_ref,
    cot_ref,
    gain1,
    gain2,
    grad_ref,
    sums_ref,
    qkv_sums,
):
    step = pl.program_id(0)
    qkv = qkv_ref[...]
    qkv_sums[...] = jnp.sum(qkv.astype(WIDE), axis=0, keepdims=True)
    part = plain_dot(qkv, weight_ref[...], ROWS_ROWS)

    @pl.when(step == 0)
    def _():
        grad_ref[...] = part

    @pl.when(step > 0)
    def _():
        grad_ref[...] += part

    @pl.when(step == pl.num_programs(0) - 1)
    def _():
        size = 64
        gain_attn, gain_mlp = as_row(gain1), as_row(gain2)
        totals = [jnp.zeros((1, D), WIDE)] * 5
        for k in range(grad_ref.shape[0] // size):
            rows = pl.ds(k * size, size)
            attn, mlp, unit = grad_ref[rows, :], mlp_ref[rows, :], unit_ref[rows, :]
            cot = cot_ref[rows, :].astype(WIDE)
            together = attn * gain_attn + mlp * gain_mlp
            grad_ref[rows, :] = cot + rate_ref[rows, 0:1] * (
                together
                - jnp.mean(together, axis=-1, keepdims=True)
                - unit * jnp.mean(together * unit, axis=-1, keepdims=True)
            )
            for i, value in enumerate((attn * unit, attn, mlp * unit, mlp, cot)):
                totals[i] = totals[i] + jnp.sum(value, axis=0, keepdims=True)
        for i, value in enumerate(totals):
            sums_ref[i : i + 1, :] = value


def norm_back(qkv_grad, qkv_weight, mlp_norm_grad, unit, rate, cot, *gains):
    tokens = cot.shape[0]
    each = 512
    total = whole_spec((tokens, D))
    return pl.pallas_call(
        norm_back_kernel,
        grid=(3 * D // each,),
        in_specs=[
            pl.BlockSpec((tokens, each), lambda i: (0, i)),
            pl.BlockSpec((D, each), lambda i: (0, i)),
            total,
            total,
            whole_spec(rate.shape),
            total,
        ]
        + [whole_spec((D,))] * len(gains),
        out_specs=[total, whole_spec((5, D)), pl.BlockSpec((1, each), lambda i: (0, i))],
        out_shape=[
            pltpu.HBM((tokens, D), WIDE),
            pltpu.HBM((5, D), WIDE),
            pltpu.HBM((1, 3 * D), WIDE),
        ],
        compiler_params=pltpu.CompilerParams(vmem_limit_bytes=25165824),
        name="norm_back",
    )(*in_hbm(qkv_grad, qkv_weight, mlp_norm_grad, unit, rate, cot, *gains))


def dct_matrix():
    rows = np.arange(HEAD)[:, None]
    columns = np.arange(HEAD)[None, :]
    cosines = np.cos(np.pi * (columns + 0.5) * rows / HEAD) * np.sqrt(2.0 / HEAD)
    return np.where(rows == 0, cosines * np.sqrt(0.5), cosines).astype(np.float32)


def attention_tables(place, context, count):
    half_rot = ROT // 2
    lane = np.arange(PAIR) % HEAD
    freq = ROTARY_BASE ** (-2.0 * (lane % half_rot) / ROT)
    angles = np.arange(count * context)[:, None] * freq[None, :]
    tables = np.stack(
        [
            np.where(lane < ROT, np.cos(angles), 1.0),
            np.where(lane < half_rot, -np.sin(angles), 0.0),
            np.where((lane >= half_rot) & (lane < ROT), np.sin(angles), 0.0),
        ]
    )
    return lax.dynamic_slice_in_dim(
        jnp.asarray(tables.astype(np.float32)), place * context, context, 1
    )


def lane_is_low(shape):
    return lax.broadcasted_iota(jnp.int32, shape, len(shape) - 1) % PAIR < HEAD


def halves(full):
    return jnp.where(lane_is_low((HEAD, PAIR)), full[:HEAD], full[HEAD:])


def spread_pair(block):
    low = lane_is_low(block.shape)
    zero = jnp.zeros_like(block)
    return jnp.concatenate([jnp.where(low, block, zero), jnp.where(low, zero, block)], axis=0)


def one_head(tile, head):
    low = lane_is_low(tile.shape)
    zero = jnp.zeros_like(tile)
    return jnp.where(low, tile, zero) if head == 0 else jnp.where(low, zero, tile)


def in_two(value):
    high = value.astype(NARROW)
    return high, (value - high.astype(WIDE)).astype(NARROW)


def fine_dot(left, right, dims):
    left_high, left_low = in_two(left)
    right_high, right_low = in_two(right)
    return (
        plain_dot(left_high, right_high, dims)
        + plain_dot(left_low, right_high, dims)
        + plain_dot(left_high, right_low, dims)
    )


def head_sums(tile):
    rows = lax.broadcasted_iota(jnp.int32, (PAIR, PAIR), 0) // HEAD
    columns = lax.broadcasted_iota(jnp.int32, (PAIR, PAIR), 1) // HEAD
    ones = (rows == columns).astype(WIDE).astype(NARROW)
    high, low = in_two(tile)
    return plain_dot(
        jnp.concatenate([high, low], axis=1), jnp.concatenate([ones, ones], axis=0), ROWS_COLS
    )


def turn(tile, cos, sin_up, sin_down):
    half_rot = ROT // 2
    return (
        tile * cos
        + pltpu.roll(tile, PAIR - half_rot, 1) * sin_up
        + pltpu.roll(tile, half_rot, 1) * sin_down
    )


def turn_back(tile, cos, sin_up, sin_down):
    half_rot = ROT // 2
    return (
        tile * cos
        + pltpu.roll(tile * sin_up, half_rot, 1)
        + pltpu.roll(tile * sin_down, PAIR - half_rot, 1)
    )


def all_rows(tables_ref, seqs):
    return [jnp.concatenate([tables_ref[k]] * seqs, axis=0) for k in range(3)]


def feature_grad(grad, phi, turned, mix, tables):
    weighted = grad * phi
    back = fine_dot(weighted, mix, ROWS_ROWS) - (HEAD**-0.5) * turned * head_sums(weighted)
    return turn_back(back, *tables)


def doc_at(where, lengths_ref, b):
    start, found = 0, jnp.zeros_like(where) - 1
    for k in range(lengths_ref.shape[1]):
        found = found + jnp.where(start <= where, 1, 0)
        start = start + lengths_ref[b, k]
    return found


def same_doc_before(lengths_ref, b, first, context):
    query = first + lax.broadcasted_iota(jnp.int32, (context, context), 0)
    key = first + lax.broadcasted_iota(jnp.int32, (context, context), 1)
    same = doc_at(query, lengths_ref, b) == doc_at(key, lengths_ref, b)
    return jnp.where(same & (key <= query), 1.0, 0.0)


def in_doc_of(lengths_ref, b, first, context, where):
    rows = first + lax.broadcasted_iota(jnp.int32, (context, PAIR), 0)
    return jnp.where(doc_at(rows, lengths_ref, b) == doc_at(where, lengths_ref, b), 1.0, 0.0)


def local_kernel(
    seqs,
    lengths_ref,
    first_ref,
    attn_ref,
    weight_ref,
    bias_ref,
    tables_ref,
    dct_ref,
    points_ref,
    weights_ref,
    fq_ref,
    fk_ref,
    val_ref,
    phiq_ref,
    phik_ref,
    rotq_ref,
    rotk_ref,
    num_ref,
    den_ref,
    score_ref,
    carry_ref,
    mix_ref,
):
    context = tables_ref.shape[1]
    first = first_ref[0]

    @pl.when(pl.program_id(0) == 0)
    def _():
        both = lax.dot_general(
            dct_ref[...],
            points_ref[...],
            (COLS_COLS, ((), ())),
            precision=lax.Precision.HIGHEST,
            preferred_element_type=WIDE,
        )
        mix_ref[...] = spread_pair(jnp.concatenate([both, both], axis=1) * HEAD ** (-0.25))

    mix = mix_ref[...]
    weights = as_row(weights_ref)
    wrow = jnp.concatenate([weights, weights], axis=1)
    tables = all_rows(tables_ref, seqs)
    low = lane_is_low((seqs * context, PAIR))
    block = plain_dot(attn_ref[...], weight_ref[...], ROWS_COLS) + bias_ref[...]
    one, two, three = block[:, :PAIR], block[:, PAIR : 2 * PAIR], block[:, 2 * PAIR :]
    query = jnp.where(low, one, two)
    key = pltpu.roll(jnp.where(low, three, one), HEAD, 1)
    value_all = jnp.where(low, two, three).astype(NARROW)
    val_ref[...] = value_all

    def features(raw):
        turned = turn(raw, *tables)
        power = fine_dot(turned, mix, ROWS_COLS) - (0.5 * HEAD**-0.5) * head_sums(turned * turned)
        return turned, wrow * jnp.exp(power)

    turned_q, phi_q = features(query)
    turned_k, phi_k = features(key)
    rotq_ref[...], rotk_ref[...] = turned_q, turned_k
    phiq_ref[...], phik_ref[...] = phi_q, phi_k
    fq_all, fk_all = phi_q.astype(NARROW), phi_k.astype(NARROW)
    fq_ref[...], fk_ref[...] = fq_all, fk_all
    low = lane_is_low((context, PAIR))
    for b in range(seqs):
        rows = slice(b * context, (b + 1) * context)
        fq, fk, value = fq_all[rows], fk_all[rows], value_all[rows]
        mask = same_doc_before(lengths_ref, b, first, context)
        keep = in_doc_of(lengths_ref, b, first, context, first + context - 1)
        wide_value = jnp.concatenate([value, jnp.ones_like(value)], axis=1)
        sums = []
        for h in range(2):
            scores = (plain_dot(one_head(fq, h), fk, ROWS_ROWS) * mask).astype(NARROW)
            score_ref[0, b, h] = scores
            sums.append(plain_dot(scores, wide_value, ROWS_COLS))
        num_ref[rows, :] = jnp.where(low, sums[0][:, :PAIR], sums[1][:, :PAIR])
        den_ref[rows, :] = jnp.where(low, sums[0][:, PAIR:], sums[1][:, PAIR:])
        kept = fk * keep.astype(NARROW)
        carry_ref[b, 0, :HEAD, :] = halves(plain_dot(kept, value, COLS_COLS))
        norm = jnp.sum(kept.astype(WIDE), axis=0, keepdims=True)
        carry_ref[b, 0, HEAD:, :] = jnp.broadcast_to(norm, (8, PAIR))


def middle_kernel(
    seqs,
    lengths_ref,
    first_ref,
    cot_ref,
    dense_ref,
    fq_ref,
    fk_ref,
    val_ref,
    phiq_ref,
    rotq_ref,
    num_ref,
    den_ref,
    score_ref,
    carry_ref,
    tables_ref,
    mix_ref,
    low_ref,
    gradq_ref,
    gradk_ref,
    gradv_ref,
    out_ref,
):
    context = tables_ref.shape[1]
    first = first_ref[0]
    mix = mix_ref[...]
    tables = all_rows(tables_ref, seqs)
    low = lane_is_low((context, PAIR))
    back_all = plain_dot(cot_ref[...], dense_ref[...], ROWS_ROWS)
    grads_q = []
    for b in range(seqs):
        rows = pl.ds(b * context, context)
        fq, fk, value = fq_ref[rows, :], fk_ref[rows, :], val_ref[rows, :]
        use = in_doc_of(lengths_ref, b, first, context, first - 1)
        state = spread_pair(carry_ref[b, 0, :HEAD, :].astype(NARROW))
        norm = carry_ref[b, 0, HEAD : HEAD + 1, :]
        wide_fq = fq.astype(WIDE)
        num = num_ref[rows, :] + use * plain_dot(fq, state, ROWS_COLS)
        den = den_ref[rows, :] + use * head_sums(wide_fq * norm)
        heads_out = num / den
        low_ref[rows, :] = heads_out.astype(NARROW)
        back = back_all[b * context : (b + 1) * context]
        num_grad = (back / den).astype(NARROW)
        den_grad = -head_sums(back * heads_out) / den
        mask = same_doc_before(lengths_ref, b, first, context)
        parts_q, parts_k, parts_v = [], [], []
        for h in range(2):
            column = den_grad[:, h * HEAD : h * HEAD + 1]
            score_grad = plain_dot(one_head(num_grad, h), value, ROWS_ROWS) + column
            score_grad = (score_grad * mask).astype(NARROW)
            parts_q.append(plain_dot(score_grad, fk, ROWS_COLS))
            parts_k.append(plain_dot(score_grad, fq, COLS_COLS))
            parts_v.append(plain_dot(score_ref[0, b, h], num_grad, COLS_COLS))
        gradk_ref[rows, :] = jnp.where(low, parts_k[0], parts_k[1])
        gradv_ref[rows, :] = jnp.where(low, parts_v[0], parts_v[1])
        num_used = num_grad * use.astype(NARROW)
        den_used = den_grad * use
        grads_q.append(
            jnp.where(low, parts_q[0], parts_q[1])
            + plain_dot(num_used, state, ROWS_ROWS)
            + den_used * norm
        )
        out_ref[b, 0, :HEAD, :] = halves(plain_dot(fq, num_used, COLS_COLS))
        norm_grad = jnp.sum(den_used * wide_fq, axis=0, keepdims=True)
        out_ref[b, 0, HEAD:, :] = jnp.broadcast_to(norm_grad, (8, PAIR))
    gradq_ref[...] = feature_grad(
        jnp.concatenate(grads_q, axis=0), phiq_ref[...], rotq_ref[...], mix, tables
    ).astype(NARROW)


def last_kernel(
    seqs,
    lengths_ref,
    first_ref,
    gradq_ref,
    gradk_ref,
    gradv_ref,
    fk_ref,
    val_ref,
    phik_ref,
    rotk_ref,
    carry_ref,
    tables_ref,
    mix_ref,
    out_ref,
    *send_refs,
):
    context = tables_ref.shape[1]
    first = first_ref[0]
    tables = all_rows(tables_ref, seqs)
    grads_k, grads_v = [], []
    for b in range(seqs):
        rows = pl.ds(b * context, context)
        keep = in_doc_of(lengths_ref, b, first, context, first + context - 1)
        state = spread_pair(carry_ref[b, 0, :HEAD, :].astype(NARROW))
        norm = carry_ref[b, 0, HEAD : HEAD + 1, :]
        grads_k.append(
            gradk_ref[rows, :] + keep * (plain_dot(val_ref[rows, :], state, ROWS_ROWS) + norm)
        )
        grads_v.append(gradv_ref[rows, :] + keep * plain_dot(fk_ref[rows, :], state, ROWS_COLS))
    grad_k = feature_grad(
        jnp.concatenate(grads_k, axis=0), phik_ref[...], rotk_ref[...], mix_ref[...], tables
    )
    grad_k = pltpu.roll(grad_k, HEAD, 1)
    grad_v = jnp.concatenate(grads_v, axis=0)
    grad_q = gradq_ref[...].astype(WIDE)
    low = lane_is_low(grad_q.shape)
    grad = jnp.concatenate(
        [
            jnp.where(low, grad_q, grad_k),
            jnp.where(low, grad_v, grad_q),
            jnp.where(low, grad_k, grad_v),
        ],
        axis=1,
    ).astype(NARROW)
    out_ref[...] = grad
    wide = grad.astype(WIDE)
    for step in range(HEADS // 2):

        @pl.when(pl.program_id(0) == step)
        def _(step=step):
            for k in range(3):
                at = (3 * step + k) * PAIR
                ref, at = (send_refs[0], at) if at < D else (send_refs[1], at - D)
                ref[:, at : at + PAIR] = wide[:, k * PAIR : (k + 1) * PAIR]


def pass_kernel(lengths_ref, first_ref, own_ref, arrived_ref, out_ref):
    context = first_ref[1]
    for b in range(own_ref.shape[0]):
        last = doc_at(first_ref[0] + context - 1, lengths_ref, b)
        through = last == doc_at(first_ref[0] - 1, lengths_ref, b)
        out_ref[b] = own_ref[b] + jnp.where(through, arrived_ref[b], 0.0)


SMEM_SPEC = pl.BlockSpec(memory_space=pltpu.SMEM)


def pass_on(own, arrived, lengths, first):
    seqs, pairs = own.shape[:2]
    spec = pl.BlockSpec((seqs, pairs // 2, *own.shape[2:]), lambda i: (0, i, 0, 0))
    return pl.pallas_call(
        pass_kernel,
        grid=(2,),
        in_specs=[SMEM_SPEC, SMEM_SPEC, spec, spec],
        out_specs=spec,
        out_shape=pltpu.HBM(own.shape, WIDE),
        cost_estimate=lasting(2.0),
        name="pass_carry",
    )(*in_hbm(lengths, first, own, arrived))


def pair_spec(rows):
    return pl.BlockSpec((None, rows, PAIR), lambda i: (i, 0, 0))


def pair_shapes(tokens):
    shape = (HEADS // 2, tokens, PAIR)
    return pltpu.HBM(shape, NARROW), pltpu.HBM(shape, WIDE)


def attention_specs(seqs, context):
    carry = pl.BlockSpec((seqs, 1, HEAD + 8, PAIR), lambda i: (0, i, 0, 0))
    scores = pl.BlockSpec((1, seqs, 2, context, context), lambda i: (i, 0, 0, 0, 0))
    return carry, scores, [whole_spec((3, context, PAIR)), whole_spec((PAIR, PAIR))]


def attention_local(lengths, first, attn_in, weight, bias, tables, points, weights):
    seqs, context, tokens = lengths.shape[0], tables.shape[1], attn_in.shape[0]
    pairs = HEADS // 2
    carry, scores, shared = attention_specs(seqs, context)
    narrow, wide = pair_shapes(tokens)
    return pl.pallas_call(
        partial(local_kernel, seqs),
        grid=(pairs,),
        in_specs=[
            SMEM_SPEC,
            SMEM_SPEC,
            whole_spec((tokens, D)),
            pl.BlockSpec((D, 3 * PAIR), lambda i: (0, i)),
            pl.BlockSpec((1, 3 * PAIR), lambda i: (0, i)),
            shared[0],
            whole_spec((HEAD, HEAD)),
            whole_spec((HEAD, HEAD)),
            whole_spec((HEAD,)),
        ],
        out_specs=[pair_spec(tokens)] * 9 + [scores, carry, shared[1]],
        out_shape=[narrow] * 3
        + [wide] * 6
        + [
            pltpu.HBM((pairs, seqs, 2, context, context), NARROW),
            pltpu.HBM((seqs, pairs, HEAD + 8, PAIR), WIDE),
            pltpu.HBM((PAIR, PAIR), WIDE),
        ],
        cost_estimate=lasting(14.0),
        compiler_params=pltpu.CompilerParams(vmem_limit_bytes=25165824),
        name="attention_local",
    )(*in_hbm(lengths, first, attn_in, weight, bias, tables, dct_matrix(), points, weights))


def attention_middle(lengths, first, cot, dense_weight, *rest):
    seqs, context, tokens = lengths.shape[0], rest[-2].shape[1], cot.shape[0]
    pairs = HEADS // 2
    carry, scores, shared = attention_specs(seqs, context)
    narrow, wide = pair_shapes(tokens)
    return pl.pallas_call(
        partial(middle_kernel, seqs),
        grid=(pairs,),
        in_specs=[
            SMEM_SPEC,
            SMEM_SPEC,
            whole_spec((tokens, D)),
            pl.BlockSpec((PAIR, D), lambda i: (i, 0)),
        ]
        + [pair_spec(tokens)] * 7
        + [scores, carry, *shared],
        out_specs=[pl.BlockSpec((tokens, PAIR), lambda i: (0, i))]
        + [pair_spec(tokens)] * 3
        + [carry],
        out_shape=[pltpu.HBM((tokens, D), NARROW), narrow, wide, wide]
        + [pltpu.HBM((seqs, pairs, HEAD + 8, PAIR), WIDE)],
        cost_estimate=lasting(20.0),
        compiler_params=pltpu.CompilerParams(vmem_limit_bytes=25165824),
        name="attention_middle",
    )(*in_hbm(lengths, first, cot, dense_weight, *rest))


def attention_last(lengths, first, *rest):
    seqs, context, tokens = lengths.shape[0], rest[-2].shape[1], rest[0].shape[1]
    carry, _, shared = attention_specs(seqs, context)
    return pl.pallas_call(
        partial(last_kernel, seqs),
        grid=(HEADS // 2,),
        in_specs=[SMEM_SPEC, SMEM_SPEC] + [pair_spec(tokens)] * 7 + [carry, *shared],
        out_specs=[pl.BlockSpec((tokens, 3 * PAIR), lambda i: (0, i))]
        + [whole_spec((tokens, D)), whole_spec((tokens, 2 * D))],
        out_shape=[
            pltpu.HBM((tokens, 3 * D), NARROW),
        ]
        + [pltpu.HBM((tokens, D), WIDE), pltpu.HBM((tokens, 2 * D), WIDE)],
        cost_estimate=lasting(10),
        compiler_params=pltpu.CompilerParams(vmem_limit_bytes=25165824),
        name="attention_last",
    )(*in_hbm(lengths, first, *rest))


def shards(
    inputs,
    lengths,
    ln1_gain,
    ln1_bias,
    ln2_gain,
    ln2_bias,
    qkv_weight,
    qkv_bias,
    dense_weight,
    dense_bias,
    up_weight,
    up_bias,
    down_weight,
    down_bias,
    qmc_points,
    qmc_weights,
    cotangent,
):
    seqs, context = inputs.shape[:2]
    tokens = seqs * context
    owners, count, place = lax.axis_size("batch"), lax.axis_size("seq"), lax.axis_index("seq")
    bits = list(range(owners.bit_length() - 2))[::-1]
    across = D // COLUMNS
    hops = max(1, count // 2)

    line = Line()
    me = lax.axis_index("batch").astype(jnp.int32)[None]
    edge = ((place == 0) | (place == count - 1)).astype(jnp.int32)[None]
    if owners == 8 and count == 4:
        reduction = Rounds(line, edge, [2, 2, 2, 2, 1, 1, 1, 1])
    else:
        reduction = Singly(line, bits)

    def group(name, shape, at, left, blocks, right, rights_in, columns, begin=0, arrived=()):
        many = len(rights_in)
        pieces = [
            (*left, block, right, rights_in[column % many], place, (row, column))
            for column in range(columns)
            for row, block in enumerate(blocks)
            for place in [(begin + column, columns) if many == 1 else (0, 1)]
        ]
        size = (len(blocks) * BLOCK_ROWS, columns * COLUMNS // Rounds.PARTS)
        reduction.prepare((name, shape, at, size), pieces, *arrived)

    BLOCK_ROWS = min(BLOCK, D // owners)
    inputs_flat = inputs.reshape(tokens, D)
    cot = cotangent.reshape(tokens, D)
    cot_in = swap(cot.astype(WIDE), 0)
    start = place * context
    first = jnp.stack([start, jnp.full((), context, jnp.int32)])
    qkv_row = qkv_bias.astype(WIDE)[None, :]
    tables = attention_tables(place, context, count)
    attn_in, mlp_in, unit, rate = line.step(
        two_norms, inputs_flat, ln1_gain, ln1_bias, ln2_gain, ln2_bias
    )
    act, slope, act_own, act_send = line.step(mlp_up, mlp_in, up_weight, up_bias, me)
    act_in = swap(act_send, 0)
    norm_own, norm_send = line.step(lambda *a: pick(a[:2], a[2]), attn_in, mlp_in, me)
    subs = act_own.shape[0]

    def down_group(sub):
        shape = (FF // owners, D)
        at = (sub // 2, 0)
        group("down", shape, at, (act_own, act_in), (sub, sub + 1), cot, [cot_in], across)

    down_group(0)
    up_grad, up_send, up_sums, mlp_out, mlp_norm_grad = line.step(
        mlp_back, cot, down_weight, up_weight, act, slope
    )
    for sub in range(2, subs, 2):
        down_group(sub)
    reduction.step(tables, qkv_row, first)
    up_in = line.send(up_send, lambda a: swap(a, 0))
    norm_in = line.send(norm_send, lambda a: swap(a, 0))

    fq, fk, value, phi_q, phi_k, rot_q, rot_k, num, den, scores, carry, mix = line.step(
        attention_local,
        lengths,
        first,
        attn_in,
        qkv_weight,
        qkv_row,
        tables,
        qmc_points,
        qmc_weights,
    )
    arrived = shift_rows(carry, "seq", 1)

    def up_group(part):
        shape = (D // owners, FF)
        at = (0, part * Rounds.PARTS)
        columns = FF // COLUMNS // 2
        group("up", shape, at, (norm_own, norm_in), (1,), up_grad, [up_in], columns, part * Rounds.PARTS * columns)

    up_group(0)
    for _ in range(hops - 1):
        passed = line.step(pass_on, carry, arrived, lengths, first)
        arrived = shift_rows(passed, "seq", 1)
    reduction.step()
    up_group(1)
    attn_low, grad_q, grad_k, grad_v, carry_back = line.step(
        attention_middle,
        lengths,
        first,
        cot,
        dense_weight,
        fq,
        fk,
        value,
        phi_q,
        rot_q,
        num,
        den,
        scores,
        arrived,
        tables,
        mix,
    )
    arrived_back = shift_rows(carry_back, "seq", -1)
    low_own, low_send = line.step(lambda *a: pick(a[:1], a[1]), attn_low, me)
    low_in = swap(low_send, 0)
    reduction.step()
    output = line.step(
        layer_output,
        attn_low,
        dense_weight,
        inputs_flat,
        mlp_out,
        dense_bias,
        down_bias,
    )
    for _ in range(hops - 1):
        passed = line.step(pass_on, carry_back, arrived_back, lengths, first)
        arrived_back = shift_rows(passed, "seq", -1)
    shape = (D // owners, D)
    group("dense", shape, (0, 0), (low_own, low_in), (0,), cot, [cot_in], across)
    reduction.step()
    qkv_grad, *qkv_send = line.step(
        attention_last,
        lengths,
        first,
        grad_q,
        grad_k,
        grad_v,
        fk,
        value,
        phi_k,
        rot_k,
        arrived_back,
        tables,
        mix,
    )
    qkv_in = [swap(qkv_send[0], 0)]
    qkv_rest = swap(qkv_send[1], 0)
    def qkv_group(part, *arrived):
        shape = (D // owners, 3 * D)
        at = (0, part * Rounds.PARTS)
        left = (norm_own, norm_in)
        group("qkv", shape, at, left, (0,), qkv_grad, qkv_in, 2, max(part - 1, 0) * 4, arrived)

    arriving = reduction.arriving()
    qkv_group(0, *([line.step(lambda *a: settle(a), *arriving)] if arriving else []))
    reduction.step()
    qkv_in = [qkv_rest]
    qkv_group(1)
    input_grad, sums, qkv_sums = line.step(
        norm_back,
        qkv_grad,
        qkv_weight,
        mlp_norm_grad,
        unit,
        rate,
        cot,
        ln1_gain,
        ln2_gain,
    )

    vectors = Vectors(line, (sums, qkv_sums, up_sums), [])
    vectors.send()
    vectors.take()
    vectors.send()
    reduction.step()
    qkv_group(2)
    vectors.take()
    vectors.send()
    while not reduction.finished():
        reduction.step()
        vectors.take()
        vectors.send()
    totals = reduction.results()
    (
        attn_gain_total,
        attn_shift_total,
        mlp_gain_total,
        mlp_shift_total,
        bias_total,
        qkv_bias_total,
        up_bias_total,
    ) = vectors.results()

    return (
        output.reshape(inputs.shape),
        input_grad.reshape(inputs.shape),
        attn_gain_total,
        attn_shift_total,
        mlp_gain_total,
        mlp_shift_total,
        totals["qkv"],
        qkv_bias_total,
        totals["dense"],
        bias_total,
        totals["up"],
        up_bias_total,
        totals["down"],
        bias_total,
    )


def solution(mesh):
    placed = (
        P("batch", "seq", None),
        P("batch", None),
        P(),
        P(),
        P(),
        P(),
        P(),
        P(),
        P(),
        P(),
        P(),
        P(),
        P(),
        P(),
        P(),
        P(),
        P("batch", "seq", None),
    )
    return jax.shard_map(
        shards,
        mesh=mesh,
        in_specs=placed,
        out_specs=(
            P("batch", "seq", None),
            P("batch", "seq", None),
            P("batch"),
            P("batch"),
            P("batch"),
            P("batch"),
            P("batch", None),
            P("batch"),
            P("batch", None),
            P("batch"),
            P("batch", None),
            P("batch"),
            P("batch", None),
            P("batch"),
        ),
        check_vma=False,
    )
```
